32 devices in a mesh: groups: 1, tm: 8 (over z, y), cell: 2 (over x), sub: 2 (over core).
Axes of the slice: x: 2, y: 2, z: 4, core: 2. Of those that a mesh axis runs over, the one named last changes fastest.
Arguments:
- frames: bfloat16 [512, 128, 384], P(('groups', 'tm', 'sub'), 'cell'), may hold values from -6 to 6
- w_qkv: bfloat16 [384, 1152], P('sub'), may hold values from -1.5 to 1.5
- w_out: bfloat16 [384, 384], P('sub'), may hold values from -0.3125 to 0.3125
- w_up: bfloat16 [384, 1536], P('sub'), may hold values from -0.3125 to 0.3125
- w_down: bfloat16 [1536, 384], P('sub'), may hold values from -0.15625 to 0.15625
- temporal_weight_first: bfloat16 [1152, 768], P('sub'), may hold values from -0.1875 to 0.1875
- temporal_weight_second: bfloat16 [1152, 768], P('sub'), may hold values from -0.1875 to 0.1875
Outputs:
- features_out: bfloat16 [512, 128, 384], P(('groups', 'tm', 'sub'), 'cell')
The draws below stay inside these ranges and needn't reach their ends.
All inputs are finite; a program needn't handle non-finite values.
Results may differ from the reference program's by a relative error of at most 0.009.
Values may be sent and summed in bfloat16 or wider, within the bound.
A program may use at most 64 MiB of HBM per device.

```python
import math
import jax
import jax.numpy as jnp
from jax import lax

C = 384
FF = 1536
HEAD_DIM = 64
P_SIZE = 128
F_LOC = 32
DILATION_FIRST = 16
DILATION_SECOND = 256
FRAMES = 512


def draw_w_qkv(key, part):
    key_base = jax.random.fold_in(key, 0)
    base = jax.random.truncated_normal(key_base, -4.0, 4.0, (C, 3 * C), jnp.float32) / math.sqrt(C)
    return base.astype(jnp.bfloat16)


def levels(key, extent, shards, smallest, top_value):
    gain, own = 1.0, jax.random.fold_in(key, 6)
    for dim, shards_of in shards:
        steps = jnp.exp(jax.random.uniform(jax.random.fold_in(own, dim), (shards_of,), jnp.float32, smallest / len(shards), top_value / len(shards)))
        gain = gain * jnp.repeat(steps, extent[dim] // shards_of).reshape([-1 if axis == dim else 1 for axis in range(len(extent))])
    return gain


def noise(rng, extent, scale, bound, cuts=(), dtype=jnp.bfloat16):
    level = levels(rng, extent, cuts, -0.22, 0.18) if cuts else 1.0
    drawn = jax.random.normal(rng, extent, jnp.float32) * scale * level
    return jnp.minimum(jnp.maximum(drawn, -bound), bound).astype(dtype)


def setup_inputs(seed: int = 0, part: int = 0) -> dict:
    key_list = jax.random.split(jax.random.key(seed), 8)
    own_keys = jax.random.split(jax.random.fold_in(key_list[7], part), 8)
    frames = noise(own_keys[0], (FRAMES, P_SIZE, C), 1.0, 6.0, ((0, 16), (1, 2)))
    w_qkv = draw_w_qkv(jax.random.fold_in(key_list[7], 71), part)
    w_out = noise(key_list[2], (C, C), C ** -0.5, 0.3125, ((0, 2),))
    w_up = noise(key_list[3], (C, FF), C ** -0.5, 0.3125, ((0, 2),))
    w_down = noise(key_list[4], (FF, C), FF ** -0.5, 0.15625, ((0, 2),))
    temporal_weight_first = noise(key_list[5], (3 * C, 2 * C), (3 * C) ** -0.5, 0.1875, ((0, 2),))
    temporal_weight_second = noise(key_list[6], (3 * C, 2 * C), (3 * C) ** -0.5, 0.1875, ((0, 2),))
    return {"frames": frames, "w_qkv": w_qkv, "w_out": w_out, "w_up": w_up, "w_down": w_down, "temporal_weight_first": temporal_weight_first, "temporal_weight_second": temporal_weight_second}


def normalize(values):
    row_mean = lax.optimization_barrier(jnp.mean(values, axis=-1, keepdims=True))
    centred = values - row_mean
    row_var = lax.optimization_barrier(jnp.mean(centred * centred, axis=-1, keepdims=True))
    return centred * lax.rsqrt(row_var + 1e-05)

def attend(queries, key_part, value_part):
    frame_count, q_cells, features = queries.shape
    head_count = features // HEAD_DIM
    q_heads = queries.reshape(frame_count, q_cells, head_count, HEAD_DIM).astype(jnp.float32)
    k_heads = key_part.reshape(frame_count, -1, head_count, HEAD_DIM).astype(jnp.float32)
    v_heads = value_part.reshape(frame_count, -1, head_count, HEAD_DIM).astype(jnp.float32)
    scores = jnp.einsum('fqhd,fkhd->fhqk', q_heads, k_heads) * HEAD_DIM ** (-0.5)
    row_max = lax.optimization_barrier(jnp.max(scores, axis=-1, keepdims=True))
    exp_terms = jnp.exp(scores - row_max)
    attn_probs = (exp_terms / lax.optimization_barrier(jnp.sum(exp_terms, axis=-1, keepdims=True))).astype(jnp.bfloat16)
    attn_probs = lax.optimization_barrier(attn_probs)
    mixed = jnp.einsum('fhqk,fkhd->fqhd', attn_probs.astype(jnp.float32), v_heads)
    return mixed.astype(jnp.bfloat16).reshape(frame_count, q_cells, features)

def section_one(block, w_qkv, w_out, w_up, w_down):
    frame_count, cells, features = block.shape
    residual = block.astype(jnp.float32)
    normed = normalize(residual).astype(jnp.bfloat16).reshape(-1, features)
    projected = jnp.dot(normed, w_qkv, preferred_element_type=jnp.float32).astype(jnp.bfloat16)
    projected = lax.optimization_barrier(projected).reshape(frame_count, cells, 3 * features)
    attended = attend(projected[..., :features], projected[..., features:2 * features], projected[..., 2 * features:])
    out_part = jnp.dot(attended.reshape(-1, features), w_out, preferred_element_type=jnp.float32)
    mid_state = (residual + out_part.reshape(frame_count, cells, features)).astype(jnp.bfloat16)
    mid_float = lax.optimization_barrier(mid_state).astype(jnp.float32)
    normed_two = normalize(mid_float).astype(jnp.bfloat16).reshape(-1, features)
    hidden = jax.nn.gelu(jnp.dot(normed_two, w_up, preferred_element_type=jnp.float32)).astype(jnp.bfloat16)
    down_part = jnp.dot(hidden, w_down, preferred_element_type=jnp.float32)
    return (mid_float + down_part.reshape(frame_count, cells, features)).astype(jnp.bfloat16)

def gated_temporal_layer(center, weight, dilation):
    frame_total = center.shape[0]
    features = center.shape[-1]
    padded_frames = jnp.pad(center, ((dilation, dilation), (0, 0), (0, 0)))
    earlier = padded_frames[:frame_total]
    later_frames = padded_frames[2 * dilation:]
    stacked = jnp.concatenate([earlier, center, later_frames], axis=-1).reshape(-1, 3 * features)
    preact = jnp.dot(stacked, weight, preferred_element_type=jnp.float32)
    gated_part = jnp.tanh(preact[:, :features]) * jax.nn.sigmoid(preact[:, features:])
    return (center.astype(jnp.float32) + gated_part.reshape(center.shape)).astype(jnp.bfloat16)

def reference(frames, w_qkv, w_out, w_up, w_down, temporal_weight_first, temporal_weight_second):
    frame_total = frames.shape[0]
    blocks = frames.reshape(frame_total // F_LOC, F_LOC, P_SIZE, C)
    sectioned_frames = lax.map(lambda block: section_one(block, w_qkv, w_out, w_up, w_down), blocks)
    sectioned_frames = sectioned_frames.reshape(frame_total, P_SIZE, C)
    opening_layer = gated_temporal_layer(sectioned_frames, temporal_weight_first, DILATION_FIRST)
    return gated_temporal_layer(opening_layer, temporal_weight_second, DILATION_SECOND)
```

```python
import functools

import jax
import jax.numpy as jnp
from jax import lax
from jax.experimental import pallas as pl
from jax.experimental.pallas import tpu as pltpu
from jax.sharding import PartitionSpec as P

HEAD_DIM = 64
DILATION_FIRST = 16
DILATION_SECOND = 256
CHUNK = 2
AHEAD = 2
PAIR = 2 * HEAD_DIM
MESH = pl.DeviceIdType.MESH
F32 = jnp.float32
BF16 = jnp.bfloat16


def normalize(values):
    row_mean = jnp.mean(values, axis=-1, keepdims=True)
    centred = values - row_mean
    row_var = jnp.mean(centred * centred, axis=-1, keepdims=True)
    return centred * lax.rsqrt(row_var + 1e-05)


def dot(a, b):
    return jnp.dot(a, b, preferred_element_type=F32)


def attend(projected, frame_count, cells, features):
    lane = lax.broadcasted_iota(jnp.int32, (cells, PAIR), 1)
    scale = HEAD_DIM ** (-0.5)
    keep_a = jnp.where(lane < HEAD_DIM, scale, 0.0).astype(BF16)
    keep_b = jnp.where(lane < HEAD_DIM, 0.0, scale).astype(BF16)
    rows = []
    for f in range(frame_count):
        here = projected[f * cells : (f + 1) * cells]
        columns = []
        for p in range(features // PAIR):
            q = here[:, p * PAIR : (p + 1) * PAIR]
            k = here[:, features + p * PAIR : features + (p + 1) * PAIR]
            v = here[:, 2 * features + p * PAIR : 2 * features + (p + 1) * PAIR]
            stacked = jnp.concatenate([q * keep_a, q * keep_b], axis=0)
            scores = lax.dot_general(
                stacked, k, (((1,), (1,)), ((), ())), preferred_element_type=F32
            )
            exp_terms = jnp.exp(scores - jnp.max(scores, axis=-1, keepdims=True))
            probs = exp_terms * (1.0 / jnp.sum(exp_terms, axis=-1, keepdims=True))
            mixed = dot(probs.astype(BF16), v)
            columns.append(jnp.where(lane < HEAD_DIM, mixed[:cells], mixed[cells:]).astype(BF16))
        rows.append(jnp.concatenate(columns, axis=1))
    return jnp.concatenate(rows, axis=0)


def gated(center, earlier, later, weight_ref):
    features = center.shape[-1]
    preact = dot(center, weight_ref[features : 2 * features])
    if earlier is not None:
        preact += dot(earlier, weight_ref[:features])
    if later is not None:
        preact += dot(later, weight_ref[2 * features :])
    gate = 0.5 * jnp.tanh(0.5 * preact[:, features:]) + 0.5
    return (center.astype(F32) + jnp.tanh(preact[:, :features]) * gate).astype(BF16)


def kernel(
    sizes,
    frames, h_qkv, h_out, h_up, h_down, h_first, h_second,
    out,
    w_qkv, w_out, w_up, w_down, w_first, w_second,
    work, stage, pad, first, far, result,
    ws, wr, wl, in_s, in_r, in_l, own_s, own_r, halo_s, halo_r, far_s, far_r, out_s,
):
    n_tm, n_cell, n_sub = sizes
    n_blocks = n_tm * n_sub
    frames_local, cells_local, features = frames.shape
    per = frames_local // n_cell
    cells = n_cell * cells_local
    steps = per // CHUNK
    reach = DILATION_SECOND // frames_local
    width = DILATION_FIRST
    tm, x, sub = lax.axis_index("tm"), lax.axis_index("cell"), lax.axis_index("sub")
    block = tm * n_sub + sub

    def at(b, j):
        return {"tm": b // n_sub, "cell": j, "sub": lax.rem(b, n_sub)}

    def peer(d):
        return lax.rem(x + d, n_cell)

    def source(d):
        return lax.rem(x + n_cell - d, n_cell)

    def remote(src, dst, s, r, where):
        return pltpu.make_async_remote_copy(
            src_ref=src, dst_ref=dst, send_sem=s, recv_sem=r, device_id=where, device_id_type=MESH
        )

    has = {
        -1: block >= 1,
        1: block + 1 < n_blocks,
        -reach: block >= reach,
        reach: block + reach < n_blocks,
    }

    halves = (h_qkv, h_out, h_up, h_down, h_first, h_second)
    wholes = (w_qkv, w_out, w_up, w_down, w_first, w_second)

    def rows_of(half):
        size = half.shape[0]
        return pl.ds(pl.multiple_of(sub * size, 16), size)

    def local_weight(i):
        return pltpu.make_async_copy(halves[i], wholes[i].at[rows_of(halves[i])], wl.at[i])

    def remote_weight(i, d):
        return remote(
            halves[i], wholes[i].at[rows_of(halves[i])], ws.at[i, d - 1], wr.at[i, d - 1],
            {"sub": lax.rem(sub + d, n_sub)},
        )

    my_cells = pl.ds(pl.multiple_of(x * cells_local, 16), cells_local)

    def local_in(k):
        return pltpu.make_async_copy(
            frames.at[pl.ds(x * per + k * CHUNK, CHUNK)],
            work.at[pl.ds(k * CHUNK, CHUNK), my_cells],
            in_l.at[k],
        )

    def remote_in(k, d):
        return remote(
            frames.at[pl.ds(peer(d) * per + k * CHUNK, CHUNK)],
            work.at[pl.ds(k * CHUNK, CHUNK), my_cells],
            in_s.at[k, d - 1], in_r.at[k, d - 1], {"cell": peer(d)},
        )

    def staged(k, d):
        their_cells = pl.ds(pl.multiple_of(peer(d) * cells_local, 16), cells_local)
        return stage.at[pl.ds(k * CHUNK, CHUNK), their_cells]

    def own_copy(k, d):
        return remote(
            staged(k, d), pad.at[pl.ds(width + x * per + k * CHUNK, CHUNK)],
            own_s.at[k, d - 1], own_r.at[k, d - 1], {"cell": peer(d)},
        )

    def to_next(k, d):
        start = source(d) * per + k * CHUNK
        return remote(
            pad.at[pl.ds(width + start, CHUNK)],
            pad.at[pl.ds(start - (frames_local - width), CHUNK)],
            halo_s.at[0, k, d], halo_r.at[0, k, d], at(block + 1, x),
        )

    def to_last(k, d):
        start = width + source(d) * per + k * CHUNK
        return remote(
            pad.at[pl.ds(start, CHUNK)], pad.at[pl.ds(start + frames_local, CHUNK)],
            halo_s.at[1, k, d], halo_r.at[1, k, d], at(block - 1, x),
        )

    def from_halo(side, k, d):
        return remote(
            pad.at[pl.ds(width, CHUNK)], pad.at[pl.ds(0, CHUNK)],
            halo_s.at[side, k, d], halo_r.at[side, k, d], {"cell": x},
        )

    def late_half(j, k):
        return j * per + k * CHUNK >= frames_local - width

    def early_half(j, k):
        return j * per + k * CHUNK < width

    def far_copy(side, k):
        piece = pl.ds(k * CHUNK, CHUNK)
        by = reach if side == 0 else -reach
        return remote(
            first.at[:, piece], far.at[side, :, piece],
            far_s.at[side, k], far_r.at[side, k], at(block + by, x),
        )

    def out_copy(k):
        piece = pl.ds(k * CHUNK, CHUNK)
        return pltpu.make_async_copy(result.at[:, piece], out.at[:, piece], out_s.at[k])

    for i in range(6):
        local_weight(i).start()

    @pl.loop(0, steps)
    def _(k):
        local_in(k).start()

    barrier = pltpu.get_barrier_semaphore()
    for d in range(1, n_cell):
        pl.semaphore_signal(barrier, inc=1, device_id={"cell": peer(d)}, device_id_type=MESH)
    for by, cond in has.items():
        @pl.when(cond)
        def _():
            pl.semaphore_signal(
                barrier, inc=1, device_id=at(block + by, x), device_id_type=MESH
            )
    heard = n_cell - 1
    for cond in has.values():
        heard = heard + jnp.where(cond, 1, 0)
    pl.semaphore_wait(barrier, heard)

    for i in range(6):
        for d in range(1, n_sub):
            remote_weight(i, d).start()

    for k in range(min(AHEAD, steps)):
        for d in range(1, n_cell):
            remote_in(k, d).start()

    @pl.when(jnp.logical_not(has[-1]))
    def _():
        pad[:width] = jnp.zeros((width, cells_local, features), BF16)

    @pl.when(jnp.logical_not(has[1]))
    def _():
        pad[width + frames_local :] = jnp.zeros((width, cells_local, features), BF16)

    @pl.when(jnp.logical_not(has[-reach]))
    def _():
        far[0] = jnp.zeros(far.shape[1:], BF16)

    @pl.when(jnp.logical_not(has[reach]))
    def _():
        far[1] = jnp.zeros(far.shape[1:], BF16)

    def weight_ready(i):
        local_weight(i).wait()
        for d in range(1, n_sub):
            remote_weight(i, d).wait_recv()

    for i in range(4):
        weight_ready(i)

    def forward(k):
        for d in range(n_cell):
            if d:
                own_copy(k, d).wait_recv()

            @pl.when(jnp.logical_and(late_half(source(d), k), has[1]))
            def _():
                to_next(k, d).start()

            @pl.when(jnp.logical_and(early_half(source(d), k), has[-1]))
            def _():
                to_last(k, d).start()

    def block_step(k):
        @pl.when(k + AHEAD < steps)
        def _():
            for d in range(1, n_cell):
                remote_in(k + AHEAD, d).start()

        local_in(k).wait()
        for d in range(1, n_cell):
            remote_in(k, d).wait_recv()
        piece = pl.ds(k * CHUNK, CHUNK)
        residual = work[piece].reshape(CHUNK * cells, features).astype(F32)
        projected = dot(normalize(residual).astype(BF16), w_qkv[...]).astype(BF16)
        attended = attend(projected, CHUNK, cells, features)

        @pl.when(k >= 1)
        def _():
            forward(k - 1)

        mid = (residual + dot(attended, w_out[...])).astype(BF16).astype(F32)
        hidden = jax.nn.gelu(dot(normalize(mid).astype(BF16), w_up[...])).astype(BF16)
        done = (mid + dot(hidden, w_down[...])).astype(BF16)
        stage[piece] = done.reshape(CHUNK, cells, features)
        for d in range(1, n_cell):
            own_copy(k, d).start()
        pad[pl.ds(width + x * per + k * CHUNK, CHUNK)] = stage[piece, my_cells]

    def gather(ref, k, shift):
        parts = [
            ref[pl.ds(j * per + k * CHUNK + shift, CHUNK)].reshape(CHUNK * cells_local, features)
            for j in range(n_cell)
        ]
        return jnp.concatenate(parts, axis=0)

    def first_step(k):
        for d in range(n_cell):
            @pl.when(jnp.logical_and(late_half(source(d), k), has[-1]))
            def _():
                from_halo(0, k, d).wait_recv()

            @pl.when(jnp.logical_and(early_half(source(d), k), has[1]))
            def _():
                from_halo(1, k, d).wait_recv()
        value = gated(gather(pad, k, width), gather(pad, k, 0), gather(pad, k, 2 * width), w_first)
        first[:, pl.ds(k * CHUNK, CHUNK)] = value.reshape(n_cell, CHUNK, cells_local, features)

        @pl.when(has[reach])
        def _():
            far_copy(0, k).start()

        @pl.when(has[-reach])
        def _():
            far_copy(1, k).start()

    extra = 1 if steps >= 6 else 0
    late = steps - 2 * extra

    @pl.loop(0, steps)
    def _(k):
        block_step(k)

        @pl.when(k == min(1, steps - 1))
        def _():
            weight_ready(4)

        @pl.when(jnp.where(k < late, lax.rem(k, 2), 1) == 1)
        def _():
            first_step(jnp.where(k == steps - 1, (steps - 2) // 2 + extra, k // 2))

    forward(steps - 1)

    @pl.loop(steps // 2 + extra, steps)
    def _(k):
        first_step(k)

    weight_ready(5)

    @pl.loop(0, steps)
    def _(k):
        @pl.when(has[-reach])
        def _():
            far_copy(0, k).wait_recv()

        @pl.when(has[reach])
        def _():
            far_copy(1, k).wait_recv()

        piece = pl.ds(k * CHUNK, CHUNK)
        flat = (n_cell * CHUNK * cells_local, features)
        value = gated(
            first[:, piece].reshape(flat),
            far[0, :, piece].reshape(flat),
            far[1, :, piece].reshape(flat),
            w_second,
        )
        result[:, piece] = value.reshape(n_cell, CHUNK, cells_local, features)
        out_copy(k).start()

    for i in range(6):
        for d in range(1, n_sub):
            remote_weight(i, d).wait_send()

    @pl.loop(0, steps)
    def _(k):
        for d in range(n_cell):
            if d:
                remote_in(k, d).wait_send()
                own_copy(k, d).wait_send()

            @pl.when(jnp.logical_and(late_half(source(d), k), has[1]))
            def _():
                to_next(k, d).wait_send()

            @pl.when(jnp.logical_and(early_half(source(d), k), has[-1]))
            def _():
                to_last(k, d).wait_send()

        @pl.when(has[reach])
        def _():
            far_copy(0, k).wait_send()

        @pl.when(has[-reach])
        def _():
            far_copy(1, k).wait_send()

        out_copy(k).wait()


def regroup_kernel(
    sizes,
    frames, h_qkv, h_out, h_up, h_down, h_first, h_second,
    out,
    w_qkv, w_out, w_up, w_down, w_first, w_second,
    work, sect, first, result,
    ws, wr, wl, in_s, in_r, in_l, halo_s, halo_r, out_s, out_r, out_l,
):
    n_tm, n_cell, n_sub = sizes
    n_blocks = n_tm * n_sub
    per, classes, cells_local, features = frames.shape
    segments, span, cells, _ = first.shape
    group = span // per
    reach = group * n_sub
    steps = segments * group
    tm, x, sub = lax.axis_index("tm"), lax.axis_index("cell"), lax.axis_index("sub")
    block = tm * n_sub + sub
    mine = tm * n_cell + x

    home = lax.rem(block, reach) // group
    my_slot = (block // reach) * group + lax.rem(block, group)
    my_cells = pl.ds(pl.multiple_of(x * cells_local, 16), cells_local)

    def remote(src, dst, s, r, where):
        return pltpu.make_async_remote_copy(
            src_ref=src, dst_ref=dst, send_sem=s, recv_sem=r, device_id=where, device_id_type=MESH
        )

    halves = (h_qkv, h_out, h_up, h_down, h_first, h_second)
    wholes = (w_qkv, w_out, w_up, w_down, w_first, w_second)

    def rows_of(half):
        size = half.shape[0]
        return pl.ds(pl.multiple_of(sub * size, 16), size)

    def local_weight(i):
        return pltpu.make_async_copy(halves[i], wholes[i].at[rows_of(halves[i])], wl.at[i])

    def remote_weight(i, d):
        return remote(
            halves[i], wholes[i].at[rows_of(halves[i])], ws.at[i, d - 1], wr.at[i, d - 1],
            {"sub": lax.rem(sub + d, n_sub)},
        )

    def weight_ready(i):
        local_weight(i).wait()
        for d in range(1, n_sub):
            remote_weight(i, d).wait_recv()

    def cells_of(j):
        return pl.ds(pl.multiple_of(j * cells_local, 16), cells_local)

    order = sorted(range(n_tm), key=lambda d: (d % n_sub, abs(d - n_tm // 2)))
    moves = [(d, e) for d in order for e in range(n_cell)]

    def in_copy(i):
        d, e = moves[i]
        to_tm, to_x = lax.rem(tm + d, n_tm), lax.rem(x + e, n_cell)
        return remote(
            frames.at[:, to_tm * n_cell + to_x], work.at[my_slot, :, my_cells],
            in_s.at[i], in_r.at[my_slot, x], {"tm": to_tm, "cell": to_x, "sub": home},
        )

    def in_away(i):
        return home != sub if moves[i] == (0, 0) else True

    def in_local():
        return pltpu.make_async_copy(
            frames.at[:, mine], work.at[my_slot, :, my_cells], in_l.at[0]
        )

    def in_ready(h, p):
        slot = h * group + p
        for j in range(n_cell):
            here = jnp.logical_and(h * reach + sub * group + p == block, x == j)

            @pl.when(here)
            def _():
                in_local().wait()

            @pl.when(jnp.logical_not(here))
            def _():
                remote(
                    frames.at[:, 0], work.at[slot, :, cells_of(j)],
                    in_s.at[0], in_r.at[slot, j], {"cell": x},
                ).wait_recv()

    def halo_copy(side, h):
        at = h * n_sub + sub + (1 if side == 0 else -1)
        start, end = (span, 0) if side == 0 else (1, span + 1)
        to = at // n_sub
        return remote(
            sect.at[h, start], sect.at[to, end],
            halo_s.at[side, h], halo_r.at[side, to], {"sub": lax.rem(at, n_sub)},
        )

    def has_halo(side, h):
        at = h * n_sub + sub
        return at >= 1 if side == 0 else at + 1 < segments * n_sub

    def sends_halo(side, h):
        return has_halo(1 - side, h)

    def halo_ready(side, h):
        @pl.when(has_halo(side, h))
        def _():
            remote(
                sect.at[h, 1], sect.at[h, 0 if side == 0 else span + 1],
                halo_s.at[side, h], halo_r.at[side, h], {"cell": x},
            ).wait_recv()

    def out_target(h, p, j):
        to = h * reach + sub * group + p
        return to, jnp.logical_and(to == block, x == j)

    def out_copy(h, p, j):
        to, _ = out_target(h, p, j)
        return remote(
            result.at[h, pl.ds(p * per, per), cells_of(j)], out.at[:, mine],
            out_s.at[h, p, j], out_r.at[mine],
            {"tm": to // n_sub, "cell": j, "sub": lax.rem(to, n_sub)},
        )

    def out_local(h, p, j):
        return pltpu.make_async_copy(
            result.at[h, pl.ds(p * per, per), cells_of(j)], out.at[:, mine], out_l.at[0]
        )

    for i in range(6):
        local_weight(i).start()

    @pl.when(home == sub)
    def _():
        in_local().start()

    barrier = pltpu.get_barrier_semaphore()
    others = n_blocks * n_cell - 1
    rank = block * n_cell + x
    for d in range(1, others + 1):
        to = lax.rem(rank + d, others + 1)
        b = to // n_cell
        pl.semaphore_signal(
            barrier, inc=1, device_id_type=MESH,
            device_id={"tm": b // n_sub, "cell": lax.rem(to, n_cell), "sub": lax.rem(b, n_sub)},
        )
    pl.semaphore_wait(barrier, others)

    for d in range(1, n_sub):
        remote_weight(0, d).start()
    for i in range(len(moves)):
        @pl.when(in_away(i))
        def _():
            in_copy(i).start()
    for i in range(1, 6):
        for d in range(1, n_sub):
            remote_weight(i, d).start()

    for h in range(segments):
        for side in range(2):
            @pl.when(jnp.logical_not(has_halo(side, h)))
            def _():
                sect[h, 0 if side == 0 else span + 1] = jnp.zeros((cells, features), BF16)

    for i in range(4):
        weight_ready(i)

    def block_step(h, p):
        in_ready(h, p)
        residual = work[h * group + p].reshape(per * cells, features).astype(F32)
        projected = dot(normalize(residual).astype(BF16), w_qkv[...]).astype(BF16)
        attended = attend(projected, per, cells, features)
        mid = (residual + dot(attended, w_out[...])).astype(BF16).astype(F32)
        hidden = jax.nn.gelu(dot(normalize(mid).astype(BF16), w_up[...])).astype(BF16)
        done = (mid + dot(hidden, w_down[...])).astype(BF16)
        sect[h, pl.ds(1 + p * per, per)] = done.reshape(per, cells, features)
        for side, edge in ((0, group - 1), (1, 0)):
            @pl.when(jnp.logical_and(p == edge, sends_halo(side, h)))
            def _():
                halo_copy(side, h).start()

    def flat(ref, h, start):
        return ref[h, pl.ds(start, per)].reshape(per * cells, features)

    def temporal(p):
        @pl.loop(0, segments)
        def _(h):
            for side, edge in ((0, 0), (1, group - 1)):
                @pl.when(p == edge)
                def _():
                    halo_ready(side, h)
            start = p * per
            value = gated(
                flat(sect, h, start + 1), flat(sect, h, start), flat(sect, h, start + 2), w_first
            )
            first[h, pl.ds(start, per)] = value.reshape(per, cells, features)

        for h in range(segments):
            start = p * per
            value = gated(
                flat(first, h, start),
                flat(first, h - 1, start) if h >= 1 else None,
                flat(first, h + 1, start) if h + 1 < segments else None,
                w_second,
            )
            result[h, pl.ds(start, per)] = value.reshape(per, cells, features)
            for j in range(n_cell):
                _, here = out_target(h, p, j)

                @pl.when(here)
                def _():
                    out_local(h, p, j).start()

                @pl.when(jnp.logical_not(here))
                def _():
                    out_copy(h, p, j).start()

    begin, own = lax.rem(tm * n_sub, group), (tm * n_sub) // reach

    def place(i):
        return lax.rem(begin + i, group)

    @pl.loop(0, steps)
    def _(t):
        i = t // segments
        block_step(lax.rem(own + t, segments), place(i))

        @pl.when(t == 1)
        def _():
            weight_ready(4)
            weight_ready(5)

        @pl.when(jnp.logical_and(i >= 2, lax.rem(t, segments) == segments - 1))
        def _():
            temporal(place(i - 1))

    @pl.loop(0, 2)
    def _(k):
        temporal(place(group - 1 + k))

    for r in range(classes):
        here = jnp.logical_and(mine == r, home == sub)

        @pl.when(here)
        def _():
            pltpu.make_async_copy(
                result.at[0, pl.ds(0, per), my_cells], out.at[:, r], out_l.at[0]
            ).wait()

        @pl.when(jnp.logical_not(here))
        def _():
            remote(
                result.at[0, pl.ds(0, per), my_cells], out.at[:, r],
                out_s.at[0, 0, 0], out_r.at[r], {"cell": x},
            ).wait_recv()

    for i in range(6):
        for d in range(1, n_sub):
            remote_weight(i, d).wait_send()
    for i in range(len(moves)):
        @pl.when(in_away(i))
        def _():
            in_copy(i).wait_send()
    for h in range(segments):
        for side in range(2):
            @pl.when(sends_halo(side, h))
            def _():
                halo_copy(side, h).wait_send()

        @pl.loop(0, group)
        def _(p):
            for j in range(n_cell):
                _, here = out_target(h, p, j)

                @pl.when(jnp.logical_not(here))
                def _():
                    out_copy(h, p, j).wait_send()


def regroup(sizes, frames, *halves):
    n_tm, n_cell, n_sub = sizes
    frames_local, cells_local, features = frames.shape
    classes = DILATION_FIRST
    per = frames_local // classes
    cells = n_cell * cells_local
    reach = DILATION_SECOND // frames_local
    group = reach // n_sub
    segments = n_tm * n_sub // reach
    span = group * per
    split = (per, classes, cells_local, features)
    dma = pltpu.SemaphoreType.DMA
    anywhere = pl.BlockSpec(memory_space=pl.ANY)
    call = pl.pallas_call(
        functools.partial(regroup_kernel, sizes),
        out_shape=jax.ShapeDtypeStruct(split, BF16),
        in_specs=[anywhere] * 7,
        out_specs=anywhere,
        scratch_shapes=[pltpu.VMEM((n_sub * w.shape[0], w.shape[1]), BF16) for w in halves]
        + [
            pltpu.VMEM((segments * group, per, cells, features), BF16),
            pltpu.VMEM((segments, span + 2, cells, features), BF16),
            pltpu.VMEM((segments, span, cells, features), BF16),
            pltpu.VMEM((segments, span, cells, features), BF16),
            dma((6, n_sub - 1)), dma((6, n_sub - 1)), dma((6,)),
            dma((n_tm * n_cell,)), dma((segments * group, n_cell)), dma((1,)),
            dma((2, segments)), dma((2, segments)),
            dma((segments, group, n_cell)), dma((classes,)), dma((1,)),
        ],
        compiler_params=pltpu.CompilerParams(
            collective_id=0, has_side_effects=True, vmem_limit_bytes=56 * 1024 * 1024
        ),
        name="video_regroup",
    )
    return call(frames.reshape(split), *halves).reshape(frames.shape)


def regroups(sizes, frames):
    n_tm, n_cell, n_sub = sizes
    frames_local = frames.shape[0]
    reach = DILATION_SECOND // frames_local
    return (
        n_tm * n_cell == DILATION_FIRST
        and n_sub >= 2
        and frames_local % DILATION_FIRST == 0
        and DILATION_SECOND % frames_local == 0
        and reach % n_sub == 0
        and reach // n_sub >= 2
        and n_tm * n_sub % reach == 0
    )


def local(sizes, frames, *halves):
    if regroups(sizes, frames):
        return regroup(sizes, frames, *halves)
    _, n_cell, n_sub = sizes
    frames_local, cells_local, features = frames.shape
    per = frames_local // n_cell
    cells = n_cell * cells_local
    steps = per // CHUNK
    split = (n_cell, per, cells_local, features)
    dma = pltpu.SemaphoreType.DMA
    anywhere = pl.BlockSpec(memory_space=pl.ANY)
    call = pl.pallas_call(
        functools.partial(kernel, sizes),
        out_shape=jax.ShapeDtypeStruct(split, BF16),
        in_specs=[anywhere] * 7,
        out_specs=anywhere,
        scratch_shapes=[pltpu.VMEM((n_sub * w.shape[0], w.shape[1]), BF16) for w in halves]
        + [
            pltpu.VMEM((per, cells, features), BF16),
            pltpu.VMEM((per, cells, features), BF16),
            pltpu.VMEM((frames_local + 2 * DILATION_FIRST, cells_local, features), BF16),
            pltpu.VMEM(split, BF16),
            pltpu.VMEM((2,) + split, BF16),
            pltpu.VMEM(split, BF16),
            dma((6, n_sub - 1)), dma((6, n_sub - 1)), dma((6,)),
            dma((steps, n_cell - 1)), dma((steps, n_cell - 1)), dma((steps,)),
            dma((steps, n_cell - 1)), dma((steps, n_cell - 1)),
            dma((2, steps, n_cell)), dma((2, steps, n_cell)),
            dma((2, steps)), dma((2, steps)), dma((steps,)),
        ],
        compiler_params=pltpu.CompilerParams(
            collective_id=0, has_side_effects=True, vmem_limit_bytes=56 * 1024 * 1024
        ),
        name="video_block",
    )
    return call(frames, *halves).reshape(frames.shape)


def solution(mesh):
    sizes = (mesh.shape["tm"], mesh.shape["cell"], mesh.shape["sub"])
    placed = (P(("groups", "tm", "sub"), "cell", None),) + (P("sub", None),) * 6
    return jax.shard_map(
        functools.partial(local, sizes),
        mesh=mesh,
        in_specs=placed,
        out_specs=P(("groups", "tm", "sub"), "cell", None),
        check_vma=False,
    )
```

```python
import functools

import jax
import jax.numpy as jnp
from jax import lax
from jax.experimental import pallas as pl
from jax.experimental.pallas import tpu as pltpu
from jax.sharding import PartitionSpec as P

HEAD_DIM = 64
DILATION_FIRST = 16
DILATION_SECOND = 256
CHUNK = 2
AHEAD = 2
PAIR = 2 * HEAD_DIM
MESH = pl.DeviceIdType.MESH
F32 = jnp.float32
BF16 = jnp.bfloat16


def normalize(values):
    row_mean = jnp.mean(values, axis=-1, keepdims=True)
    centred = values - row_mean
    row_var = jnp.mean(centred * centred, axis=-1, keepdims=True)
    return centred * lax.rsqrt(row_var + 1e-05)


def dot(a, b):
    return jnp.dot(a, b, preferred_element_type=F32)


def attend(projected, frame_count, cells, features):
    lane = lax.broadcasted_iota(jnp.int32, (cells, PAIR), 1)
    scale = HEAD_DIM ** (-0.5)
    keep_a = jnp.where(lane < HEAD_DIM, scale, 0.0).astype(BF16)
    keep_b = jnp.where(lane < HEAD_DIM, 0.0, scale).astype(BF16)
    rows = []
    for f in range(frame_count):
        here = projected[f * cells : (f + 1) * cells]
        columns = []
        for p in range(features // PAIR):
            q = here[:, p * PAIR : (p + 1) * PAIR]
            k = here[:, features + p * PAIR : features + (p + 1) * PAIR]
            v = here[:, 2 * features + p * PAIR : 2 * features + (p + 1) * PAIR]
            stacked = jnp.concatenate([q * keep_a, q * keep_b], axis=0)
            scores = lax.dot_general(
                stacked, k, (((1,), (1,)), ((), ())), preferred_element_type=F32
            )
            exp_terms = jnp.exp(scores - jnp.max(scores, axis=-1, keepdims=True))
            probs = exp_terms * (1.0 / jnp.sum(exp_terms, axis=-1, keepdims=True))
            mixed = dot(probs.astype(BF16), v)
            columns.append(jnp.where(lane < HEAD_DIM, mixed[:cells], mixed[cells:]).astype(BF16))
        rows.append(jnp.concatenate(columns, axis=1))
    return jnp.concatenate(rows, axis=0)


def gated(center, earlier, later, weight_ref):
    features = center.shape[-1]
    preact = (
        dot(center, weight_ref[features : 2 * features])
        + dot(earlier, weight_ref[:features])
        + dot(later, weight_ref[2 * features :])
    )
    gate = 0.5 * jnp.tanh(0.5 * preact[:, features:]) + 0.5
    return (center.astype(F32) + jnp.tanh(preact[:, :features]) * gate).astype(BF16)


def gated_pair(center, other, weight_ref, earlier):
    features = center.shape[-1]
    other_rows = pl.ds(pl.multiple_of(jnp.where(earlier, 0, 2 * features), features), features)
    preact = dot(center, weight_ref[features : 2 * features]) + dot(other, weight_ref[other_rows])
    gate = 0.5 * jnp.tanh(0.5 * preact[:, features:]) + 0.5
    return (center.astype(F32) + jnp.tanh(preact[:, :features]) * gate).astype(BF16)


def kernel(
    sizes,
    frames, h_qkv, h_out, h_up, h_down, h_first, h_second,
    out,
    w_qkv, w_out, w_up, w_down, w_first, w_second,
    work, stage, pad, first, far, result,
    ws, wr, wl, in_s, in_r, in_l, own_s, own_r, halo_s, halo_r, far_s, far_r, out_s,
):
    n_tm, n_cell, n_sub = sizes
    n_blocks = n_tm * n_sub
    frames_local, cells_local, features = frames.shape
    per = frames_local // n_cell
    cells = n_cell * cells_local
    steps = per // CHUNK
    reach = DILATION_SECOND // frames_local
    width = DILATION_FIRST
    tm, x, sub = lax.axis_index("tm"), lax.axis_index("cell"), lax.axis_index("sub")
    block = tm * n_sub + sub

    def at(b, j):
        return {"tm": b // n_sub, "cell": j, "sub": lax.rem(b, n_sub)}

    def peer(d):
        return lax.rem(x + d, n_cell)

    def source(d):
        return lax.rem(x + n_cell - d, n_cell)

    def remote(src, dst, s, r, where):
        return pltpu.make_async_remote_copy(
            src_ref=src, dst_ref=dst, send_sem=s, recv_sem=r, device_id=where, device_id_type=MESH
        )

    has = {
        -1: block >= 1,
        1: block + 1 < n_blocks,
        -reach: block >= reach,
        reach: block + reach < n_blocks,
    }

    halves = (h_qkv, h_out, h_up, h_down, h_first, h_second)
    wholes = (w_qkv, w_out, w_up, w_down, w_first, w_second)

    def rows_of(half):
        size = half.shape[0]
        return pl.ds(pl.multiple_of(sub * size, 16), size)

    def local_weight(i):
        return pltpu.make_async_copy(halves[i], wholes[i].at[rows_of(halves[i])], wl.at[i])

    def remote_weight(i, d):
        return remote(
            halves[i], wholes[i].at[rows_of(halves[i])], ws.at[i, d - 1], wr.at[i, d - 1],
            {"sub": lax.rem(sub + d, n_sub)},
        )

    my_cells = pl.ds(pl.multiple_of(x * cells_local, 16), cells_local)

    def local_in(k):
        return pltpu.make_async_copy(
            frames.at[pl.ds(x * per + k * CHUNK, CHUNK)],
            work.at[pl.ds(k * CHUNK, CHUNK), my_cells],
            in_l.at[k],
        )

    def remote_in(k, d):
        return remote(
            frames.at[pl.ds(peer(d) * per + k * CHUNK, CHUNK)],
            work.at[pl.ds(k * CHUNK, CHUNK), my_cells],
            in_s.at[k, d - 1], in_r.at[k, d - 1], {"cell": peer(d)},
        )

    def staged(k, d):
        their_cells = pl.ds(pl.multiple_of(peer(d) * cells_local, 16), cells_local)
        return stage.at[pl.ds(k * CHUNK, CHUNK), their_cells]

    def own_copy(k, d):
        return remote(
            staged(k, d), pad.at[pl.ds(width + x * per + k * CHUNK, CHUNK)],
            own_s.at[k, d - 1], own_r.at[k, d - 1], {"cell": peer(d)},
        )

    def to_next(k, d):
        start = source(d) * per + k * CHUNK
        return remote(
            pad.at[pl.ds(width + start, CHUNK)],
            pad.at[pl.ds(start - (frames_local - width), CHUNK)],
            halo_s.at[0, k, d], halo_r.at[0, k, d], at(block + 1, x),
        )

    def to_last(k, d):
        start = width + source(d) * per + k * CHUNK
        return remote(
            pad.at[pl.ds(start, CHUNK)], pad.at[pl.ds(start + frames_local, CHUNK)],
            halo_s.at[1, k, d], halo_r.at[1, k, d], at(block - 1, x),
        )

    def from_halo(side, k, d):
        return remote(
            pad.at[pl.ds(width, CHUNK)], pad.at[pl.ds(0, CHUNK)],
            halo_s.at[side, k, d], halo_r.at[side, k, d], {"cell": x},
        )

    def late_half(j, k):
        return j * per + k * CHUNK >= frames_local - width

    def early_half(j, k):
        return j * per + k * CHUNK < width

    def far_copy(side, k):
        piece = pl.ds(k * CHUNK, CHUNK)
        by = reach if side == 0 else -reach
        return remote(
            first.at[:, piece], far.at[side, :, piece],
            far_s.at[side, k], far_r.at[side, k], at(block + by, x),
        )

    def out_copy(k):
        piece = pl.ds(k * CHUNK, CHUNK)
        return pltpu.make_async_copy(result.at[:, piece], out.at[:, piece], out_s.at[k])

    for i in range(6):
        local_weight(i).start()

    @pl.loop(0, steps)
    def _(k):
        local_in(k).start()

    barrier = pltpu.get_barrier_semaphore()
    for d in range(1, n_cell):
        pl.semaphore_signal(barrier, inc=1, device_id={"cell": peer(d)}, device_id_type=MESH)
    for by, cond in has.items():
        @pl.when(cond)
        def _():
            pl.semaphore_signal(
                barrier, inc=1, device_id=at(block + by, x), device_id_type=MESH
            )
    heard = n_cell - 1
    for cond in has.values():
        heard = heard + jnp.where(cond, 1, 0)
    pl.semaphore_wait(barrier, heard)

    for i in range(6):
        for d in range(1, n_sub):
            remote_weight(i, d).start()

    for k in range(min(AHEAD, steps)):
        for d in range(1, n_cell):
            remote_in(k, d).start()

    @pl.when(jnp.logical_not(has[-1]))
    def _():
        pad[:width] = jnp.zeros((width, cells_local, features), BF16)

    @pl.when(jnp.logical_not(has[1]))
    def _():
        pad[width + frames_local :] = jnp.zeros((width, cells_local, features), BF16)

    @pl.when(jnp.logical_not(has[-reach]))
    def _():
        far[0] = jnp.zeros(far.shape[1:], BF16)

    @pl.when(jnp.logical_not(has[reach]))
    def _():
        far[1] = jnp.zeros(far.shape[1:], BF16)

    def weight_ready(i):
        local_weight(i).wait()
        for d in range(1, n_sub):
            remote_weight(i, d).wait_recv()

    for i in range(4):
        weight_ready(i)

    def forward(k):
        for d in range(n_cell):
            if d:
                own_copy(k, d).wait_recv()

            @pl.when(jnp.logical_and(late_half(source(d), k), has[1]))
            def _():
                to_next(k, d).start()

            @pl.when(jnp.logical_and(early_half(source(d), k), has[-1]))
            def _():
                to_last(k, d).start()

    def block_step(k):
        @pl.when(k + AHEAD < steps)
        def _():
            for d in range(1, n_cell):
                remote_in(k + AHEAD, d).start()

        local_in(k).wait()
        for d in range(1, n_cell):
            remote_in(k, d).wait_recv()
        piece = pl.ds(k * CHUNK, CHUNK)
        residual = work[piece].reshape(CHUNK * cells, features).astype(F32)
        projected = dot(normalize(residual).astype(BF16), w_qkv[...]).astype(BF16)
        attended = attend(projected, CHUNK, cells, features)

        @pl.when(k >= 1)
        def _():
            forward(k - 1)

        mid = (residual + dot(attended, w_out[...])).astype(BF16).astype(F32)
        hidden = jax.nn.gelu(dot(normalize(mid).astype(BF16), w_up[...])).astype(BF16)
        done = (mid + dot(hidden, w_down[...])).astype(BF16)
        stage[piece] = done.reshape(CHUNK, cells, features)
        for d in range(1, n_cell):
            own_copy(k, d).start()
        pad[pl.ds(width + x * per + k * CHUNK, CHUNK)] = stage[piece, my_cells]

    def gather(ref, k, shift):
        parts = [
            ref[pl.ds(j * per + k * CHUNK + shift, CHUNK)].reshape(CHUNK * cells_local, features)
            for j in range(n_cell)
        ]
        return jnp.concatenate(parts, axis=0)

    def first_step(k):
        for d in range(n_cell):
            @pl.when(jnp.logical_and(late_half(source(d), k), has[-1]))
            def _():
                from_halo(0, k, d).wait_recv()

            @pl.when(jnp.logical_and(early_half(source(d), k), has[1]))
            def _():
                from_halo(1, k, d).wait_recv()
        value = gated(gather(pad, k, width), gather(pad, k, 0), gather(pad, k, 2 * width), w_first)
        first[:, pl.ds(k * CHUNK, CHUNK)] = value.reshape(n_cell, CHUNK, cells_local, features)

        @pl.when(has[reach])
        def _():
            far_copy(0, k).start()

        @pl.when(has[-reach])
        def _():
            far_copy(1, k).start()

    extra = 1 if steps >= 6 else 0
    late = steps - 2 * extra

    @pl.loop(0, steps)
    def _(k):
        block_step(k)

        @pl.when(k == min(1, steps - 1))
        def _():
            weight_ready(4)

        @pl.when(jnp.where(k < late, lax.rem(k, 2), 1) == 1)
        def _():
            first_step(jnp.where(k == steps - 1, (steps - 2) // 2 + extra, k // 2))

    forward(steps - 1)

    @pl.loop(steps // 2 + extra, steps)
    def _(k):
        first_step(k)

    weight_ready(5)

    @pl.loop(0, steps)
    def _(k):
        @pl.when(has[-reach])
        def _():
            far_copy(0, k).wait_recv()

        @pl.when(has[reach])
        def _():
            far_copy(1, k).wait_recv()

        piece = pl.ds(k * CHUNK, CHUNK)
        flat = (n_cell * CHUNK * cells_local, features)
        value = gated(
            first[:, piece].reshape(flat),
            far[0, :, piece].reshape(flat),
            far[1, :, piece].reshape(flat),
            w_second,
        )
        result[:, piece] = value.reshape(n_cell, CHUNK, cells_local, features)
        out_copy(k).start()

    for i in range(6):
        for d in range(1, n_sub):
            remote_weight(i, d).wait_send()

    @pl.loop(0, steps)
    def _(k):
        for d in range(n_cell):
            if d:
                remote_in(k, d).wait_send()
                own_copy(k, d).wait_send()

            @pl.when(jnp.logical_and(late_half(source(d), k), has[1]))
            def _():
                to_next(k, d).wait_send()

            @pl.when(jnp.logical_and(early_half(source(d), k), has[-1]))
            def _():
                to_last(k, d).wait_send()

        @pl.when(has[reach])
        def _():
            far_copy(0, k).wait_send()

        @pl.when(has[-reach])
        def _():
            far_copy(1, k).wait_send()

        out_copy(k).wait()


def regroup_kernel(
    sizes,
    frames, h_qkv, h_out, h_up, h_down, h_first, h_second,
    out,
    w_qkv, w_out, w_up, w_down, w_first, w_second,
    work, sect, first, result,
    ws, wr, wl, in_s, in_r, in_l, halo_s, halo_r, out_s, out_r, out_l,
):
    n_tm, n_cell, n_sub = sizes
    n_blocks = n_tm * n_sub
    per, classes, cells_local, features = frames.shape
    segments, span, cells, _ = first.shape
    group = span // per
    reach = group * n_sub
    steps = segments * group
    tm, x, sub = lax.axis_index("tm"), lax.axis_index("cell"), lax.axis_index("sub")
    block = tm * n_sub + sub
    mine = tm * n_cell + x

    home, own = lax.rem(block, reach) // group, block // reach
    my_slot = (block // reach) * group + lax.rem(block, group)
    my_cells = pl.ds(pl.multiple_of(x * cells_local, 16), cells_local)

    def remote(src, dst, s, r, where):
        return pltpu.make_async_remote_copy(
            src_ref=src, dst_ref=dst, send_sem=s, recv_sem=r, device_id=where, device_id_type=MESH
        )

    halves = (h_qkv, h_out, h_up, h_down, h_first, h_second)
    wholes = (w_qkv, w_out, w_up, w_down, w_first, w_second)

    def rows_of(half):
        size = half.shape[0]
        return pl.ds(pl.multiple_of(sub * size, 16), size)

    def local_weight(i):
        return pltpu.make_async_copy(halves[i], wholes[i].at[rows_of(halves[i])], wl.at[i])

    def remote_weight(i, d):
        return remote(
            halves[i], wholes[i].at[rows_of(halves[i])], ws.at[i, d - 1], wr.at[i, d - 1],
            {"sub": lax.rem(sub + d, n_sub)},
        )

    def weight_ready(i):
        local_weight(i).wait()
        for d in range(1, n_sub):
            remote_weight(i, d).wait_recv()

    def cells_of(j):
        return pl.ds(pl.multiple_of(j * cells_local, 16), cells_local)

    near = classes // group // 2
    moves = [(0, d, k) for d in range(near) for k in range(group)]
    moves += [(near, d, k) for k in range(group) for d in range(near)]
    level = block // group

    def in_chip(i):
        across, d, k = moves[i]
        base = lax.rem(level // near * near + across, 2 * near)
        return (base + lax.rem(level + d, near)) * group + lax.rem(block + group - k, group)

    def in_copy(i):
        to = in_chip(i)
        return remote(
            frames.at[:, to], work.at[my_slot, :, my_cells], in_s.at[i], in_r.at[my_slot, x],
            {"tm": to // n_cell, "cell": lax.rem(to, n_cell), "sub": home},
        )

    def in_away(i):
        return jnp.logical_not(jnp.logical_and(in_chip(i) == mine, home == sub))

    def in_local():
        return pltpu.make_async_copy(
            frames.at[:, mine], work.at[my_slot, :, my_cells], in_l.at[0]
        )

    def in_ready(h, p):
        slot = h * group + p
        for j in range(n_cell):
            here = jnp.logical_and(h * reach + sub * group + p == block, x == j)

            @pl.when(here)
            def _():
                in_local().wait()

            @pl.when(jnp.logical_not(here))
            def _():
                remote(
                    frames.at[:, 0], work.at[slot, :, cells_of(j)],
                    in_s.at[0], in_r.at[slot, j], {"cell": x},
                ).wait_recv()

    def halo_copy(side, h):
        at = h * n_sub + sub + (1 if side == 0 else -1)
        start, end = (span, 0) if side == 0 else (1, span + 1)
        to = at // n_sub
        return remote(
            sect.at[h, start], sect.at[to, end],
            halo_s.at[side, h], halo_r.at[side, to], {"sub": lax.rem(at, n_sub)},
        )

    def has_halo(side, h):
        at = h * n_sub + sub
        return at >= 1 if side == 0 else at + 1 < segments * n_sub

    def sends_halo(side, h):
        return has_halo(1 - side, h)

    def halo_ready(side, h):
        @pl.when(has_halo(side, h))
        def _():
            remote(
                sect.at[h, 1], sect.at[h, 0 if side == 0 else span + 1],
                halo_s.at[side, h], halo_r.at[side, h], {"cell": x},
            ).wait_recv()

    def out_target(h, p, j):
        to = h * reach + sub * group + p
        return to, jnp.logical_and(to == block, x == j)

    def out_copy(h, p, j):
        to, _ = out_target(h, p, j)
        return remote(
            result.at[h, pl.ds(p * per, per), cells_of(j)], out.at[:, mine],
            out_s.at[h, p, j], out_r.at[mine],
            {"tm": to // n_sub, "cell": j, "sub": lax.rem(to, n_sub)},
        )

    def out_local(h, p, j):
        return pltpu.make_async_copy(
            result.at[h, pl.ds(p * per, per), cells_of(j)], out.at[:, mine], out_l.at[0]
        )

    for i in range(6):
        local_weight(i).start()

    @pl.when(home == sub)
    def _():
        in_local().start()

    barrier = pltpu.get_barrier_semaphore()
    others = n_blocks * n_cell - 1
    rank = block * n_cell + x
    for d in range(1, others + 1):
        to = lax.rem(rank + d, others + 1)
        b = to // n_cell
        pl.semaphore_signal(
            barrier, inc=1, device_id_type=MESH,
            device_id={"tm": b // n_sub, "cell": lax.rem(to, n_cell), "sub": lax.rem(b, n_sub)},
        )
    pl.semaphore_wait(barrier, others)

    for d in range(1, n_sub):
        remote_weight(0, d).start()
    for i in range(len(moves)):
        @pl.when(in_away(i))
        def _():
            in_copy(i).start()
    for i in range(1, 6):
        for d in range(1, n_sub):
            remote_weight(i, d).start()

    for h in range(segments):
        for side in range(2):
            @pl.when(jnp.logical_not(has_halo(side, h)))
            def _():
                sect[h, 0 if side == 0 else span + 1] = jnp.zeros((cells, features), BF16)

    for i in range(4):
        weight_ready(i)

    def block_step(h, p):
        in_ready(h, p)
        residual = work[h * group + p].reshape(per * cells, features).astype(F32)
        projected = dot(normalize(residual).astype(BF16), w_qkv[...]).astype(BF16)
        attended = attend(projected, per, cells, features)
        mid = (residual + dot(attended, w_out[...])).astype(BF16).astype(F32)
        hidden = jax.nn.gelu(dot(normalize(mid).astype(BF16), w_up[...])).astype(BF16)
        done = (mid + dot(hidden, w_down[...])).astype(BF16)
        sect[h, pl.ds(1 + p * per, per)] = done.reshape(per, cells, features)
        for side, edge in ((0, group - 1), (1, 0)):
            @pl.when(jnp.logical_and(p == edge, sends_halo(side, h)))
            def _():
                halo_copy(side, h).start()

    def flat(ref, h, start):
        return ref[h, pl.ds(start, per)].reshape(per * cells, features)

    def temporal(p):
        @pl.loop(0, segments)
        def _(h):
            for side, edge in ((0, 0), (1, group - 1)):
                @pl.when(p == edge)
                def _():
                    halo_ready(side, h)
            start = p * per
            value = gated(
                flat(sect, h, start + 1), flat(sect, h, start), flat(sect, h, start + 2), w_first
            )
            first[h, pl.ds(start, per)] = value.reshape(per, cells, features)

        @pl.loop(0, segments)
        def _(k):
            h = lax.rem(own + 1 + k, segments)
            value = gated_pair(
                flat(first, h, p * per), flat(first, 1 - h, p * per), w_second, h == 1
            )
            result[h, pl.ds(p * per, per)] = value.reshape(per, cells, features)
            for j in range(n_cell):
                _, here = out_target(h, p, j)

                @pl.when(here)
                def _():
                    out_local(h, p, j).start()

                @pl.when(jnp.logical_not(here))
                def _():
                    out_copy(h, p, j).start()

    def place(i):
        return lax.rem(mine + i, group)

    @pl.loop(0, steps)
    def _(t):
        across = jnp.logical_or(t == group - 1, t > group)
        i = jnp.where(t < group - 1, t, jnp.where(t > group, t - group, jnp.where(across, 0, t - 1)))
        block_step(jnp.where(across, 1 - own, own), place(i))

        @pl.when(t == 1)
        def _():
            weight_ready(4)
            weight_ready(5)

        @pl.when(t >= group + 2)
        def _():
            temporal(place(i - 1))

    @pl.loop(0, 2)
    def _(k):
        temporal(place(group - 1 + k))

    for r in range(classes):
        here = jnp.logical_and(mine == r, home == sub)

        @pl.when(here)
        def _():
            pltpu.make_async_copy(
                result.at[0, pl.ds(0, per), my_cells], out.at[:, r], out_l.at[0]
            ).wait()

        @pl.when(jnp.logical_not(here))
        def _():
            remote(
                result.at[0, pl.ds(0, per), my_cells], out.at[:, r],
                out_s.at[0, 0, 0], out_r.at[r], {"cell": x},
            ).wait_recv()

    for i in range(6):
        for d in range(1, n_sub):
            remote_weight(i, d).wait_send()
    for i in range(len(moves)):
        @pl.when(in_away(i))
        def _():
            in_copy(i).wait_send()
    for h in range(segments):
        for side in range(2):
            @pl.when(sends_halo(side, h))
            def _():
                halo_copy(side, h).wait_send()

        @pl.loop(0, group)
        def _(p):
            for j in range(n_cell):
                _, here = out_target(h, p, j)

                @pl.when(jnp.logical_not(here))
                def _():
                    out_copy(h, p, j).wait_send()


def regroup(sizes, frames, *halves):
    n_tm, n_cell, n_sub = sizes
    frames_local, cells_local, features = frames.shape
    classes = DILATION_FIRST
    per = frames_local // classes
    cells = n_cell * cells_local
    reach = DILATION_SECOND // frames_local
    group = reach // n_sub
    segments = n_tm * n_sub // reach
    span = group * per
    split = (per, classes, cells_local, features)
    dma = pltpu.SemaphoreType.DMA
    anywhere = pl.BlockSpec(memory_space=pl.ANY)
    call = pl.pallas_call(
        functools.partial(regroup_kernel, sizes),
        out_shape=jax.ShapeDtypeStruct(split, BF16),
        in_specs=[anywhere] * 7,
        out_specs=anywhere,
        scratch_shapes=[pltpu.VMEM((n_sub * w.shape[0], w.shape[1]), BF16) for w in halves]
        + [
            pltpu.VMEM((segments * group, per, cells, features), BF16),
            pltpu.VMEM((segments, span + 2, cells, features), BF16),
            pltpu.VMEM((segments, span, cells, features), BF16),
            pltpu.VMEM((segments, span, cells, features), BF16),
            dma((6, n_sub - 1)), dma((6, n_sub - 1)), dma((6,)),
            dma((n_tm * n_cell,)), dma((segments * group, n_cell)), dma((1,)),
            dma((2, segments)), dma((2, segments)),
            dma((segments, group, n_cell)), dma((classes,)), dma((1,)),
        ],
        compiler_params=pltpu.CompilerParams(
            collective_id=0, has_side_effects=True, vmem_limit_bytes=56 * 1024 * 1024
        ),
        name="video_regroup",
    )
    return call(frames.reshape(split), *halves).reshape(frames.shape)


def regroups(sizes, frames):
    n_tm, n_cell, n_sub = sizes
    frames_local = frames.shape[0]
    reach = DILATION_SECOND // frames_local
    return (
        n_tm * n_cell == DILATION_FIRST
        and n_sub >= 2
        and frames_local % DILATION_FIRST == 0
        and DILATION_SECOND % frames_local == 0
        and reach % n_sub == 0
        and reach // n_sub >= 2
        and n_tm * n_sub == 2 * reach
        and DILATION_FIRST % (2 * (reach // n_sub)) == 0
    )


def local(sizes, frames, *halves):
    if regroups(sizes, frames):
        return regroup(sizes, frames, *halves)
    _, n_cell, n_sub = sizes
    frames_local, cells_local, features = frames.shape
    per = frames_local // n_cell
    cells = n_cell * cells_local
    steps = per // CHUNK
    split = (n_cell, per, cells_local, features)
    dma = pltpu.SemaphoreType.DMA
    anywhere = pl.BlockSpec(memory_space=pl.ANY)
    call = pl.pallas_call(
        functools.partial(kernel, sizes),
        out_shape=jax.ShapeDtypeStruct(split, BF16),
        in_specs=[anywhere] * 7,
        out_specs=anywhere,
        scratch_shapes=[pltpu.VMEM((n_sub * w.shape[0], w.shape[1]), BF16) for w in halves]
        + [
            pltpu.VMEM((per, cells, features), BF16),
            pltpu.VMEM((per, cells, features), BF16),
            pltpu.VMEM((frames_local + 2 * DILATION_FIRST, cells_local, features), BF16),
            pltpu.VMEM(split, BF16),
            pltpu.VMEM((2,) + split, BF16),
            pltpu.VMEM(split, BF16),
            dma((6, n_sub - 1)), dma((6, n_sub - 1)), dma((6,)),
            dma((steps, n_cell - 1)), dma((steps, n_cell - 1)), dma((steps,)),
            dma((steps, n_cell - 1)), dma((steps, n_cell - 1)),
            dma((2, steps, n_cell)), dma((2, steps, n_cell)),
            dma((2, steps)), dma((2, steps)), dma((steps,)),
        ],
        compiler_params=pltpu.CompilerParams(
            collective_id=0, has_side_effects=True, vmem_limit_bytes=56 * 1024 * 1024
        ),
        name="video_block",
    )
    return call(frames, *halves).reshape(frames.shape)


def solution(mesh):
    sizes = (mesh.shape["tm"], mesh.shape["cell"], mesh.shape["sub"])
    placed = (P(("groups", "tm", "sub"), "cell", None),) + (P("sub", None),) * 6
    return jax.shard_map(
        functools.partial(local, sizes),
        mesh=mesh,
        in_specs=placed,
        out_specs=P(("groups", "tm", "sub"), "cell", None),
        check_vma=False,
    )
```

```python
import functools

import jax
import jax.numpy as jnp
from jax import lax
from jax.experimental import pallas as pl
from jax.experimental.pallas import tpu as pltpu
from jax.sharding import PartitionSpec as P

HEAD_DIM = 64
DILATION_FIRST = 16
DILATION_SECOND = 256
CHUNK = 2
AHEAD = 2
PAIR = 2 * HEAD_DIM
MESH = pl.DeviceIdType.MESH
F32 = jnp.float32
BF16 = jnp.bfloat16


def normalize(values):
    row_mean = jnp.mean(values, axis=-1, keepdims=True)
    centred = values - row_mean
    row_var = jnp.mean(centred * centred, axis=-1, keepdims=True)
    return centred * lax.rsqrt(row_var + 1e-05)


def dot(a, b):
    return jnp.dot(a, b, preferred_element_type=F32)


def attend(projected, frame_count, cells, features):
    lane = lax.broadcasted_iota(jnp.int32, (cells, PAIR), 1)
    scale = HEAD_DIM ** (-0.5)
    keep_a = jnp.where(lane < HEAD_DIM, scale, 0.0).astype(BF16)
    keep_b = jnp.where(lane < HEAD_DIM, 0.0, scale).astype(BF16)
    rows = []
    for f in range(frame_count):
        here = projected[f * cells : (f + 1) * cells]
        columns = []
        for p in range(features // PAIR):
            q = here[:, p * PAIR : (p + 1) * PAIR]
            k = here[:, features + p * PAIR : features + (p + 1) * PAIR]
            v = here[:, 2 * features + p * PAIR : 2 * features + (p + 1) * PAIR]
            stacked = jnp.concatenate([q * keep_a, q * keep_b], axis=0)
            scores = lax.dot_general(
                stacked, k, (((1,), (1,)), ((), ())), preferred_element_type=F32
            )
            exp_terms = jnp.exp(scores - jnp.max(scores, axis=-1, keepdims=True))
            probs = exp_terms * (1.0 / jnp.sum(exp_terms, axis=-1, keepdims=True))
            mixed = dot(probs.astype(BF16), v)
            columns.append(jnp.where(lane < HEAD_DIM, mixed[:cells], mixed[cells:]).astype(BF16))
        rows.append(jnp.concatenate(columns, axis=1))
    return jnp.concatenate(rows, axis=0)


def gated(center, earlier, later, weight_ref):
    features = center.shape[-1]
    preact = (
        dot(center, weight_ref[features : 2 * features])
        + dot(earlier, weight_ref[:features])
        + dot(later, weight_ref[2 * features :])
    )
    gate = 0.5 * jnp.tanh(0.5 * preact[:, features:]) + 0.5
    return (center.astype(F32) + jnp.tanh(preact[:, :features]) * gate).astype(BF16)


def gated_pair(center, other, weight_ref, earlier):
    features = center.shape[-1]
    other_rows = pl.ds(pl.multiple_of(jnp.where(earlier, 0, 2 * features), features), features)
    preact = dot(center, weight_ref[features : 2 * features]) + dot(other, weight_ref[other_rows])
    gate = 0.5 * jnp.tanh(0.5 * preact[:, features:]) + 0.5
    return (center.astype(F32) + jnp.tanh(preact[:, :features]) * gate).astype(BF16)


def kernel(
    sizes,
    frames, h_qkv, h_out, h_up, h_down, h_first, h_second,
    out,
    w_qkv, w_out, w_up, w_down, w_first, w_second,
    work, stage, pad, first, far, result,
    ws, wr, wl, in_s, in_r, in_l, own_s, own_r, halo_s, halo_r, far_s, far_r, out_s,
):
    n_tm, n_cell, n_sub = sizes
    n_blocks = n_tm * n_sub
    frames_local, cells_local, features = frames.shape
    per = frames_local // n_cell
    cells = n_cell * cells_local
    steps = per // CHUNK
    reach = DILATION_SECOND // frames_local
    width = DILATION_FIRST
    tm, x, sub = lax.axis_index("tm"), lax.axis_index("cell"), lax.axis_index("sub")
    block = tm * n_sub + sub

    def at(b, j):
        return {"tm": b // n_sub, "cell": j, "sub": lax.rem(b, n_sub)}

    def peer(d):
        return lax.rem(x + d, n_cell)

    def source(d):
        return lax.rem(x + n_cell - d, n_cell)

    def remote(src, dst, s, r, where):
        return pltpu.make_async_remote_copy(
            src_ref=src, dst_ref=dst, send_sem=s, recv_sem=r, device_id=where, device_id_type=MESH
        )

    has = {
        -1: block >= 1,
        1: block + 1 < n_blocks,
        -reach: block >= reach,
        reach: block + reach < n_blocks,
    }

    halves = (h_qkv, h_out, h_up, h_down, h_first, h_second)
    wholes = (w_qkv, w_out, w_up, w_down, w_first, w_second)

    def rows_of(half):
        size = half.shape[0]
        return pl.ds(pl.multiple_of(sub * size, 16), size)

    def local_weight(i):
        return pltpu.make_async_copy(halves[i], wholes[i].at[rows_of(halves[i])], wl.at[i])

    def remote_weight(i, d):
        return remote(
            halves[i], wholes[i].at[rows_of(halves[i])], ws.at[i, d - 1], wr.at[i, d - 1],
            {"sub": lax.rem(sub + d, n_sub)},
        )

    my_cells = pl.ds(pl.multiple_of(x * cells_local, 16), cells_local)

    def local_in(k):
        return pltpu.make_async_copy(
            frames.at[pl.ds(x * per + k * CHUNK, CHUNK)],
            work.at[pl.ds(k * CHUNK, CHUNK), my_cells],
            in_l.at[k],
        )

    def remote_in(k, d):
        return remote(
            frames.at[pl.ds(peer(d) * per + k * CHUNK, CHUNK)],
            work.at[pl.ds(k * CHUNK, CHUNK), my_cells],
            in_s.at[k, d - 1], in_r.at[k, d - 1], {"cell": peer(d)},
        )

    def staged(k, d):
        their_cells = pl.ds(pl.multiple_of(peer(d) * cells_local, 16), cells_local)
        return stage.at[pl.ds(k * CHUNK, CHUNK), their_cells]

    def own_copy(k, d):
        return remote(
            staged(k, d), pad.at[pl.ds(width + x * per + k * CHUNK, CHUNK)],
            own_s.at[k, d - 1], own_r.at[k, d - 1], {"cell": peer(d)},
        )

    def to_next(k, d):
        start = source(d) * per + k * CHUNK
        return remote(
            pad.at[pl.ds(width + start, CHUNK)],
            pad.at[pl.ds(start - (frames_local - width), CHUNK)],
            halo_s.at[0, k, d], halo_r.at[0, k, d], at(block + 1, x),
        )

    def to_last(k, d):
        start = width + source(d) * per + k * CHUNK
        return remote(
            pad.at[pl.ds(start, CHUNK)], pad.at[pl.ds(start + frames_local, CHUNK)],
            halo_s.at[1, k, d], halo_r.at[1, k, d], at(block - 1, x),
        )

    def from_halo(side, k, d):
        return remote(
            pad.at[pl.ds(width, CHUNK)], pad.at[pl.ds(0, CHUNK)],
            halo_s.at[side, k, d], halo_r.at[side, k, d], {"cell": x},
        )

    def late_half(j, k):
        return j * per + k * CHUNK >= frames_local - width

    def early_half(j, k):
        return j * per + k * CHUNK < width

    def far_copy(side, k):
        piece = pl.ds(k * CHUNK, CHUNK)
        by = reach if side == 0 else -reach
        return remote(
            first.at[:, piece], far.at[side, :, piece],
            far_s.at[side, k], far_r.at[side, k], at(block + by, x),
        )

    def out_copy(k):
        piece = pl.ds(k * CHUNK, CHUNK)
        return pltpu.make_async_copy(result.at[:, piece], out.at[:, piece], out_s.at[k])

    for i in range(6):
        local_weight(i).start()

    @pl.loop(0, steps)
    def _(k):
        local_in(k).start()

    barrier = pltpu.get_barrier_semaphore()
    for d in range(1, n_cell):
        pl.semaphore_signal(barrier, inc=1, device_id={"cell": peer(d)}, device_id_type=MESH)
    for by, cond in has.items():
        @pl.when(cond)
        def _():
            pl.semaphore_signal(
                barrier, inc=1, device_id=at(block + by, x), device_id_type=MESH
            )
    heard = n_cell - 1
    for cond in has.values():
        heard = heard + jnp.where(cond, 1, 0)
    pl.semaphore_wait(barrier, heard)

    for i in range(6):
        for d in range(1, n_sub):
            remote_weight(i, d).start()

    for k in range(min(AHEAD, steps)):
        for d in range(1, n_cell):
            remote_in(k, d).start()

    @pl.when(jnp.logical_not(has[-1]))
    def _():
        pad[:width] = jnp.zeros((width, cells_local, features), BF16)

    @pl.when(jnp.logical_not(has[1]))
    def _():
        pad[width + frames_local :] = jnp.zeros((width, cells_local, features), BF16)

    @pl.when(jnp.logical_not(has[-reach]))
    def _():
        far[0] = jnp.zeros(far.shape[1:], BF16)

    @pl.when(jnp.logical_not(has[reach]))
    def _():
        far[1] = jnp.zeros(far.shape[1:], BF16)

    def weight_ready(i):
        local_weight(i).wait()
        for d in range(1, n_sub):
            remote_weight(i, d).wait_recv()

    for i in range(4):
        weight_ready(i)

    def forward(k):
        for d in range(n_cell):
            if d:
                own_copy(k, d).wait_recv()

            @pl.when(jnp.logical_and(late_half(source(d), k), has[1]))
            def _():
                to_next(k, d).start()

            @pl.when(jnp.logical_and(early_half(source(d), k), has[-1]))
            def _():
                to_last(k, d).start()

    def block_step(k):
        @pl.when(k + AHEAD < steps)
        def _():
            for d in range(1, n_cell):
                remote_in(k + AHEAD, d).start()

        local_in(k).wait()
        for d in range(1, n_cell):
            remote_in(k, d).wait_recv()
        piece = pl.ds(k * CHUNK, CHUNK)
        residual = work[piece].reshape(CHUNK * cells, features).astype(F32)
        projected = dot(normalize(residual).astype(BF16), w_qkv[...]).astype(BF16)
        attended = attend(projected, CHUNK, cells, features)

        @pl.when(k >= 1)
        def _():
            forward(k - 1)

        mid = (residual + dot(attended, w_out[...])).astype(BF16).astype(F32)
        hidden = jax.nn.gelu(dot(normalize(mid).astype(BF16), w_up[...])).astype(BF16)
        done = (mid + dot(hidden, w_down[...])).astype(BF16)
        stage[piece] = done.reshape(CHUNK, cells, features)
        for d in range(1, n_cell):
            own_copy(k, d).start()
        pad[pl.ds(width + x * per + k * CHUNK, CHUNK)] = stage[piece, my_cells]

    def gather(ref, k, shift):
        parts = [
            ref[pl.ds(j * per + k * CHUNK + shift, CHUNK)].reshape(CHUNK * cells_local, features)
            for j in range(n_cell)
        ]
        return jnp.concatenate(parts, axis=0)

    def first_step(k):
        for d in range(n_cell):
            @pl.when(jnp.logical_and(late_half(source(d), k), has[-1]))
            def _():
                from_halo(0, k, d).wait_recv()

            @pl.when(jnp.logical_and(early_half(source(d), k), has[1]))
            def _():
                from_halo(1, k, d).wait_recv()
        value = gated(gather(pad, k, width), gather(pad, k, 0), gather(pad, k, 2 * width), w_first)
        first[:, pl.ds(k * CHUNK, CHUNK)] = value.reshape(n_cell, CHUNK, cells_local, features)

        @pl.when(has[reach])
        def _():
            far_copy(0, k).start()

        @pl.when(has[-reach])
        def _():
            far_copy(1, k).start()

    extra = 1 if steps >= 6 else 0
    late = steps - 2 * extra

    @pl.loop(0, steps)
    def _(k):
        block_step(k)

        @pl.when(k == min(1, steps - 1))
        def _():
            weight_ready(4)

        @pl.when(jnp.where(k < late, lax.rem(k, 2), 1) == 1)
        def _():
            first_step(jnp.where(k == steps - 1, (steps - 2) // 2 + extra, k // 2))

    forward(steps - 1)

    @pl.loop(steps // 2 + extra, steps)
    def _(k):
        first_step(k)

    weight_ready(5)

    @pl.loop(0, steps)
    def _(k):
        @pl.when(has[-reach])
        def _():
            far_copy(0, k).wait_recv()

        @pl.when(has[reach])
        def _():
            far_copy(1, k).wait_recv()

        piece = pl.ds(k * CHUNK, CHUNK)
        flat = (n_cell * CHUNK * cells_local, features)
        value = gated(
            first[:, piece].reshape(flat),
            far[0, :, piece].reshape(flat),
            far[1, :, piece].reshape(flat),
            w_second,
        )
        result[:, piece] = value.reshape(n_cell, CHUNK, cells_local, features)
        out_copy(k).start()

    for i in range(6):
        for d in range(1, n_sub):
            remote_weight(i, d).wait_send()

    @pl.loop(0, steps)
    def _(k):
        for d in range(n_cell):
            if d:
                remote_in(k, d).wait_send()
                own_copy(k, d).wait_send()

            @pl.when(jnp.logical_and(late_half(source(d), k), has[1]))
            def _():
                to_next(k, d).wait_send()

            @pl.when(jnp.logical_and(early_half(source(d), k), has[-1]))
            def _():
                to_last(k, d).wait_send()

        @pl.when(has[reach])
        def _():
            far_copy(0, k).wait_send()

        @pl.when(has[-reach])
        def _():
            far_copy(1, k).wait_send()

        out_copy(k).wait()


def regroup_kernel(
    sizes,
    frames, h_qkv, h_out, h_up, h_down, h_first, h_second,
    out,
    w_qkv, w_out, w_up, w_down, w_first, w_second,
    work, sect, first, result,
    ws, wr, wl, in_s, in_r, in_l, halo_s, halo_r, out_s, out_r, out_l,
):
    n_tm, n_cell, n_sub = sizes
    n_blocks = n_tm * n_sub
    per, classes, cells_local, features = frames.shape
    segments, span, cells, _ = first.shape
    group = span // per
    reach = group * n_sub
    steps = segments * group
    tm, x, sub = lax.axis_index("tm"), lax.axis_index("cell"), lax.axis_index("sub")
    block = tm * n_sub + sub
    mine = tm * n_cell + x

    home, own = lax.rem(block, reach) // group, block // reach
    my_slot = (block // reach) * group + lax.rem(block, group)
    my_cells = pl.ds(pl.multiple_of(x * cells_local, 16), cells_local)

    def remote(src, dst, s, r, where):
        return pltpu.make_async_remote_copy(
            src_ref=src, dst_ref=dst, send_sem=s, recv_sem=r, device_id=where, device_id_type=MESH
        )

    halves = (h_qkv, h_out, h_up, h_down, h_first, h_second)
    wholes = (w_qkv, w_out, w_up, w_down, w_first, w_second)

    def rows_of(half):
        size = half.shape[0]
        return pl.ds(pl.multiple_of(sub * size, 16), size)

    def local_weight(i):
        return pltpu.make_async_copy(halves[i], wholes[i].at[rows_of(halves[i])], wl.at[i])

    def remote_weight(i, d):
        return remote(
            halves[i], wholes[i].at[rows_of(halves[i])], ws.at[i, d - 1], wr.at[i, d - 1],
            {"sub": lax.rem(sub + d, n_sub)},
        )

    def weight_ready(i):
        local_weight(i).wait()
        for d in range(1, n_sub):
            remote_weight(i, d).wait_recv()

    def cells_of(j):
        return pl.ds(pl.multiple_of(j * cells_local, 16), cells_local)

    near = classes // group // 2
    moves = [(0, d, k) for d in range(near) for k in range(group)]
    moves += [(near, d, k) for k in range(group) for d in range(near)]
    level = block // group

    def in_chip(i):
        across, d, k = moves[i]
        base = lax.rem(level // near * near + across, 2 * near)
        return (base + lax.rem(level + d, near)) * group + lax.rem(block + group - k, group)

    def in_copy(i):
        to = in_chip(i)
        return remote(
            frames.at[:, to], work.at[my_slot, :, my_cells], in_s.at[i], in_r.at[my_slot, x],
            {"tm": to // n_cell, "cell": lax.rem(to, n_cell), "sub": home},
        )

    def in_away(i):
        return jnp.logical_not(jnp.logical_and(in_chip(i) == mine, home == sub))

    def in_local():
        return pltpu.make_async_copy(
            frames.at[:, mine], work.at[my_slot, :, my_cells], in_l.at[0]
        )

    def in_ready(h, p):
        slot = h * group + p
        for j in range(n_cell):
            here = jnp.logical_and(h * reach + sub * group + p == block, x == j)

            @pl.when(here)
            def _():
                in_local().wait()

            @pl.when(jnp.logical_not(here))
            def _():
                remote(
                    frames.at[:, 0], work.at[slot, :, cells_of(j)],
                    in_s.at[0], in_r.at[slot, j], {"cell": x},
                ).wait_recv()

    def halo_copy(side, h):
        at = h * n_sub + sub + (1 if side == 0 else -1)
        start, end = (span, 0) if side == 0 else (1, span + 1)
        to = at // n_sub
        return remote(
            sect.at[h, start], sect.at[to, end],
            halo_s.at[side, h], halo_r.at[side, to], {"sub": lax.rem(at, n_sub)},
        )

    def has_halo(side, h):
        at = h * n_sub + sub
        return at >= 1 if side == 0 else at + 1 < segments * n_sub

    def sends_halo(side, h):
        return has_halo(1 - side, h)

    def halo_ready(side, h):
        @pl.when(has_halo(side, h))
        def _():
            remote(
                sect.at[h, 1], sect.at[h, 0 if side == 0 else span + 1],
                halo_s.at[side, h], halo_r.at[side, h], {"cell": x},
            ).wait_recv()

    def out_target(h, f, j):
        to = h * reach + sub * group + f // per
        return to, jnp.logical_and(to == block, x == j)

    def out_copy(h, f, j):
        to, _ = out_target(h, f, j)
        part = lax.rem(f, per)
        return remote(
            result.at[h, f, cells_of(j)], out.at[part, mine],
            out_s.at[h, f, j], out_r.at[part, mine],
            {"tm": to // n_sub, "cell": j, "sub": lax.rem(to, n_sub)},
        )

    def out_local(h, f, j):
        part = lax.rem(f, per)
        return pltpu.make_async_copy(
            result.at[h, f, cells_of(j)], out.at[part, mine], out_l.at[part]
        )

    for i in range(6):
        local_weight(i).start()

    @pl.when(home == sub)
    def _():
        in_local().start()

    barrier = pltpu.get_barrier_semaphore()
    others = n_blocks * n_cell - 1
    rank = block * n_cell + x
    for d in range(1, others + 1):
        to = lax.rem(rank + d, others + 1)
        b = to // n_cell
        pl.semaphore_signal(
            barrier, inc=1, device_id_type=MESH,
            device_id={"tm": b // n_sub, "cell": lax.rem(to, n_cell), "sub": lax.rem(b, n_sub)},
        )
    pl.semaphore_wait(barrier, others)

    for d in range(1, n_sub):
        remote_weight(0, d).start()
    for i in range(len(moves)):
        @pl.when(in_away(i))
        def _():
            in_copy(i).start()
    for i in range(1, 6):
        for d in range(1, n_sub):
            remote_weight(i, d).start()

    for h in range(segments):
        for side in range(2):
            @pl.when(jnp.logical_not(has_halo(side, h)))
            def _():
                sect[h, 0 if side == 0 else span + 1] = jnp.zeros((cells, features), BF16)

    for i in range(4):
        weight_ready(i)

    def block_step(h, p):
        in_ready(h, p)
        residual = work[h * group + p].reshape(per * cells, features).astype(F32)
        projected = dot(normalize(residual).astype(BF16), w_qkv[...]).astype(BF16)
        attended = attend(projected, per, cells, features)
        mid = (residual + dot(attended, w_out[...])).astype(BF16).astype(F32)
        hidden = jax.nn.gelu(dot(normalize(mid).astype(BF16), w_up[...])).astype(BF16)
        done = (mid + dot(hidden, w_down[...])).astype(BF16)
        sect[h, pl.ds(1 + p * per, per)] = done.reshape(per, cells, features)
        for side, edge in ((0, group - 1), (1, 0)):
            @pl.when(jnp.logical_and(p == edge, sends_halo(side, h)))
            def _():
                halo_copy(side, h).start()

    def flat(ref, h, picks):
        return jnp.concatenate([ref[h, f] for f in picks], axis=0)

    def temporal(p):
        picks = [lax.rem(p * per + 1 + q, span) for q in range(per)]

        @pl.loop(0, segments)
        def _(h):
            for side in range(2):
                @pl.when(p == group - 1)
                def _():
                    halo_ready(side, h)
            value = gated(
                flat(sect, h, [f + 1 for f in picks]),
                flat(sect, h, picks),
                flat(sect, h, [f + 2 for f in picks]),
                w_first,
            )
            for q, f in enumerate(picks):
                first[h, f] = value[q * cells : (q + 1) * cells]

        @pl.loop(0, segments)
        def _(k):
            h = lax.rem(own + 1 + k, segments)
            value = gated_pair(flat(first, h, picks), flat(first, 1 - h, picks), w_second, h == 1)
            for q, f in enumerate(picks):
                result[h, f] = value[q * cells : (q + 1) * cells]
            for f in picks[::-1]:
                for j in range(n_cell):
                    _, here = out_target(h, f, j)

                    @pl.when(here)
                    def _():
                        out_local(h, f, j).start()

                    @pl.when(jnp.logical_not(here))
                    def _():
                        out_copy(h, f, j).start()

    def place(i):
        return lax.rem(mine + i, group)

    @pl.loop(0, steps)
    def _(t):
        across = jnp.logical_or(t == group - 1, t > group)
        i = jnp.where(t < group - 1, t, jnp.where(t > group, t - group, jnp.where(across, 0, t - 1)))
        block_step(jnp.where(across, 1 - own, own), place(i))

        @pl.when(t == 1)
        def _():
            weight_ready(4)
            weight_ready(5)

        @pl.when(jnp.logical_and(t >= group + 1, place(i - 1) != group - 1))
        def _():
            temporal(place(i - 1))

    left = jnp.where(place(group - 1) == group - 1, 1, 2)

    @pl.loop(0, left)
    def _(k):
        temporal(jnp.where(k == left - 1, group - 1, place(group - 1)))

    for r in range(classes):
        for part in range(per):
            here = jnp.logical_and(mine == r, home == sub)

            @pl.when(here)
            def _():
                pltpu.make_async_copy(
                    result.at[0, 0, my_cells], out.at[part, r], out_l.at[part]
                ).wait()

            @pl.when(jnp.logical_not(here))
            def _():
                remote(
                    result.at[0, 0, my_cells], out.at[part, r],
                    out_s.at[0, 0, 0], out_r.at[part, r], {"cell": x},
                ).wait_recv()

    for i in range(6):
        for d in range(1, n_sub):
            remote_weight(i, d).wait_send()
    for i in range(len(moves)):
        @pl.when(in_away(i))
        def _():
            in_copy(i).wait_send()
    for h in range(segments):
        for side in range(2):
            @pl.when(sends_halo(side, h))
            def _():
                halo_copy(side, h).wait_send()

        @pl.loop(0, span)
        def _(f):
            for j in range(n_cell):
                _, here = out_target(h, f, j)

                @pl.when(jnp.logical_not(here))
                def _():
                    out_copy(h, f, j).wait_send()


def regroup(sizes, frames, *halves):
    n_tm, n_cell, n_sub = sizes
    frames_local, cells_local, features = frames.shape
    classes = DILATION_FIRST
    per = frames_local // classes
    cells = n_cell * cells_local
    reach = DILATION_SECOND // frames_local
    group = reach // n_sub
    segments = n_tm * n_sub // reach
    span = group * per
    split = (per, classes, cells_local, features)
    dma = pltpu.SemaphoreType.DMA
    anywhere = pl.BlockSpec(memory_space=pl.ANY)
    call = pl.pallas_call(
        functools.partial(regroup_kernel, sizes),
        out_shape=pltpu.VMEM(split, BF16),
        in_specs=[anywhere] * 7,
        out_specs=anywhere,
        scratch_shapes=[pltpu.VMEM((n_sub * w.shape[0], w.shape[1]), BF16) for w in halves]
        + [
            pltpu.VMEM((segments * group, per, cells, features), BF16),
            pltpu.VMEM((segments, span + 2, cells, features), BF16),
            pltpu.VMEM((segments, span, cells, features), BF16),
            pltpu.VMEM((segments, span, cells, features), BF16),
            dma((6, n_sub - 1)), dma((6, n_sub - 1)), dma((6,)),
            dma((n_tm * n_cell,)), dma((segments * group, n_cell)), dma((1,)),
            dma((2, segments)), dma((2, segments)),
            dma((segments, span, n_cell)), dma((per, classes)), dma((per,)),
        ],
        compiler_params=pltpu.CompilerParams(
            collective_id=0, has_side_effects=True, vmem_limit_bytes=56 * 1024 * 1024
        ),
        name="video_regroup",
    )
    return call(frames.reshape(split), *halves).reshape(frames.shape)


def regroups(sizes, frames):
    n_tm, n_cell, n_sub = sizes
    frames_local = frames.shape[0]
    reach = DILATION_SECOND // frames_local
    return (
        n_tm * n_cell == DILATION_FIRST
        and n_sub >= 2
        and frames_local % DILATION_FIRST == 0
        and DILATION_SECOND % frames_local == 0
        and reach % n_sub == 0
        and reach // n_sub >= 2
        and n_tm * n_sub == 2 * reach
        and DILATION_FIRST % (2 * (reach // n_sub)) == 0
    )


def local(sizes, frames, *halves):
    if regroups(sizes, frames):
        return regroup(sizes, frames, *halves)
    _, n_cell, n_sub = sizes
    frames_local, cells_local, features = frames.shape
    per = frames_local // n_cell
    cells = n_cell * cells_local
    steps = per // CHUNK
    split = (n_cell, per, cells_local, features)
    dma = pltpu.SemaphoreType.DMA
    anywhere = pl.BlockSpec(memory_space=pl.ANY)
    call = pl.pallas_call(
        functools.partial(kernel, sizes),
        out_shape=jax.ShapeDtypeStruct(split, BF16),
        in_specs=[anywhere] * 7,
        out_specs=anywhere,
        scratch_shapes=[pltpu.VMEM((n_sub * w.shape[0], w.shape[1]), BF16) for w in halves]
        + [
            pltpu.VMEM((per, cells, features), BF16),
            pltpu.VMEM((per, cells, features), BF16),
            pltpu.VMEM((frames_local + 2 * DILATION_FIRST, cells_local, features), BF16),
            pltpu.VMEM(split, BF16),
            pltpu.VMEM((2,) + split, BF16),
            pltpu.VMEM(split, BF16),
            dma((6, n_sub - 1)), dma((6, n_sub - 1)), dma((6,)),
            dma((steps, n_cell - 1)), dma((steps, n_cell - 1)), dma((steps,)),
            dma((steps, n_cell - 1)), dma((steps, n_cell - 1)),
            dma((2, steps, n_cell)), dma((2, steps, n_cell)),
            dma((2, steps)), dma((2, steps)), dma((steps,)),
        ],
        compiler_params=pltpu.CompilerParams(
            collective_id=0, has_side_effects=True, vmem_limit_bytes=56 * 1024 * 1024
        ),
        name="video_block",
    )
    return call(frames, *halves).reshape(frames.shape)


def solution(mesh):
    sizes = (mesh.shape["tm"], mesh.shape["cell"], mesh.shape["sub"])
    placed = (P(("groups", "tm", "sub"), "cell", None),) + (P("sub", None),) * 6
    return jax.shard_map(
        functools.partial(local, sizes),
        mesh=mesh,
        in_specs=placed,
        out_specs=P(("groups", "tm", "sub"), "cell", None),
        check_vma=False,
    )
```

```python
import functools

import jax
import jax.numpy as jnp
from jax import lax
from jax.experimental import pallas as pl
from jax.experimental.pallas import tpu as pltpu
from jax.sharding import PartitionSpec as P

HEAD_DIM = 64
DILATION_FIRST = 16
DILATION_SECOND = 256
CHUNK = 2
AHEAD = 2
PAIR = 2 * HEAD_DIM
MESH = pl.DeviceIdType.MESH
F32 = jnp.float32
BF16 = jnp.bfloat16


def normalize(values):
    row_mean = jnp.mean(values, axis=-1, keepdims=True)
    centred = values - row_mean
    row_var = jnp.mean(centred * centred, axis=-1, keepdims=True)
    return centred * lax.rsqrt(row_var + 1e-05)


def dot(a, b):
    return jnp.dot(a, b, preferred_element_type=F32)


def attend(projected, frame_count, cells, features):
    lane = lax.broadcasted_iota(jnp.int32, (cells, PAIR), 1)
    scale = HEAD_DIM ** (-0.5)
    keep_a = jnp.where(lane < HEAD_DIM, scale, 0.0).astype(BF16)
    keep_b = jnp.where(lane < HEAD_DIM, 0.0, scale).astype(BF16)
    rows = []
    for f in range(frame_count):
        here = projected[f * cells : (f + 1) * cells]
        columns = []
        for p in range(features // PAIR):
            q = here[:, p * PAIR : (p + 1) * PAIR]
            k = here[:, features + p * PAIR : features + (p + 1) * PAIR]
            v = here[:, 2 * features + p * PAIR : 2 * features + (p + 1) * PAIR]
            stacked = jnp.concatenate([q * keep_a, q * keep_b], axis=0)
            scores = lax.dot_general(
                stacked, k, (((1,), (1,)), ((), ())), preferred_element_type=F32
            )
            exp_terms = jnp.exp(scores - jnp.max(scores, axis=-1, keepdims=True))
            probs = exp_terms * (1.0 / jnp.sum(exp_terms, axis=-1, keepdims=True))
            mixed = dot(probs.astype(BF16), v)
            columns.append(jnp.where(lane < HEAD_DIM, mixed[:cells], mixed[cells:]).astype(BF16))
        rows.append(jnp.concatenate(columns, axis=1))
    return jnp.concatenate(rows, axis=0)


def gated(center, earlier, later, weight_ref):
    features = center.shape[-1]
    preact = (
        dot(center, weight_ref[features : 2 * features])
        + dot(earlier, weight_ref[:features])
        + dot(later, weight_ref[2 * features :])
    )
    gate = 0.5 * jnp.tanh(0.5 * preact[:, features:]) + 0.5
    return (center.astype(F32) + jnp.tanh(preact[:, :features]) * gate).astype(BF16)


def gated_pair(center, other, weight_ref, earlier):
    features = center.shape[-1]
    other_rows = pl.ds(pl.multiple_of(jnp.where(earlier, 0, 2 * features), features), features)
    preact = dot(center, weight_ref[features : 2 * features]) + dot(other, weight_ref[other_rows])
    gate = 0.5 * jnp.tanh(0.5 * preact[:, features:]) + 0.5
    return (center.astype(F32) + jnp.tanh(preact[:, :features]) * gate).astype(BF16)


def kernel(
    sizes,
    frames, h_qkv, h_out, h_up, h_down, h_first, h_second,
    out,
    w_qkv, w_out, w_up, w_down, w_first, w_second,
    work, stage, pad, first, far, result,
    ws, wr, wl, in_s, in_r, in_l, own_s, own_r, halo_s, halo_r, far_s, far_r, out_s,
):
    n_tm, n_cell, n_sub = sizes
    n_blocks = n_tm * n_sub
    frames_local, cells_local, features = frames.shape
    per = frames_local // n_cell
    cells = n_cell * cells_local
    steps = per // CHUNK
    reach = DILATION_SECOND // frames_local
    width = DILATION_FIRST
    tm, x, sub = lax.axis_index("tm"), lax.axis_index("cell"), lax.axis_index("sub")
    block = tm * n_sub + sub

    def at(b, j):
        return {"tm": b // n_sub, "cell": j, "sub": lax.rem(b, n_sub)}

    def peer(d):
        return lax.rem(x + d, n_cell)

    def source(d):
        return lax.rem(x + n_cell - d, n_cell)

    def remote(src, dst, s, r, where):
        return pltpu.make_async_remote_copy(
            src_ref=src, dst_ref=dst, send_sem=s, recv_sem=r, device_id=where, device_id_type=MESH
        )

    has = {
        -1: block >= 1,
        1: block + 1 < n_blocks,
        -reach: block >= reach,
        reach: block + reach < n_blocks,
    }

    halves = (h_qkv, h_out, h_up, h_down, h_first, h_second)
    wholes = (w_qkv, w_out, w_up, w_down, w_first, w_second)

    def rows_of(half):
        size = half.shape[0]
        return pl.ds(pl.multiple_of(sub * size, 16), size)

    def local_weight(i):
        return pltpu.make_async_copy(halves[i], wholes[i].at[rows_of(halves[i])], wl.at[i])

    def remote_weight(i, d):
        return remote(
            halves[i], wholes[i].at[rows_of(halves[i])], ws.at[i, d - 1], wr.at[i, d - 1],
            {"sub": lax.rem(sub + d, n_sub)},
        )

    my_cells = pl.ds(pl.multiple_of(x * cells_local, 16), cells_local)

    def local_in(k):
        return pltpu.make_async_copy(
            frames.at[pl.ds(x * per + k * CHUNK, CHUNK)],
            work.at[pl.ds(k * CHUNK, CHUNK), my_cells],
            in_l.at[k],
        )

    def remote_in(k, d):
        return remote(
            frames.at[pl.ds(peer(d) * per + k * CHUNK, CHUNK)],
            work.at[pl.ds(k * CHUNK, CHUNK), my_cells],
            in_s.at[k, d - 1], in_r.at[k, d - 1], {"cell": peer(d)},
        )

    def staged(k, d):
        their_cells = pl.ds(pl.multiple_of(peer(d) * cells_local, 16), cells_local)
        return stage.at[pl.ds(k * CHUNK, CHUNK), their_cells]

    def own_copy(k, d):
        return remote(
            staged(k, d), pad.at[pl.ds(width + x * per + k * CHUNK, CHUNK)],
            own_s.at[k, d - 1], own_r.at[k, d - 1], {"cell": peer(d)},
        )

    def to_next(k, d):
        start = source(d) * per + k * CHUNK
        return remote(
            pad.at[pl.ds(width + start, CHUNK)],
            pad.at[pl.ds(start - (frames_local - width), CHUNK)],
            halo_s.at[0, k, d], halo_r.at[0, k, d], at(block + 1, x),
        )

    def to_last(k, d):
        start = width + source(d) * per + k * CHUNK
        return remote(
            pad.at[pl.ds(start, CHUNK)], pad.at[pl.ds(start + frames_local, CHUNK)],
            halo_s.at[1, k, d], halo_r.at[1, k, d], at(block - 1, x),
        )

    def from_halo(side, k, d):
        return remote(
            pad.at[pl.ds(width, CHUNK)], pad.at[pl.ds(0, CHUNK)],
            halo_s.at[side, k, d], halo_r.at[side, k, d], {"cell": x},
        )

    def late_half(j, k):
        return j * per + k * CHUNK >= frames_local - width

    def early_half(j, k):
        return j * per + k * CHUNK < width

    def far_copy(side, k):
        piece = pl.ds(k * CHUNK, CHUNK)
        by = reach if side == 0 else -reach
        return remote(
            first.at[:, piece], far.at[side, :, piece],
            far_s.at[side, k], far_r.at[side, k], at(block + by, x),
        )

    def out_copy(k):
        piece = pl.ds(k * CHUNK, CHUNK)
        return pltpu.make_async_copy(result.at[:, piece], out.at[:, piece], out_s.at[k])

    for i in range(6):
        local_weight(i).start()

    @pl.loop(0, steps)
    def _(k):
        local_in(k).start()

    barrier = pltpu.get_barrier_semaphore()
    for d in range(1, n_cell):
        pl.semaphore_signal(barrier, inc=1, device_id={"cell": peer(d)}, device_id_type=MESH)
    for by, cond in has.items():
        @pl.when(cond)
        def _():
            pl.semaphore_signal(
                barrier, inc=1, device_id=at(block + by, x), device_id_type=MESH
            )
    heard = n_cell - 1
    for cond in has.values():
        heard = heard + jnp.where(cond, 1, 0)
    pl.semaphore_wait(barrier, heard)

    for i in range(6):
        for d in range(1, n_sub):
            remote_weight(i, d).start()

    for k in range(min(AHEAD, steps)):
        for d in range(1, n_cell):
            remote_in(k, d).start()

    @pl.when(jnp.logical_not(has[-1]))
    def _():
        pad[:width] = jnp.zeros((width, cells_local, features), BF16)

    @pl.when(jnp.logical_not(has[1]))
    def _():
        pad[width + frames_local :] = jnp.zeros((width, cells_local, features), BF16)

    @pl.when(jnp.logical_not(has[-reach]))
    def _():
        far[0] = jnp.zeros(far.shape[1:], BF16)

    @pl.when(jnp.logical_not(has[reach]))
    def _():
        far[1] = jnp.zeros(far.shape[1:], BF16)

    def weight_ready(i):
        local_weight(i).wait()
        for d in range(1, n_sub):
            remote_weight(i, d).wait_recv()

    for i in range(4):
        weight_ready(i)

    def forward(k):
        for d in range(n_cell):
            if d:
                own_copy(k, d).wait_recv()

            @pl.when(jnp.logical_and(late_half(source(d), k), has[1]))
            def _():
                to_next(k, d).start()

            @pl.when(jnp.logical_and(early_half(source(d), k), has[-1]))
            def _():
                to_last(k, d).start()

    def block_step(k):
        @pl.when(k + AHEAD < steps)
        def _():
            for d in range(1, n_cell):
                remote_in(k + AHEAD, d).start()

        local_in(k).wait()
        for d in range(1, n_cell):
            remote_in(k, d).wait_recv()
        piece = pl.ds(k * CHUNK, CHUNK)
        residual = work[piece].reshape(CHUNK * cells, features).astype(F32)
        projected = dot(normalize(residual).astype(BF16), w_qkv[...]).astype(BF16)
        attended = attend(projected, CHUNK, cells, features)

        @pl.when(k >= 1)
        def _():
            forward(k - 1)

        mid = (residual + dot(attended, w_out[...])).astype(BF16).astype(F32)
        hidden = jax.nn.gelu(dot(normalize(mid).astype(BF16), w_up[...])).astype(BF16)
        done = (mid + dot(hidden, w_down[...])).astype(BF16)
        stage[piece] = done.reshape(CHUNK, cells, features)
        for d in range(1, n_cell):
            own_copy(k, d).start()
        pad[pl.ds(width + x * per + k * CHUNK, CHUNK)] = stage[piece, my_cells]

    def gather(ref, k, shift):
        parts = [
            ref[pl.ds(j * per + k * CHUNK + shift, CHUNK)].reshape(CHUNK * cells_local, features)
            for j in range(n_cell)
        ]
        return jnp.concatenate(parts, axis=0)

    def first_step(k):
        for d in range(n_cell):
            @pl.when(jnp.logical_and(late_half(source(d), k), has[-1]))
            def _():
                from_halo(0, k, d).wait_recv()

            @pl.when(jnp.logical_and(early_half(source(d), k), has[1]))
            def _():
                from_halo(1, k, d).wait_recv()
        value = gated(gather(pad, k, width), gather(pad, k, 0), gather(pad, k, 2 * width), w_first)
        first[:, pl.ds(k * CHUNK, CHUNK)] = value.reshape(n_cell, CHUNK, cells_local, features)

        @pl.when(has[reach])
        def _():
            far_copy(0, k).start()

        @pl.when(has[-reach])
        def _():
            far_copy(1, k).start()

    extra = 1 if steps >= 6 else 0
    late = steps - 2 * extra

    @pl.loop(0, steps)
    def _(k):
        block_step(k)

        @pl.when(k == min(1, steps - 1))
        def _():
            weight_ready(4)

        @pl.when(jnp.where(k < late, lax.rem(k, 2), 1) == 1)
        def _():
            first_step(jnp.where(k == steps - 1, (steps - 2) // 2 + extra, k // 2))

    forward(steps - 1)

    @pl.loop(steps // 2 + extra, steps)
    def _(k):
        first_step(k)

    weight_ready(5)

    @pl.loop(0, steps)
    def _(k):
        @pl.when(has[-reach])
        def _():
            far_copy(0, k).wait_recv()

        @pl.when(has[reach])
        def _():
            far_copy(1, k).wait_recv()

        piece = pl.ds(k * CHUNK, CHUNK)
        flat = (n_cell * CHUNK * cells_local, features)
        value = gated(
            first[:, piece].reshape(flat),
            far[0, :, piece].reshape(flat),
            far[1, :, piece].reshape(flat),
            w_second,
        )
        result[:, piece] = value.reshape(n_cell, CHUNK, cells_local, features)
        out_copy(k).start()

    for i in range(6):
        for d in range(1, n_sub):
            remote_weight(i, d).wait_send()

    @pl.loop(0, steps)
    def _(k):
        for d in range(n_cell):
            if d:
                remote_in(k, d).wait_send()
                own_copy(k, d).wait_send()

            @pl.when(jnp.logical_and(late_half(source(d), k), has[1]))
            def _():
                to_next(k, d).wait_send()

            @pl.when(jnp.logical_and(early_half(source(d), k), has[-1]))
            def _():
                to_last(k, d).wait_send()

        @pl.when(has[reach])
        def _():
            far_copy(0, k).wait_send()

        @pl.when(has[-reach])
        def _():
            far_copy(1, k).wait_send()

        out_copy(k).wait()


def regroup_kernel(
    sizes,
    frames, h_qkv, h_out, h_up, h_down, h_first, h_second,
    out,
    w_qkv, w_out, w_up, w_down, w_first, w_second,
    work, sect, first, result,
    ws, wr, wl, in_s, in_r, in_l, halo_s, halo_r, out_s, out_r, out_l, met,
):
    n_tm, n_cell, n_sub = sizes
    n_blocks = n_tm * n_sub
    per, classes, cells_local, features = frames.shape
    segments, span, cells, _ = first.shape
    group = span // per
    reach = group * n_sub
    steps = segments * group
    tm, x, sub = lax.axis_index("tm"), lax.axis_index("cell"), lax.axis_index("sub")
    block = tm * n_sub + sub
    mine = tm * n_cell + x

    home, own = lax.rem(block, reach) // group, block // reach
    my_slot = (block // reach) * group + lax.rem(block, group)
    my_cells = pl.ds(pl.multiple_of(x * cells_local, 16), cells_local)

    def remote(src, dst, s, r, where):
        return pltpu.make_async_remote_copy(
            src_ref=src, dst_ref=dst, send_sem=s, recv_sem=r, device_id=where, device_id_type=MESH
        )

    halves = (h_qkv, h_out, h_up, h_down, h_first, h_second)
    wholes = (w_qkv, w_out, w_up, w_down, w_first, w_second)

    def rows_of(half):
        size = half.shape[0]
        return pl.ds(pl.multiple_of(sub * size, 16), size)

    def local_weight(i):
        return pltpu.make_async_copy(halves[i], wholes[i].at[rows_of(halves[i])], wl.at[i])

    def remote_weight(i, d):
        return remote(
            halves[i], wholes[i].at[rows_of(halves[i])], ws.at[i, d - 1], wr.at[i, d - 1],
            {"sub": lax.rem(sub + d, n_sub)},
        )

    def weight_ready(i):
        local_weight(i).wait()
        for d in range(1, n_sub):
            remote_weight(i, d).wait_recv()

    def cells_of(j):
        return pl.ds(pl.multiple_of(j * cells_local, 16), cells_local)

    near = classes // group // 2
    lanes = group // n_cell
    level, turn = block // group, lax.rem(mine, group)

    def shift(a, k, sign):
        high = lax.rem(a // n_cell + lanes + sign * (k // n_cell), lanes)
        return high * n_cell + lax.rem(a + n_cell + sign * (k % n_cell), n_cell)

    def in_chip(across, d, k):
        base = lax.rem(level // near * near + near * across, 2 * near)
        return (base + lax.rem(level + d, near)) * group + shift(lax.rem(block, group), k, -1)

    def in_copy(across, d, k):
        to = in_chip(across, d, k)
        return remote(
            frames.at[:, to], work.at[my_slot, :, my_cells],
            in_s.at[across, d, k], in_r.at[my_slot, x],
            {"tm": to // n_cell, "cell": lax.rem(to, n_cell), "sub": home},
        )

    def in_away(across, d, k):
        return jnp.logical_not(jnp.logical_and(in_chip(across, d, k) == mine, home == sub))

    first_turn = shift(lax.rem(block, group), turn, -1)

    def in_local():
        return pltpu.make_async_copy(
            frames.at[:, mine], work.at[my_slot, :, my_cells], in_l.at[0]
        )

    def in_ready(h, p):
        slot = h * group + p
        for j in range(n_cell):
            here = jnp.logical_and(h * reach + sub * group + p == block, x == j)

            @pl.when(here)
            def _():
                in_local().wait()

            @pl.when(jnp.logical_not(here))
            def _():
                remote(
                    frames.at[:, 0], work.at[slot, :, cells_of(j)],
                    in_s.at[0, 0, 0], in_r.at[slot, j], {"cell": x},
                ).wait_recv()

    def halo_copy(side, h):
        at = h * n_sub + sub + (1 if side == 0 else -1)
        start, end = (span, 0) if side == 0 else (1, span + 1)
        to = at // n_sub
        return remote(
            sect.at[h, start], sect.at[to, end],
            halo_s.at[side, h], halo_r.at[side, to], {"sub": lax.rem(at, n_sub)},
        )

    def has_halo(side, h):
        at = h * n_sub + sub
        return at >= 1 if side == 0 else at + 1 < segments * n_sub

    def sends_halo(side, h):
        return has_halo(1 - side, h)

    def halo_ready(side, h):
        @pl.when(has_halo(side, h))
        def _():
            remote(
                sect.at[h, 1], sect.at[h, 0 if side == 0 else span + 1],
                halo_s.at[side, h], halo_r.at[side, h], {"cell": x},
            ).wait_recv()

    def out_target(h, f, j):
        to = h * reach + sub * group + f // per
        return to, jnp.logical_and(to == block, x == j)

    def out_copy(h, f, j):
        to, _ = out_target(h, f, j)
        part = lax.rem(f, per)
        return remote(
            result.at[h, f, cells_of(j)], out.at[part, mine],
            out_s.at[h, f, j], out_r.at[part, mine],
            {"tm": to // n_sub, "cell": j, "sub": lax.rem(to, n_sub)},
        )

    def out_local(h, f, j):
        part = lax.rem(f, per)
        return pltpu.make_async_copy(
            result.at[h, f, cells_of(j)], out.at[part, mine], out_l.at[part]
        )

    for i in range(6):
        local_weight(i).start()

    @pl.when(home == sub)
    def _():
        in_local().start()

    column = 2 * near * n_sub
    rank, lane = (tm // lanes) * n_sub + sub, lax.rem(tm, lanes)
    beside = [{"tm": tm, "cell": lax.rem(x + e, n_cell), "sub": sub} for e in range(1, n_cell)]
    below = [{"tm": tm - lane + lax.rem(lane + e, lanes), "cell": x, "sub": sub} for e in range(1, lanes)]
    barrier = pltpu.get_barrier_semaphore()
    for e in range(1, column):
        to = lax.rem(rank + e, column)
        pl.semaphore_signal(
            barrier, inc=1, device_id_type=MESH,
            device_id={"tm": to // n_sub * lanes + lane, "cell": x, "sub": lax.rem(to, n_sub)},
        )
    for where in beside + below:
        pl.semaphore_signal(barrier, inc=1, device_id=where, device_id_type=MESH)
    pl.semaphore_wait(barrier, column - 1 + len(beside) + len(below))

    for across in (1, 0):
        for d in range(near):
            @pl.when(in_away(across, d, first_turn))
            def _():
                in_copy(across, d, first_turn).start()
    for d in range(1, n_sub):
        remote_weight(0, d).start()

    for i, (around, count) in enumerate(((beside, len(beside)), (below, len(below)))):
        for where in around:
            pl.semaphore_signal(met.at[i], inc=1, device_id=where, device_id_type=MESH)
        pl.semaphore_wait(met.at[i], count)

    for across, d, k in [(0, d, k) for d in range(near) for k in range(group)] + [
        (1, d, k) for k in range(group) for d in range(near)
    ]:
        @pl.when(k != first_turn)
        def _():
            in_copy(across, d, k).start()
    for i in range(1, 6):
        for d in range(1, n_sub):
            remote_weight(i, d).start()

    for h in range(segments):
        for side in range(2):
            @pl.when(jnp.logical_not(has_halo(side, h)))
            def _():
                sect[h, 0 if side == 0 else span + 1] = jnp.zeros((cells, features), BF16)

    for i in range(4):
        weight_ready(i)

    def block_step(h, p):
        in_ready(h, p)
        residual = work[h * group + p].reshape(per * cells, features).astype(F32)
        projected = dot(normalize(residual).astype(BF16), w_qkv[...]).astype(BF16)
        attended = attend(projected, per, cells, features)
        mid = (residual + dot(attended, w_out[...])).astype(BF16).astype(F32)
        hidden = jax.nn.gelu(dot(normalize(mid).astype(BF16), w_up[...])).astype(BF16)
        done = (mid + dot(hidden, w_down[...])).astype(BF16)
        sect[h, pl.ds(1 + p * per, per)] = done.reshape(per, cells, features)
        for side, edge in ((0, group - 1), (1, 0)):
            @pl.when(jnp.logical_and(p == edge, sends_halo(side, h)))
            def _():
                halo_copy(side, h).start()

    def flat(ref, h, picks):
        return jnp.concatenate([ref[h, f] for f in picks], axis=0)

    def temporal(p):
        picks = [lax.rem(p * per + 1 + q, span) for q in range(per)]

        @pl.loop(0, segments)
        def _(h):
            for side in range(2):
                @pl.when(p == group - 1)
                def _():
                    halo_ready(side, h)
            value = gated(
                flat(sect, h, [f + 1 for f in picks]),
                flat(sect, h, picks),
                flat(sect, h, [f + 2 for f in picks]),
                w_first,
            )
            for q, f in enumerate(picks):
                first[h, f] = value[q * cells : (q + 1) * cells]

        @pl.loop(0, segments)
        def _(k):
            h = lax.rem(own + 1 + k, segments)
            value = gated_pair(flat(first, h, picks), flat(first, 1 - h, picks), w_second, h == 1)
            for q, f in enumerate(picks):
                result[h, f] = value[q * cells : (q + 1) * cells]
            for f, e in [(f, e) for f in picks[::-1] for e in range(n_cell)]:
                j = lax.rem(x + 1 + e, n_cell)
                _, here = out_target(h, f, j)

                @pl.when(here)
                def _():
                    out_local(h, f, j).start()

                @pl.when(jnp.logical_not(here))
                def _():
                    out_copy(h, f, j).start()

    def position(p):
        return shift(lax.rem(p + group, group), turn, -1)

    @pl.loop(0, steps)
    def _(t):
        across = jnp.logical_or(t == group - 1, t > group)
        i = jnp.where(t < group - 1, t, jnp.where(t > group, t - group, jnp.where(across, 0, t - 1)))
        p = shift(turn, i, 1)
        block_step(jnp.where(across, 1 - own, own), p)

        @pl.when(t == 1)
        def _():
            weight_ready(4)
            weight_ready(5)

        @pl.when(t > group)
        def _():
            @pl.loop(0, 3)
            def _(m):
                q = jnp.where(m == 2, group - 1, p - 1 + m)
                both = jnp.logical_and(position(q) <= i, position(q + 1) <= i)
                inner = jnp.logical_and(q >= 0, q < group - 1)

                @pl.when(jnp.where(m == 2, i == group - 1, jnp.logical_and(both, inner)))
                def _():
                    temporal(q)

    for r in range(classes):
        for part in range(per):
            here = jnp.logical_and(mine == r, home == sub)

            @pl.when(here)
            def _():
                pltpu.make_async_copy(
                    result.at[0, 0, my_cells], out.at[part, r], out_l.at[part]
                ).wait()

            @pl.when(jnp.logical_not(here))
            def _():
                remote(
                    result.at[0, 0, my_cells], out.at[part, r],
                    out_s.at[0, 0, 0], out_r.at[part, r], {"cell": x},
                ).wait_recv()

    for i in range(6):
        for d in range(1, n_sub):
            remote_weight(i, d).wait_send()
    for across, d, k in [(a, d, k) for a in range(2) for d in range(near) for k in range(group)]:
        @pl.when(in_away(across, d, k))
        def _():
            in_copy(across, d, k).wait_send()
    for h in range(segments):
        for side in range(2):
            @pl.when(sends_halo(side, h))
            def _():
                halo_copy(side, h).wait_send()

        @pl.loop(0, span)
        def _(f):
            for j in range(n_cell):
                _, here = out_target(h, f, j)

                @pl.when(jnp.logical_not(here))
                def _():
                    out_copy(h, f, j).wait_send()


def regroup(sizes, frames, *halves):
    n_tm, n_cell, n_sub = sizes
    frames_local, cells_local, features = frames.shape
    classes = DILATION_FIRST
    per = frames_local // classes
    cells = n_cell * cells_local
    reach = DILATION_SECOND // frames_local
    group = reach // n_sub
    segments = n_tm * n_sub // reach
    span = group * per
    split = (per, classes, cells_local, features)
    dma = pltpu.SemaphoreType.DMA
    anywhere = pl.BlockSpec(memory_space=pl.ANY)
    call = pl.pallas_call(
        functools.partial(regroup_kernel, sizes),
        out_shape=pltpu.VMEM(split, BF16),
        in_specs=[anywhere] * 7,
        out_specs=anywhere,
        scratch_shapes=[pltpu.VMEM((n_sub * w.shape[0], w.shape[1]), BF16) for w in halves]
        + [
            pltpu.VMEM((segments * group, per, cells, features), BF16),
            pltpu.VMEM((segments, span + 2, cells, features), BF16),
            pltpu.VMEM((segments, span, cells, features), BF16),
            pltpu.VMEM((segments, span, cells, features), BF16),
            dma((6, n_sub - 1)), dma((6, n_sub - 1)), dma((6,)),
            dma((2, classes // group // 2, group)), dma((segments * group, n_cell)), dma((1,)),
            dma((2, segments)), dma((2, segments)),
            dma((segments, span, n_cell)), dma((per, classes)), dma((per,)),
            pltpu.SemaphoreType.REGULAR((2,)),
        ],
        compiler_params=pltpu.CompilerParams(
            collective_id=0, has_side_effects=True, vmem_limit_bytes=56 * 1024 * 1024
        ),
        name="video_regroup",
    )
    return call(frames.reshape(split), *halves).reshape(frames.shape)


def regroups(sizes, frames):
    n_tm, n_cell, n_sub = sizes
    frames_local = frames.shape[0]
    reach = DILATION_SECOND // frames_local
    return (
        n_tm * n_cell == DILATION_FIRST
        and n_sub >= 2
        and frames_local % DILATION_FIRST == 0
        and DILATION_SECOND % frames_local == 0
        and reach % n_sub == 0
        and reach // n_sub >= 2
        and n_tm * n_sub == 2 * reach
        and DILATION_FIRST % (2 * (reach // n_sub)) == 0
        and reach // n_sub % n_cell == 0
    )


def local(sizes, frames, *halves):
    if regroups(sizes, frames):
        return regroup(sizes, frames, *halves)
    _, n_cell, n_sub = sizes
    frames_local, cells_local, features = frames.shape
    per = frames_local // n_cell
    cells = n_cell * cells_local
    steps = per // CHUNK
    split = (n_cell, per, cells_local, features)
    dma = pltpu.SemaphoreType.DMA
    anywhere = pl.BlockSpec(memory_space=pl.ANY)
    call = pl.pallas_call(
        functools.partial(kernel, sizes),
        out_shape=jax.ShapeDtypeStruct(split, BF16),
        in_specs=[anywhere] * 7,
        out_specs=anywhere,
        scratch_shapes=[pltpu.VMEM((n_sub * w.shape[0], w.shape[1]), BF16) for w in halves]
        + [
            pltpu.VMEM((per, cells, features), BF16),
            pltpu.VMEM((per, cells, features), BF16),
            pltpu.VMEM((frames_local + 2 * DILATION_FIRST, cells_local, features), BF16),
            pltpu.VMEM(split, BF16),
            pltpu.VMEM((2,) + split, BF16),
            pltpu.VMEM(split, BF16),
            dma((6, n_sub - 1)), dma((6, n_sub - 1)), dma((6,)),
            dma((steps, n_cell - 1)), dma((steps, n_cell - 1)), dma((steps,)),
            dma((steps, n_cell - 1)), dma((steps, n_cell - 1)),
            dma((2, steps, n_cell)), dma((2, steps, n_cell)),
            dma((2, steps)), dma((2, steps)), dma((steps,)),
        ],
        compiler_params=pltpu.CompilerParams(
            collective_id=0, has_side_effects=True, vmem_limit_bytes=56 * 1024 * 1024
        ),
        name="video_block",
    )
    return call(frames, *halves).reshape(frames.shape)


def solution(mesh):
    sizes = (mesh.shape["tm"], mesh.shape["cell"], mesh.shape["sub"])
    placed = (P(("groups", "tm", "sub"), "cell", None),) + (P("sub", None),) * 6
    return jax.shard_map(
        functools.partial(local, sizes),
        mesh=mesh,
        in_specs=placed,
        out_specs=P(("groups", "tm", "sub"), "cell", None),
        check_vma=False,
    )
```

```python
import functools

import jax
import jax.numpy as jnp
from jax import lax
from jax.experimental import pallas as pl
from jax.experimental.pallas import tpu as pltpu
from jax.sharding import PartitionSpec as P

HEAD_DIM = 64
DILATION_FIRST = 16
DILATION_SECOND = 256
CHUNK = 2
AHEAD = 2
PAIR = 2 * HEAD_DIM
MESH = pl.DeviceIdType.MESH
F32 = jnp.float32
BF16 = jnp.bfloat16


def normalize(values):
    row_mean = jnp.mean(values, axis=-1, keepdims=True)
    centred = values - row_mean
    row_var = jnp.mean(centred * centred, axis=-1, keepdims=True)
    return centred * lax.rsqrt(row_var + 1e-05)


def dot(a, b):
    return jnp.dot(a, b, preferred_element_type=F32)


def attend(projected, frame_count, cells, features):
    lane = lax.broadcasted_iota(jnp.int32, (cells, PAIR), 1)
    scale = HEAD_DIM ** (-0.5)
    keep_a = jnp.where(lane < HEAD_DIM, scale, 0.0).astype(BF16)
    keep_b = jnp.where(lane < HEAD_DIM, 0.0, scale).astype(BF16)
    rows = []
    for f in range(frame_count):
        here = projected[f * cells : (f + 1) * cells]
        columns = []
        for p in range(features // PAIR):
            q = here[:, p * PAIR : (p + 1) * PAIR]
            k = here[:, features + p * PAIR : features + (p + 1) * PAIR]
            v = here[:, 2 * features + p * PAIR : 2 * features + (p + 1) * PAIR]
            stacked = jnp.concatenate([q * keep_a, q * keep_b], axis=0)
            scores = lax.dot_general(
                stacked, k, (((1,), (1,)), ((), ())), preferred_element_type=F32
            )
            exp_terms = jnp.exp(scores - jnp.max(scores, axis=-1, keepdims=True))
            probs = exp_terms * (1.0 / jnp.sum(exp_terms, axis=-1, keepdims=True))
            mixed = dot(probs.astype(BF16), v)
            columns.append(jnp.where(lane < HEAD_DIM, mixed[:cells], mixed[cells:]).astype(BF16))
        rows.append(jnp.concatenate(columns, axis=1))
    return jnp.concatenate(rows, axis=0)


def gated(center, earlier, later, weight_ref):
    features = center.shape[-1]
    preact = (
        dot(center, weight_ref[features : 2 * features])
        + dot(earlier, weight_ref[:features])
        + dot(later, weight_ref[2 * features :])
    )
    gate = 0.5 * jnp.tanh(0.5 * preact[:, features:]) + 0.5
    return (center.astype(F32) + jnp.tanh(preact[:, :features]) * gate).astype(BF16)


def gated_pair(center, other, weight_ref, earlier):
    features = center.shape[-1]
    other_rows = pl.ds(pl.multiple_of(jnp.where(earlier, 0, 2 * features), features), features)
    preact = dot(center, weight_ref[features : 2 * features]) + dot(other, weight_ref[other_rows])
    gate = 0.5 * jnp.tanh(0.5 * preact[:, features:]) + 0.5
    return (center.astype(F32) + jnp.tanh(preact[:, :features]) * gate).astype(BF16)


def kernel(
    sizes,
    frames, h_qkv, h_out, h_up, h_down, h_first, h_second,
    out,
    w_qkv, w_out, w_up, w_down, w_first, w_second,
    work, stage, pad, first, far, result,
    ws, wr, wl, in_s, in_r, in_l, own_s, own_r, halo_s, halo_r, far_s, far_r, out_s,
):
    n_tm, n_cell, n_sub = sizes
    n_blocks = n_tm * n_sub
    frames_local, cells_local, features = frames.shape
    per = frames_local // n_cell
    cells = n_cell * cells_local
    steps = per // CHUNK
    reach = DILATION_SECOND // frames_local
    width = DILATION_FIRST
    tm, x, sub = lax.axis_index("tm"), lax.axis_index("cell"), lax.axis_index("sub")
    block = tm * n_sub + sub

    def at(b, j):
        return {"tm": b // n_sub, "cell": j, "sub": lax.rem(b, n_sub)}

    def peer(d):
        return lax.rem(x + d, n_cell)

    def source(d):
        return lax.rem(x + n_cell - d, n_cell)

    def remote(src, dst, s, r, where):
        return pltpu.make_async_remote_copy(
            src_ref=src, dst_ref=dst, send_sem=s, recv_sem=r, device_id=where, device_id_type=MESH
        )

    has = {
        -1: block >= 1,
        1: block + 1 < n_blocks,
        -reach: block >= reach,
        reach: block + reach < n_blocks,
    }

    halves = (h_qkv, h_out, h_up, h_down, h_first, h_second)
    wholes = (w_qkv, w_out, w_up, w_down, w_first, w_second)

    def rows_of(half):
        size = half.shape[0]
        return pl.ds(pl.multiple_of(sub * size, 16), size)

    def local_weight(i):
        return pltpu.make_async_copy(halves[i], wholes[i].at[rows_of(halves[i])], wl.at[i])

    def remote_weight(i, d):
        return remote(
            halves[i], wholes[i].at[rows_of(halves[i])], ws.at[i, d - 1], wr.at[i, d - 1],
            {"sub": lax.rem(sub + d, n_sub)},
        )

    my_cells = pl.ds(pl.multiple_of(x * cells_local, 16), cells_local)

    def local_in(k):
        return pltpu.make_async_copy(
            frames.at[pl.ds(x * per + k * CHUNK, CHUNK)],
            work.at[pl.ds(k * CHUNK, CHUNK), my_cells],
            in_l.at[k],
        )

    def remote_in(k, d):
        return remote(
            frames.at[pl.ds(peer(d) * per + k * CHUNK, CHUNK)],
            work.at[pl.ds(k * CHUNK, CHUNK), my_cells],
            in_s.at[k, d - 1], in_r.at[k, d - 1], {"cell": peer(d)},
        )

    def staged(k, d):
        their_cells = pl.ds(pl.multiple_of(peer(d) * cells_local, 16), cells_local)
        return stage.at[pl.ds(k * CHUNK, CHUNK), their_cells]

    def own_copy(k, d):
        return remote(
            staged(k, d), pad.at[pl.ds(width + x * per + k * CHUNK, CHUNK)],
            own_s.at[k, d - 1], own_r.at[k, d - 1], {"cell": peer(d)},
        )

    def to_next(k, d):
        start = source(d) * per + k * CHUNK
        return remote(
            pad.at[pl.ds(width + start, CHUNK)],
            pad.at[pl.ds(start - (frames_local - width), CHUNK)],
            halo_s.at[0, k, d], halo_r.at[0, k, d], at(block + 1, x),
        )

    def to_last(k, d):
        start = width + source(d) * per + k * CHUNK
        return remote(
            pad.at[pl.ds(start, CHUNK)], pad.at[pl.ds(start + frames_local, CHUNK)],
            halo_s.at[1, k, d], halo_r.at[1, k, d], at(block - 1, x),
        )

    def from_halo(side, k, d):
        return remote(
            pad.at[pl.ds(width, CHUNK)], pad.at[pl.ds(0, CHUNK)],
            halo_s.at[side, k, d], halo_r.at[side, k, d], {"cell": x},
        )

    def late_half(j, k):
        return j * per + k * CHUNK >= frames_local - width

    def early_half(j, k):
        return j * per + k * CHUNK < width

    def far_copy(side, k):
        piece = pl.ds(k * CHUNK, CHUNK)
        by = reach if side == 0 else -reach
        return remote(
            first.at[:, piece], far.at[side, :, piece],
            far_s.at[side, k], far_r.at[side, k], at(block + by, x),
        )

    def out_copy(k):
        piece = pl.ds(k * CHUNK, CHUNK)
        return pltpu.make_async_copy(result.at[:, piece], out.at[:, piece], out_s.at[k])

    for i in range(6):
        local_weight(i).start()

    @pl.loop(0, steps)
    def _(k):
        local_in(k).start()

    barrier = pltpu.get_barrier_semaphore()
    for d in range(1, n_cell):
        pl.semaphore_signal(barrier, inc=1, device_id={"cell": peer(d)}, device_id_type=MESH)
    for by, cond in has.items():
        @pl.when(cond)
        def _():
            pl.semaphore_signal(
                barrier, inc=1, device_id=at(block + by, x), device_id_type=MESH
            )
    heard = n_cell - 1
    for cond in has.values():
        heard = heard + jnp.where(cond, 1, 0)
    pl.semaphore_wait(barrier, heard)

    for i in range(6):
        for d in range(1, n_sub):
            remote_weight(i, d).start()

    for k in range(min(AHEAD, steps)):
        for d in range(1, n_cell):
            remote_in(k, d).start()

    @pl.when(jnp.logical_not(has[-1]))
    def _():
        pad[:width] = jnp.zeros((width, cells_local, features), BF16)

    @pl.when(jnp.logical_not(has[1]))
    def _():
        pad[width + frames_local :] = jnp.zeros((width, cells_local, features), BF16)

    @pl.when(jnp.logical_not(has[-reach]))
    def _():
        far[0] = jnp.zeros(far.shape[1:], BF16)

    @pl.when(jnp.logical_not(has[reach]))
    def _():
        far[1] = jnp.zeros(far.shape[1:], BF16)

    def weight_ready(i):
        local_weight(i).wait()
        for d in range(1, n_sub):
            remote_weight(i, d).wait_recv()

    for i in range(4):
        weight_ready(i)

    def forward(k):
        for d in range(n_cell):
            if d:
                own_copy(k, d).wait_recv()

            @pl.when(jnp.logical_and(late_half(source(d), k), has[1]))
            def _():
                to_next(k, d).start()

            @pl.when(jnp.logical_and(early_half(source(d), k), has[-1]))
            def _():
                to_last(k, d).start()

    def block_step(k):
        @pl.when(k + AHEAD < steps)
        def _():
            for d in range(1, n_cell):
                remote_in(k + AHEAD, d).start()

        local_in(k).wait()
        for d in range(1, n_cell):
            remote_in(k, d).wait_recv()
        piece = pl.ds(k * CHUNK, CHUNK)
        residual = work[piece].reshape(CHUNK * cells, features).astype(F32)
        projected = dot(normalize(residual).astype(BF16), w_qkv[...]).astype(BF16)
        attended = attend(projected, CHUNK, cells, features)

        @pl.when(k >= 1)
        def _():
            forward(k - 1)

        mid = (residual + dot(attended, w_out[...])).astype(BF16).astype(F32)
        hidden = jax.nn.gelu(dot(normalize(mid).astype(BF16), w_up[...])).astype(BF16)
        done = (mid + dot(hidden, w_down[...])).astype(BF16)
        stage[piece] = done.reshape(CHUNK, cells, features)
        for d in range(1, n_cell):
            own_copy(k, d).start()
        pad[pl.ds(width + x * per + k * CHUNK, CHUNK)] = stage[piece, my_cells]

    def gather(ref, k, shift):
        parts = [
            ref[pl.ds(j * per + k * CHUNK + shift, CHUNK)].reshape(CHUNK * cells_local, features)
            for j in range(n_cell)
        ]
        return jnp.concatenate(parts, axis=0)

    def first_step(k):
        for d in range(n_cell):
            @pl.when(jnp.logical_and(late_half(source(d), k), has[-1]))
            def _():
                from_halo(0, k, d).wait_recv()

            @pl.when(jnp.logical_and(early_half(source(d), k), has[1]))
            def _():
                from_halo(1, k, d).wait_recv()
        value = gated(gather(pad, k, width), gather(pad, k, 0), gather(pad, k, 2 * width), w_first)
        first[:, pl.ds(k * CHUNK, CHUNK)] = value.reshape(n_cell, CHUNK, cells_local, features)

        @pl.when(has[reach])
        def _():
            far_copy(0, k).start()

        @pl.when(has[-reach])
        def _():
            far_copy(1, k).start()

    extra = 1 if steps >= 6 else 0
    late = steps - 2 * extra

    @pl.loop(0, steps)
    def _(k):
        block_step(k)

        @pl.when(k == min(1, steps - 1))
        def _():
            weight_ready(4)

        @pl.when(jnp.where(k < late, lax.rem(k, 2), 1) == 1)
        def _():
            first_step(jnp.where(k == steps - 1, (steps - 2) // 2 + extra, k // 2))

    forward(steps - 1)

    @pl.loop(steps // 2 + extra, steps)
    def _(k):
        first_step(k)

    weight_ready(5)

    @pl.loop(0, steps)
    def _(k):
        @pl.when(has[-reach])
        def _():
            far_copy(0, k).wait_recv()

        @pl.when(has[reach])
        def _():
            far_copy(1, k).wait_recv()

        piece = pl.ds(k * CHUNK, CHUNK)
        flat = (n_cell * CHUNK * cells_local, features)
        value = gated(
            first[:, piece].reshape(flat),
            far[0, :, piece].reshape(flat),
            far[1, :, piece].reshape(flat),
            w_second,
        )
        result[:, piece] = value.reshape(n_cell, CHUNK, cells_local, features)
        out_copy(k).start()

    for i in range(6):
        for d in range(1, n_sub):
            remote_weight(i, d).wait_send()

    @pl.loop(0, steps)
    def _(k):
        for d in range(n_cell):
            if d:
                remote_in(k, d).wait_send()
                own_copy(k, d).wait_send()

            @pl.when(jnp.logical_and(late_half(source(d), k), has[1]))
            def _():
                to_next(k, d).wait_send()

            @pl.when(jnp.logical_and(early_half(source(d), k), has[-1]))
            def _():
                to_last(k, d).wait_send()

        @pl.when(has[reach])
        def _():
            far_copy(0, k).wait_send()

        @pl.when(has[-reach])
        def _():
            far_copy(1, k).wait_send()

        out_copy(k).wait()


def regroup_kernel(
    sizes,
    frames, h_qkv, h_out, h_up, h_down, h_first, h_second,
    out,
    w_qkv, w_out, w_up, w_down, w_first, w_second,
    work, sect, first, result,
    ws, wr, wl, in_s, in_r, in_l, halo_s, halo_r, out_s, out_r, out_l, met,
):
    n_tm, n_cell, n_sub = sizes
    n_blocks = n_tm * n_sub
    per, classes, cells_local, features = frames.shape
    segments, span, cells, _ = first.shape
    group = span // per
    reach = group * n_sub
    steps = segments * group
    tm, x, sub = lax.axis_index("tm"), lax.axis_index("cell"), lax.axis_index("sub")
    block = tm * n_sub + sub
    mine = tm * n_cell + x

    home, own = lax.rem(block, reach) // group, block // reach
    my_slot = (block // reach) * group + lax.rem(block, group)
    my_cells = pl.ds(pl.multiple_of(x * cells_local, 16), cells_local)

    def remote(src, dst, s, r, where):
        return pltpu.make_async_remote_copy(
            src_ref=src, dst_ref=dst, send_sem=s, recv_sem=r, device_id=where, device_id_type=MESH
        )

    halves = (h_qkv, h_out, h_up, h_down, h_first, h_second)
    wholes = (w_qkv, w_out, w_up, w_down, w_first, w_second)

    def rows_of(half):
        size = half.shape[0]
        return pl.ds(pl.multiple_of(sub * size, 16), size)

    def local_weight(i):
        return pltpu.make_async_copy(halves[i], wholes[i].at[rows_of(halves[i])], wl.at[i])

    def remote_weight(i, d):
        return remote(
            halves[i], wholes[i].at[rows_of(halves[i])], ws.at[i, d - 1], wr.at[i, d - 1],
            {"sub": lax.rem(sub + d, n_sub)},
        )

    def weight_ready(i):
        local_weight(i).wait()
        for d in range(1, n_sub):
            remote_weight(i, d).wait_recv()

    def cells_of(j):
        return pl.ds(pl.multiple_of(j * cells_local, 16), cells_local)

    near = classes // group // 2
    lanes = group // n_cell
    level, turn = block // group, lax.rem(mine, group)

    def shift(a, k, sign):
        high = lax.rem(a // n_cell + lanes + sign * (k // n_cell), lanes)
        return high * n_cell + lax.rem(a + n_cell + sign * (k % n_cell), n_cell)

    def in_chip(across, d, k):
        base = lax.rem(level // near * near + near * across, 2 * near)
        return (base + lax.rem(level + d, near)) * group + shift(shift(lax.rem(block, group), k, -1), home * n_cell, -1)

    def in_copy(across, d, k):
        to = in_chip(across, d, k)
        return remote(
            frames.at[:, to], work.at[my_slot, :, my_cells],
            in_s.at[across, d, k], in_r.at[my_slot, x],
            {"tm": to // n_cell, "cell": lax.rem(to, n_cell), "sub": home},
        )

    def in_away(across, d, k):
        return jnp.logical_not(jnp.logical_and(in_chip(across, d, k) == mine, home == sub))

    first_turn = shift(shift(lax.rem(block, group), turn, -1), home * n_cell, -1)
    my_turn = shift(turn, sub * n_cell, 1)

    def in_local():
        return pltpu.make_async_copy(
            frames.at[:, mine], work.at[my_slot, :, my_cells], in_l.at[0]
        )

    def in_ready(h, p):
        slot = h * group + p
        for j in range(n_cell):
            here = jnp.logical_and(h * reach + sub * group + p == block, x == j)

            @pl.when(here)
            def _():
                in_local().wait()

            @pl.when(jnp.logical_not(here))
            def _():
                remote(
                    frames.at[:, 0], work.at[slot, :, cells_of(j)],
                    in_s.at[0, 0, 0], in_r.at[slot, j], {"cell": x},
                ).wait_recv()

    def halo_copy(side, h):
        at = h * n_sub + sub + (1 if side == 0 else -1)
        start, end = (span, 0) if side == 0 else (1, span + 1)
        to = at // n_sub
        return remote(
            sect.at[h, start], sect.at[to, end],
            halo_s.at[side, h], halo_r.at[side, to], {"sub": lax.rem(at, n_sub)},
        )

    def has_halo(side, h):
        at = h * n_sub + sub
        return at >= 1 if side == 0 else at + 1 < segments * n_sub

    def sends_halo(side, h):
        return has_halo(1 - side, h)

    def halo_ready(side, h):
        @pl.when(has_halo(side, h))
        def _():
            remote(
                sect.at[h, 1], sect.at[h, 0 if side == 0 else span + 1],
                halo_s.at[side, h], halo_r.at[side, h], {"cell": x},
            ).wait_recv()

    def out_target(h, f, j):
        to = h * reach + sub * group + f // per
        return to, jnp.logical_and(to == block, x == j)

    def out_copy(h, f, j):
        to, _ = out_target(h, f, j)
        part = lax.rem(f, per)
        return remote(
            result.at[h, f, cells_of(j)], out.at[part, mine],
            out_s.at[h, f, j], out_r.at[part, mine],
            {"tm": to // n_sub, "cell": j, "sub": lax.rem(to, n_sub)},
        )

    def out_local(h, f, j):
        part = lax.rem(f, per)
        return pltpu.make_async_copy(
            result.at[h, f, cells_of(j)], out.at[part, mine], out_l.at[part]
        )

    for i in range(6):
        local_weight(i).start()

    @pl.when(home == sub)
    def _():
        in_local().start()

    column = 2 * near * n_sub
    rank, lane = (tm // lanes) * n_sub + sub, lax.rem(tm, lanes)
    beside = [{"tm": tm, "cell": lax.rem(x + e, n_cell), "sub": sub} for e in range(1, n_cell)]
    below = [{"tm": tm - lane + lax.rem(lane + e, lanes), "cell": x, "sub": sub} for e in range(1, lanes)]
    barrier = pltpu.get_barrier_semaphore()
    for e in range(1, column):
        to = lax.rem(rank + e, column)
        pl.semaphore_signal(
            barrier, inc=1, device_id_type=MESH,
            device_id={"tm": to // n_sub * lanes + lane, "cell": x, "sub": lax.rem(to, n_sub)},
        )
    for where in beside + below:
        pl.semaphore_signal(barrier, inc=1, device_id=where, device_id_type=MESH)
    pl.semaphore_wait(barrier, column - 1 + len(beside) + len(below))

    for across in (1, 0):
        for d in range(near):
            @pl.when(in_away(across, d, first_turn))
            def _():
                in_copy(across, d, first_turn).start()
    for d in range(1, n_sub):
        remote_weight(0, d).start()

    for i, (around, count) in enumerate(((beside, len(beside)), (below, len(below)))):
        for where in around:
            pl.semaphore_signal(met.at[i], inc=1, device_id=where, device_id_type=MESH)
        pl.semaphore_wait(met.at[i], count)

    for across, d, k in [(0, d, k) for d in range(near) for k in range(group)] + [
        (1, d, k) for k in range(group) for d in range(near)
    ]:
        @pl.when(k != first_turn)
        def _():
            in_copy(across, d, k).start()
    for i in range(1, 6):
        for d in range(1, n_sub):
            remote_weight(i, d).start()

    for h in range(segments):
        for side in range(2):
            @pl.when(jnp.logical_not(has_halo(side, h)))
            def _():
                sect[h, 0 if side == 0 else span + 1] = jnp.zeros((cells, features), BF16)

    for i in range(4):
        weight_ready(i)

    def block_step(h, p):
        in_ready(h, p)
        residual = work[h * group + p].reshape(per * cells, features).astype(F32)
        projected = dot(normalize(residual).astype(BF16), w_qkv[...]).astype(BF16)
        attended = attend(projected, per, cells, features)
        mid = (residual + dot(attended, w_out[...])).astype(BF16).astype(F32)
        hidden = jax.nn.gelu(dot(normalize(mid).astype(BF16), w_up[...])).astype(BF16)
        done = (mid + dot(hidden, w_down[...])).astype(BF16)
        sect[h, pl.ds(1 + p * per, per)] = done.reshape(per, cells, features)
        for side, edge in ((0, group - 1), (1, 0)):
            @pl.when(jnp.logical_and(p == edge, sends_halo(side, h)))
            def _():
                halo_copy(side, h).start()

    def flat(ref, h, picks):
        return jnp.concatenate([ref[h, f] for f in picks], axis=0)

    def temporal(p):
        picks = [lax.rem(p * per + 1 + q, span) for q in range(per)]

        @pl.loop(0, segments)
        def _(h):
            for side in range(2):
                @pl.when(p == group - 1)
                def _():
                    halo_ready(side, h)
            value = gated(
                flat(sect, h, [f + 1 for f in picks]),
                flat(sect, h, picks),
                flat(sect, h, [f + 2 for f in picks]),
                w_first,
            )
            for q, f in enumerate(picks):
                first[h, f] = value[q * cells : (q + 1) * cells]

        @pl.loop(0, segments)
        def _(k):
            h = lax.rem(own + 1 + k, segments)
            value = gated_pair(flat(first, h, picks), flat(first, 1 - h, picks), w_second, h == 1)
            for q, f in enumerate(picks):
                result[h, f] = value[q * cells : (q + 1) * cells]
            for f, e in [(f, e) for f in picks[::-1] for e in range(n_cell)]:
                j = lax.rem(x + 1 + e, n_cell)
                _, here = out_target(h, f, j)

                @pl.when(here)
                def _():
                    out_local(h, f, j).start()

                @pl.when(jnp.logical_not(here))
                def _():
                    out_copy(h, f, j).start()

    def position(p):
        return shift(lax.rem(p + group, group), my_turn, -1)

    @pl.loop(0, steps)
    def _(t):
        across = jnp.logical_or(t == group - 1, t > group)
        i = jnp.where(t < group - 1, t, jnp.where(t > group, t - group, jnp.where(across, 0, t - 1)))
        p = shift(my_turn, i, 1)
        block_step(jnp.where(across, 1 - own, own), p)

        @pl.when(t == 1)
        def _():
            weight_ready(4)
            weight_ready(5)

        @pl.when(t > group)
        def _():
            @pl.loop(0, 3)
            def _(m):
                q = jnp.where(m == 2, group - 1, p - 1 + m)
                both = jnp.logical_and(position(q) <= i, position(q + 1) <= i)
                inner = jnp.logical_and(q >= 0, q < group - 1)

                @pl.when(jnp.where(m == 2, i == group - 1, jnp.logical_and(both, inner)))
                def _():
                    temporal(q)

    for r in range(classes):
        for part in range(per):
            here = jnp.logical_and(mine == r, home == sub)

            @pl.when(here)
            def _():
                pltpu.make_async_copy(
                    result.at[0, 0, my_cells], out.at[part, r], out_l.at[part]
                ).wait()

            @pl.when(jnp.logical_not(here))
            def _():
                remote(
                    result.at[0, 0, my_cells], out.at[part, r],
                    out_s.at[0, 0, 0], out_r.at[part, r], {"cell": x},
                ).wait_recv()

    for i in range(6):
        for d in range(1, n_sub):
            remote_weight(i, d).wait_send()
    for across, d, k in [(a, d, k) for a in range(2) for d in range(near) for k in range(group)]:
        @pl.when(in_away(across, d, k))
        def _():
            in_copy(across, d, k).wait_send()
    for h in range(segments):
        for side in range(2):
            @pl.when(sends_halo(side, h))
            def _():
                halo_copy(side, h).wait_send()

        @pl.loop(0, span)
        def _(f):
            for j in range(n_cell):
                _, here = out_target(h, f, j)

                @pl.when(jnp.logical_not(here))
                def _():
                    out_copy(h, f, j).wait_send()


def regroup(sizes, frames, *halves):
    n_tm, n_cell, n_sub = sizes
    frames_local, cells_local, features = frames.shape
    classes = DILATION_FIRST
    per = frames_local // classes
    cells = n_cell * cells_local
    reach = DILATION_SECOND // frames_local
    group = reach // n_sub
    segments = n_tm * n_sub // reach
    span = group * per
    split = (per, classes, cells_local, features)
    dma = pltpu.SemaphoreType.DMA
    anywhere = pl.BlockSpec(memory_space=pl.ANY)
    call = pl.pallas_call(
        functools.partial(regroup_kernel, sizes),
        out_shape=pltpu.VMEM(split, BF16),
        in_specs=[anywhere] * 7,
        out_specs=anywhere,
        scratch_shapes=[pltpu.VMEM((n_sub * w.shape[0], w.shape[1]), BF16) for w in halves]
        + [
            pltpu.VMEM((segments * group, per, cells, features), BF16),
            pltpu.VMEM((segments, span + 2, cells, features), BF16),
            pltpu.VMEM((segments, span, cells, features), BF16),
            pltpu.VMEM((segments, span, cells, features), BF16),
            dma((6, n_sub - 1)), dma((6, n_sub - 1)), dma((6,)),
            dma((2, classes // group // 2, group)), dma((segments * group, n_cell)), dma((1,)),
            dma((2, segments)), dma((2, segments)),
            dma((segments, span, n_cell)), dma((per, classes)), dma((per,)),
            pltpu.SemaphoreType.REGULAR((2,)),
        ],
        compiler_params=pltpu.CompilerParams(
            collective_id=0, has_side_effects=True, vmem_limit_bytes=56 * 1024 * 1024
        ),
        name="video_regroup",
    )
    return call(frames.reshape(split), *halves).reshape(frames.shape)


def regroups(sizes, frames):
    n_tm, n_cell, n_sub = sizes
    frames_local = frames.shape[0]
    reach = DILATION_SECOND // frames_local
    return (
        n_tm * n_cell == DILATION_FIRST
        and n_sub >= 2
        and frames_local % DILATION_FIRST == 0
        and DILATION_SECOND % frames_local == 0
        and reach % n_sub == 0
        and reach // n_sub >= 2
        and n_tm * n_sub == 2 * reach
        and DILATION_FIRST % (2 * (reach // n_sub)) == 0
        and reach // n_sub % n_cell == 0
    )


def local(sizes, frames, *halves):
    if regroups(sizes, frames):
        return regroup(sizes, frames, *halves)
    _, n_cell, n_sub = sizes
    frames_local, cells_local, features = frames.shape
    per = frames_local // n_cell
    cells = n_cell * cells_local
    steps = per // CHUNK
    split = (n_cell, per, cells_local, features)
    dma = pltpu.SemaphoreType.DMA
    anywhere = pl.BlockSpec(memory_space=pl.ANY)
    call = pl.pallas_call(
        functools.partial(kernel, sizes),
        out_shape=jax.ShapeDtypeStruct(split, BF16),
        in_specs=[anywhere] * 7,
        out_specs=anywhere,
        scratch_shapes=[pltpu.VMEM((n_sub * w.shape[0], w.shape[1]), BF16) for w in halves]
        + [
            pltpu.VMEM((per, cells, features), BF16),
            pltpu.VMEM((per, cells, features), BF16),
            pltpu.VMEM((frames_local + 2 * DILATION_FIRST, cells_local, features), BF16),
            pltpu.VMEM(split, BF16),
            pltpu.VMEM((2,) + split, BF16),
            pltpu.VMEM(split, BF16),
            dma((6, n_sub - 1)), dma((6, n_sub - 1)), dma((6,)),
            dma((steps, n_cell - 1)), dma((steps, n_cell - 1)), dma((steps,)),
            dma((steps, n_cell - 1)), dma((steps, n_cell - 1)),
            dma((2, steps, n_cell)), dma((2, steps, n_cell)),
            dma((2, steps)), dma((2, steps)), dma((steps,)),
        ],
        compiler_params=pltpu.CompilerParams(
            collective_id=0, has_side_effects=True, vmem_limit_bytes=56 * 1024 * 1024
        ),
        name="video_block",
    )
    return call(frames, *halves).reshape(frames.shape)


def solution(mesh):
    sizes = (mesh.shape["tm"], mesh.shape["cell"], mesh.shape["sub"])
    placed = (P(("groups", "tm", "sub"), "cell", None),) + (P("sub", None),) * 6
    return jax.shard_map(
        functools.partial(local, sizes),
        mesh=mesh,
        in_specs=placed,
        out_specs=P(("groups", "tm", "sub"), "cell", None),
        check_vma=False,
    )
```

```python
import functools

import jax
import jax.numpy as jnp
from jax import lax
from jax.experimental import pallas as pl
from jax.experimental.pallas import tpu as pltpu
from jax.sharding import PartitionSpec as P

HEAD_DIM = 64
DILATION_FIRST = 16
DILATION_SECOND = 256
CHUNK = 2
AHEAD = 2
PAIR = 2 * HEAD_DIM
MESH = pl.DeviceIdType.MESH
F32 = jnp.float32
BF16 = jnp.bfloat16


def normalize(values):
    row_mean = jnp.mean(values, axis=-1, keepdims=True)
    centred = values - row_mean
    row_var = jnp.mean(centred * centred, axis=-1, keepdims=True)
    return centred * lax.rsqrt(row_var + 1e-05)


def dot(a, b):
    return jnp.dot(a, b, preferred_element_type=F32)


def attend(projected, frame_count, cells, features):
    lane = lax.broadcasted_iota(jnp.int32, (cells, PAIR), 1)
    scale = HEAD_DIM ** (-0.5)
    keep_a = jnp.where(lane < HEAD_DIM, scale, 0.0).astype(BF16)
    keep_b = jnp.where(lane < HEAD_DIM, 0.0, scale).astype(BF16)
    rows = []
    for f in range(frame_count):
        here = projected[f * cells : (f + 1) * cells]
        columns = []
        for p in range(features // PAIR):
            q = here[:, p * PAIR : (p + 1) * PAIR]
            k = here[:, features + p * PAIR : features + (p + 1) * PAIR]
            v = here[:, 2 * features + p * PAIR : 2 * features + (p + 1) * PAIR]
            stacked = jnp.concatenate([q * keep_a, q * keep_b], axis=0)
            scores = lax.dot_general(
                stacked, k, (((1,), (1,)), ((), ())), preferred_element_type=F32
            )
            exp_terms = jnp.exp(scores - jnp.max(scores, axis=-1, keepdims=True))
            probs = exp_terms * (1.0 / jnp.sum(exp_terms, axis=-1, keepdims=True))
            mixed = dot(probs.astype(BF16), v)
            columns.append(jnp.where(lane < HEAD_DIM, mixed[:cells], mixed[cells:]).astype(BF16))
        rows.append(jnp.concatenate(columns, axis=1))
    return jnp.concatenate(rows, axis=0)


def gated(center, earlier, later, weight_ref):
    features = center.shape[-1]
    preact = (
        dot(center, weight_ref[features : 2 * features])
        + dot(earlier, weight_ref[:features])
        + dot(later, weight_ref[2 * features :])
    )
    gate = 0.5 * jnp.tanh(0.5 * preact[:, features:]) + 0.5
    return (center.astype(F32) + jnp.tanh(preact[:, :features]) * gate).astype(BF16)


def gated_pair(center, other, weight_ref, earlier):
    features = center.shape[-1]
    other_rows = pl.ds(pl.multiple_of(jnp.where(earlier, 0, 2 * features), features), features)
    preact = dot(center, weight_ref[features : 2 * features]) + dot(other, weight_ref[other_rows])
    gate = 0.5 * jnp.tanh(0.5 * preact[:, features:]) + 0.5
    return (center.astype(F32) + jnp.tanh(preact[:, :features]) * gate).astype(BF16)


def kernel(
    sizes,
    frames, h_qkv, h_out, h_up, h_down, h_first, h_second,
    out,
    w_qkv, w_out, w_up, w_down, w_first, w_second,
    work, stage, pad, first, far, result,
    ws, wr, wl, in_s, in_r, in_l, own_s, own_r, halo_s, halo_r, far_s, far_r, out_s,
):
    n_tm, n_cell, n_sub = sizes
    n_blocks = n_tm * n_sub
    frames_local, cells_local, features = frames.shape
    per = frames_local // n_cell
    cells = n_cell * cells_local
    steps = per // CHUNK
    reach = DILATION_SECOND // frames_local
    width = DILATION_FIRST
    tm, x, sub = lax.axis_index("tm"), lax.axis_index("cell"), lax.axis_index("sub")
    block = tm * n_sub + sub

    def at(b, j):
        return {"tm": b // n_sub, "cell": j, "sub": lax.rem(b, n_sub)}

    def peer(d):
        return lax.rem(x + d, n_cell)

    def source(d):
        return lax.rem(x + n_cell - d, n_cell)

    def remote(src, dst, s, r, where):
        return pltpu.make_async_remote_copy(
            src_ref=src, dst_ref=dst, send_sem=s, recv_sem=r, device_id=where, device_id_type=MESH
        )

    has = {
        -1: block >= 1,
        1: block + 1 < n_blocks,
        -reach: block >= reach,
        reach: block + reach < n_blocks,
    }

    halves = (h_qkv, h_out, h_up, h_down, h_first, h_second)
    wholes = (w_qkv, w_out, w_up, w_down, w_first, w_second)

    def rows_of(half):
        size = half.shape[0]
        return pl.ds(pl.multiple_of(sub * size, 16), size)

    def local_weight(i):
        return pltpu.make_async_copy(halves[i], wholes[i].at[rows_of(halves[i])], wl.at[i])

    def remote_weight(i, d):
        return remote(
            halves[i], wholes[i].at[rows_of(halves[i])], ws.at[i, d - 1], wr.at[i, d - 1],
            {"sub": lax.rem(sub + d, n_sub)},
        )

    my_cells = pl.ds(pl.multiple_of(x * cells_local, 16), cells_local)

    def local_in(k):
        return pltpu.make_async_copy(
            frames.at[pl.ds(x * per + k * CHUNK, CHUNK)],
            work.at[pl.ds(k * CHUNK, CHUNK), my_cells],
            in_l.at[k],
        )

    def remote_in(k, d):
        return remote(
            frames.at[pl.ds(peer(d) * per + k * CHUNK, CHUNK)],
            work.at[pl.ds(k * CHUNK, CHUNK), my_cells],
            in_s.at[k, d - 1], in_r.at[k, d - 1], {"cell": peer(d)},
        )

    def staged(k, d):
        their_cells = pl.ds(pl.multiple_of(peer(d) * cells_local, 16), cells_local)
        return stage.at[pl.ds(k * CHUNK, CHUNK), their_cells]

    def own_copy(k, d):
        return remote(
            staged(k, d), pad.at[pl.ds(width + x * per + k * CHUNK, CHUNK)],
            own_s.at[k, d - 1], own_r.at[k, d - 1], {"cell": peer(d)},
        )

    def to_next(k, d):
        start = source(d) * per + k * CHUNK
        return remote(
            pad.at[pl.ds(width + start, CHUNK)],
            pad.at[pl.ds(start - (frames_local - width), CHUNK)],
            halo_s.at[0, k, d], halo_r.at[0, k, d], at(block + 1, x),
        )

    def to_last(k, d):
        start = width + source(d) * per + k * CHUNK
        return remote(
            pad.at[pl.ds(start, CHUNK)], pad.at[pl.ds(start + frames_local, CHUNK)],
            halo_s.at[1, k, d], halo_r.at[1, k, d], at(block - 1, x),
        )

    def from_halo(side, k, d):
        return remote(
            pad.at[pl.ds(width, CHUNK)], pad.at[pl.ds(0, CHUNK)],
            halo_s.at[side, k, d], halo_r.at[side, k, d], {"cell": x},
        )

    def late_half(j, k):
        return j * per + k * CHUNK >= frames_local - width

    def early_half(j, k):
        return j * per + k * CHUNK < width

    def far_copy(side, k):
        piece = pl.ds(k * CHUNK, CHUNK)
        by = reach if side == 0 else -reach
        return remote(
            first.at[:, piece], far.at[side, :, piece],
            far_s.at[side, k], far_r.at[side, k], at(block + by, x),
        )

    def out_copy(k):
        piece = pl.ds(k * CHUNK, CHUNK)
        return pltpu.make_async_copy(result.at[:, piece], out.at[:, piece], out_s.at[k])

    for i in range(6):
        local_weight(i).start()

    @pl.loop(0, steps)
    def _(k):
        local_in(k).start()

    barrier = pltpu.get_barrier_semaphore()
    for d in range(1, n_cell):
        pl.semaphore_signal(barrier, inc=1, device_id={"cell": peer(d)}, device_id_type=MESH)
    for by, cond in has.items():
        @pl.when(cond)
        def _():
            pl.semaphore_signal(
                barrier, inc=1, device_id=at(block + by, x), device_id_type=MESH
            )
    heard = n_cell - 1
    for cond in has.values():
        heard = heard + jnp.where(cond, 1, 0)
    pl.semaphore_wait(barrier, heard)

    for i in range(6):
        for d in range(1, n_sub):
            remote_weight(i, d).start()

    for k in range(min(AHEAD, steps)):
        for d in range(1, n_cell):
            remote_in(k, d).start()

    @pl.when(jnp.logical_not(has[-1]))
    def _():
        pad[:width] = jnp.zeros((width, cells_local, features), BF16)

    @pl.when(jnp.logical_not(has[1]))
    def _():
        pad[width + frames_local :] = jnp.zeros((width, cells_local, features), BF16)

    @pl.when(jnp.logical_not(has[-reach]))
    def _():
        far[0] = jnp.zeros(far.shape[1:], BF16)

    @pl.when(jnp.logical_not(has[reach]))
    def _():
        far[1] = jnp.zeros(far.shape[1:], BF16)

    def weight_ready(i):
        local_weight(i).wait()
        for d in range(1, n_sub):
            remote_weight(i, d).wait_recv()

    for i in range(4):
        weight_ready(i)

    def forward(k):
        for d in range(n_cell):
            if d:
                own_copy(k, d).wait_recv()

            @pl.when(jnp.logical_and(late_half(source(d), k), has[1]))
            def _():
                to_next(k, d).start()

            @pl.when(jnp.logical_and(early_half(source(d), k), has[-1]))
            def _():
                to_last(k, d).start()

    def block_step(k):
        @pl.when(k + AHEAD < steps)
        def _():
            for d in range(1, n_cell):
                remote_in(k + AHEAD, d).start()

        local_in(k).wait()
        for d in range(1, n_cell):
            remote_in(k, d).wait_recv()
        piece = pl.ds(k * CHUNK, CHUNK)
        residual = work[piece].reshape(CHUNK * cells, features).astype(F32)
        projected = dot(normalize(residual).astype(BF16), w_qkv[...]).astype(BF16)
        attended = attend(projected, CHUNK, cells, features)

        @pl.when(k >= 1)
        def _():
            forward(k - 1)

        mid = (residual + dot(attended, w_out[...])).astype(BF16).astype(F32)
        hidden = jax.nn.gelu(dot(normalize(mid).astype(BF16), w_up[...])).astype(BF16)
        done = (mid + dot(hidden, w_down[...])).astype(BF16)
        stage[piece] = done.reshape(CHUNK, cells, features)
        for d in range(1, n_cell):
            own_copy(k, d).start()
        pad[pl.ds(width + x * per + k * CHUNK, CHUNK)] = stage[piece, my_cells]

    def gather(ref, k, shift):
        parts = [
            ref[pl.ds(j * per + k * CHUNK + shift, CHUNK)].reshape(CHUNK * cells_local, features)
            for j in range(n_cell)
        ]
        return jnp.concatenate(parts, axis=0)

    def first_step(k):
        for d in range(n_cell):
            @pl.when(jnp.logical_and(late_half(source(d), k), has[-1]))
            def _():
                from_halo(0, k, d).wait_recv()

            @pl.when(jnp.logical_and(early_half(source(d), k), has[1]))
            def _():
                from_halo(1, k, d).wait_recv()
        value = gated(gather(pad, k, width), gather(pad, k, 0), gather(pad, k, 2 * width), w_first)
        first[:, pl.ds(k * CHUNK, CHUNK)] = value.reshape(n_cell, CHUNK, cells_local, features)

        @pl.when(has[reach])
        def _():
            far_copy(0, k).start()

        @pl.when(has[-reach])
        def _():
            far_copy(1, k).start()

    extra = 1 if steps >= 6 else 0
    late = steps - 2 * extra

    @pl.loop(0, steps)
    def _(k):
        block_step(k)

        @pl.when(k == min(1, steps - 1))
        def _():
            weight_ready(4)

        @pl.when(jnp.where(k < late, lax.rem(k, 2), 1) == 1)
        def _():
            first_step(jnp.where(k == steps - 1, (steps - 2) // 2 + extra, k // 2))

    forward(steps - 1)

    @pl.loop(steps // 2 + extra, steps)
    def _(k):
        first_step(k)

    weight_ready(5)

    @pl.loop(0, steps)
    def _(k):
        @pl.when(has[-reach])
        def _():
            far_copy(0, k).wait_recv()

        @pl.when(has[reach])
        def _():
            far_copy(1, k).wait_recv()

        piece = pl.ds(k * CHUNK, CHUNK)
        flat = (n_cell * CHUNK * cells_local, features)
        value = gated(
            first[:, piece].reshape(flat),
            far[0, :, piece].reshape(flat),
            far[1, :, piece].reshape(flat),
            w_second,
        )
        result[:, piece] = value.reshape(n_cell, CHUNK, cells_local, features)
        out_copy(k).start()

    for i in range(6):
        for d in range(1, n_sub):
            remote_weight(i, d).wait_send()

    @pl.loop(0, steps)
    def _(k):
        for d in range(n_cell):
            if d:
                remote_in(k, d).wait_send()
                own_copy(k, d).wait_send()

            @pl.when(jnp.logical_and(late_half(source(d), k), has[1]))
            def _():
                to_next(k, d).wait_send()

            @pl.when(jnp.logical_and(early_half(source(d), k), has[-1]))
            def _():
                to_last(k, d).wait_send()

        @pl.when(has[reach])
        def _():
            far_copy(0, k).wait_send()

        @pl.when(has[-reach])
        def _():
            far_copy(1, k).wait_send()

        out_copy(k).wait()


def regroup_kernel(
    sizes,
    frames, h_qkv, h_out, h_up, h_down, h_first, h_second,
    out,
    w_qkv, w_out, w_up, w_down, w_first, w_second,
    work, sect, first, result,
    ws, wr, in_s, in_r, halo_s, halo_r, out_s, out_r, met,
):
    n_tm, n_cell, n_sub = sizes
    n_blocks = n_tm * n_sub
    per, classes, cells_local, features = frames.shape
    segments, span, cells, _ = first.shape
    group = span // per
    reach = group * n_sub
    steps = segments * group
    tm, x, sub = lax.axis_index("tm"), lax.axis_index("cell"), lax.axis_index("sub")
    block = tm * n_sub + sub
    mine = tm * n_cell + x

    home, own = lax.div(lax.rem(block, reach), group), lax.div(block, reach)
    my_slot = own * group + lax.rem(block, group)
    my_cells = pl.ds(pl.multiple_of(x * cells_local, 16), cells_local)

    def remote(src, dst, s, r, where):
        return pltpu.make_async_remote_copy(
            src_ref=src, dst_ref=dst, send_sem=s, recv_sem=r, device_id=where, device_id_type=MESH
        )

    halves = (h_qkv, h_out, h_up, h_down, h_first, h_second)
    wholes = (w_qkv, w_out, w_up, w_down, w_first, w_second)

    def rows_of(half):
        size = half.shape[0]
        return pl.ds(pl.multiple_of(sub * size, 16), size)

    def local_weight(i):
        return pltpu.make_async_copy(halves[i], wholes[i].at[rows_of(halves[i])], wr.at[i])

    def remote_weight(i, d):
        return remote(
            halves[i], wholes[i].at[rows_of(halves[i])], ws.at[i], wr.at[i],
            {"sub": lax.rem(sub + d, n_sub)},
        )

    def weight_ready(i):
        pltpu.make_async_copy(wholes[i], wholes[i], wr.at[i]).wait()

    def cells_of(j):
        return pl.ds(pl.multiple_of(j * cells_local, 16), cells_local)

    near = classes // group // 2
    lanes = group // n_cell
    level, turn = lax.div(block, group), lax.rem(mine, group)

    def shift(a, k, sign):
        high = lax.rem(lax.div(a, n_cell) + lanes + sign * lax.div(k, n_cell), lanes)
        return high * n_cell + lax.rem(a + n_cell + sign * lax.rem(k, n_cell), n_cell)

    def in_chip(across, d, k):
        base = lax.rem(lax.div(level, near) * near + near * across, 2 * near)
        return (base + lax.rem(level + d, near)) * group + shift(shift(lax.rem(block, group), k, -1), home * n_cell, -1)

    def in_copy(across, d, k):
        to = in_chip(across, d, k)
        return remote(
            frames.at[:, to], work.at[my_slot, :, my_cells],
            in_s.at[0], in_r.at[my_slot],
            {"tm": lax.div(to, n_cell), "cell": lax.rem(to, n_cell), "sub": home},
        )

    def in_away(across, d, k):
        return jnp.logical_not(jnp.logical_and(in_chip(across, d, k) == mine, home == sub))

    first_turn = shift(shift(lax.rem(block, group), turn, -1), home * n_cell, -1)
    my_turn = shift(turn, sub * n_cell, 1)

    def in_local():
        return pltpu.make_async_copy(
            frames.at[:, mine], work.at[my_slot, :, my_cells], in_r.at[my_slot]
        )

    def in_ready(h, p):
        slot = h * group + p
        pltpu.make_async_copy(work.at[slot], work.at[slot], in_r.at[slot]).wait()

    def all_sent(sem):
        for away, part in ((False, frames.at[:, pl.ds(0, classes - 1)]), (True, frames)):
            @pl.when((home != sub) == away)
            def _():
                remote(part, part, sem, sem, {"cell": x}).wait_send()

    def halo_copy(side, h):
        at = h * n_sub + sub + (1 if side == 0 else -1)
        start, end = (span, 0) if side == 0 else (1, span + 1)
        to = lax.div(at, n_sub)
        return remote(
            sect.at[h, start], sect.at[to, end],
            halo_s.at[side, h], halo_r.at[side, to], {"sub": lax.rem(at, n_sub)},
        )

    def has_halo(side, h):
        at = h * n_sub + sub
        return at >= 1 if side == 0 else at + 1 < segments * n_sub

    def sends_halo(side, h):
        return has_halo(1 - side, h)

    def halo_ready(side, h):
        @pl.when(has_halo(side, h))
        def _():
            remote(
                sect.at[h, 1], sect.at[h, 0 if side == 0 else span + 1],
                halo_s.at[side, h], halo_r.at[side, h], {"cell": x},
            ).wait_recv()

    def out_target(h, f, j):
        to = h * reach + sub * group + lax.div(f, per)
        return to, jnp.logical_and(to == block, x == j)

    def out_copy(h, f, j):
        to, _ = out_target(h, f, j)
        return remote(
            result.at[h, f, cells_of(j)], out.at[lax.rem(f, per), mine], out_s.at[0], out_r.at[0],
            {"tm": lax.div(to, n_sub), "cell": j, "sub": lax.rem(to, n_sub)},
        )

    def out_local(h, f, j):
        return pltpu.make_async_copy(
            result.at[h, f, cells_of(j)], out.at[lax.rem(f, per), mine], out_r.at[0]
        )

    column = 2 * near * n_sub
    rank, lane = lax.div(tm, lanes) * n_sub + sub, lax.rem(tm, lanes)
    beside = [{"tm": tm, "cell": lax.rem(x + e, n_cell), "sub": sub} for e in range(1, n_cell)]
    below = [{"tm": tm - lane + lax.rem(lane + e, lanes), "cell": x, "sub": sub} for e in range(1, lanes)]
    barrier = pltpu.get_barrier_semaphore()
    for e in range(1, column):
        to = lax.rem(rank + e, column)
        pl.semaphore_signal(
            barrier, inc=1, device_id_type=MESH,
            device_id={"tm": lax.div(to, n_sub) * lanes + lane, "cell": x, "sub": lax.rem(to, n_sub)},
        )
    for where in beside + below:
        pl.semaphore_signal(barrier, inc=1, device_id=where, device_id_type=MESH)
    for i in range(6):
        local_weight(i).start()

    @pl.when(home == sub)
    def _():
        in_local().start()

    for h in range(segments):
        for side in range(2):
            @pl.when(jnp.logical_not(has_halo(side, h)))
            def _():
                sect[h, 0 if side == 0 else span + 1] = jnp.zeros((cells, features), BF16)

    pl.semaphore_wait(barrier, column - 1 + len(beside) + len(below))

    for across in (1, 0):
        for d in range(near):
            @pl.when(in_away(across, d, first_turn))
            def _():
                in_copy(across, d, first_turn).start()
    for d in range(1, n_sub):
        remote_weight(0, d).start()

    for i, (around, count) in enumerate(((beside, len(beside)), (below, len(below)))):
        for where in around:
            pl.semaphore_signal(met.at[i], inc=1, device_id=where, device_id_type=MESH)
        pl.semaphore_wait(met.at[i], count)

    for across, d, k in [(0, d, k) for d in range(near) for k in range(group)] + [
        (1, d, k) for k in range(group) for d in range(near)
    ]:
        @pl.when(k != first_turn)
        def _():
            in_copy(across, d, k).start()
    for i in range(1, 6):
        for d in range(1, n_sub):
            remote_weight(i, d).start()

    for i in range(4):
        weight_ready(i)

    def block_step(h, p):
        in_ready(h, p)
        residual = work[h * group + p].reshape(per * cells, features).astype(F32)
        projected = dot(normalize(residual).astype(BF16), w_qkv[...]).astype(BF16)
        attended = attend(projected, per, cells, features)
        mid = (residual + dot(attended, w_out[...])).astype(BF16).astype(F32)
        hidden = jax.nn.gelu(dot(normalize(mid).astype(BF16), w_up[...])).astype(BF16)
        done = (mid + dot(hidden, w_down[...])).astype(BF16)
        sect[h, pl.ds(1 + p * per, per)] = done.reshape(per, cells, features)
        for side, edge in ((0, group - 1), (1, 0)):
            @pl.when(jnp.logical_and(p == edge, sends_halo(side, h)))
            def _():
                halo_copy(side, h).start()

    def flat(ref, h, picks):
        return jnp.concatenate([ref[h, f] for f in picks], axis=0)

    def temporal(p):
        picks = [lax.rem(p * per + 1 + q, span) for q in range(per)]

        @pl.loop(0, segments)
        def _(h):
            for side in range(2):
                @pl.when(p == group - 1)
                def _():
                    halo_ready(side, h)
            value = gated(
                flat(sect, h, [f + 1 for f in picks]),
                flat(sect, h, picks),
                flat(sect, h, [f + 2 for f in picks]),
                w_first,
            )
            for q, f in enumerate(picks):
                first[h, f] = value[q * cells : (q + 1) * cells]

        @pl.loop(0, segments)
        def _(k):
            h = lax.rem(own + 1 + k, segments)
            value = gated_pair(flat(first, h, picks), flat(first, 1 - h, picks), w_second, h == 1)
            for q, f in enumerate(picks):
                result[h, f] = value[q * cells : (q + 1) * cells]
            for f, e in [(f, e) for f in picks[::-1] for e in range(n_cell)]:
                j = lax.rem(x + 1 + e, n_cell)
                _, here = out_target(h, f, j)

                @pl.when(here)
                def _():
                    out_local(h, f, j).start()

                @pl.when(jnp.logical_not(here))
                def _():
                    out_copy(h, f, j).start()

    def position(p):
        return shift(lax.rem(p + group, group), my_turn, -1)

    @pl.loop(0, steps)
    def _(t):
        across = jnp.logical_or(t == group - 1, t > group)
        i = jnp.where(t < group - 1, t, jnp.where(t > group, t - group, jnp.where(across, 0, t - 1)))
        p = shift(my_turn, i, 1)
        block_step(jnp.where(across, 1 - own, own), p)

        @pl.when(t == 1)
        def _():
            weight_ready(4)
            weight_ready(5)

        @pl.when(t > group)
        def _():
            @pl.loop(0, 3)
            def _(m):
                q = jnp.where(m == 2, group - 1, p - 1 + m)
                both = jnp.logical_and(position(q) <= i, position(q + 1) <= i)
                inner = jnp.logical_and(q >= 0, q < group - 1)

                @pl.when(jnp.where(m == 2, i == group - 1, jnp.logical_and(both, inner)))
                def _():
                    temporal(q)

    for i in range(6):
        for d in range(1, n_sub):
            remote_weight(i, d).wait_send()
    for h in range(segments):
        for side in range(2):
            @pl.when(sends_halo(side, h))
            def _():
                halo_copy(side, h).wait_send()

    all_sent(in_s.at[0])
    all_sent(out_s.at[0])
    pltpu.make_async_copy(out, out, out_r.at[0]).wait()


def regroup(sizes, frames, *halves):
    n_tm, n_cell, n_sub = sizes
    frames_local, cells_local, features = frames.shape
    classes = DILATION_FIRST
    per = frames_local // classes
    cells = n_cell * cells_local
    reach = DILATION_SECOND // frames_local
    group = reach // n_sub
    segments = n_tm * n_sub // reach
    span = group * per
    split = (per, classes, cells_local, features)
    dma = pltpu.SemaphoreType.DMA
    anywhere = pl.BlockSpec(memory_space=pl.ANY)
    call = pl.pallas_call(
        functools.partial(regroup_kernel, sizes),
        out_shape=pltpu.VMEM(split, BF16),
        in_specs=[anywhere] * 7,
        out_specs=anywhere,
        scratch_shapes=[pltpu.VMEM((n_sub * w.shape[0], w.shape[1]), BF16) for w in halves]
        + [
            pltpu.VMEM((segments * group, per, cells, features), BF16),
            pltpu.VMEM((segments, span + 2, cells, features), BF16),
            pltpu.VMEM((segments, span, cells, features), BF16),
            pltpu.VMEM((segments, span, cells, features), BF16),
            dma((6,)), dma((6,)), dma((1,)), dma((segments * group,)),
            dma((2, segments)), dma((2, segments)), dma((1,)), dma((1,)),
            pltpu.SemaphoreType.REGULAR((2,)),
        ],
        compiler_params=pltpu.CompilerParams(
            collective_id=0, has_side_effects=True, vmem_limit_bytes=56 * 1024 * 1024
        ),
        name="video_regroup",
    )
    return call(frames.reshape(split), *halves).reshape(frames.shape)


def regroups(sizes, frames):
    n_tm, n_cell, n_sub = sizes
    frames_local = frames.shape[0]
    reach = DILATION_SECOND // frames_local
    return (
        n_tm * n_cell == DILATION_FIRST
        and n_sub == 2
        and frames_local % DILATION_FIRST == 0
        and DILATION_SECOND % frames_local == 0
        and reach % n_sub == 0
        and reach // n_sub >= 2
        and n_tm * n_sub == 2 * reach
        and DILATION_FIRST % (2 * (reach // n_sub)) == 0
        and reach // n_sub % n_cell == 0
    )


def local(sizes, frames, *halves):
    if regroups(sizes, frames):
        return regroup(sizes, frames, *halves)
    _, n_cell, n_sub = sizes
    frames_local, cells_local, features = frames.shape
    per = frames_local // n_cell
    cells = n_cell * cells_local
    steps = per // CHUNK
    split = (n_cell, per, cells_local, features)
    dma = pltpu.SemaphoreType.DMA
    anywhere = pl.BlockSpec(memory_space=pl.ANY)
    call = pl.pallas_call(
        functools.partial(kernel, sizes),
        out_shape=jax.ShapeDtypeStruct(split, BF16),
        in_specs=[anywhere] * 7,
        out_specs=anywhere,
        scratch_shapes=[pltpu.VMEM((n_sub * w.shape[0], w.shape[1]), BF16) for w in halves]
        + [
            pltpu.VMEM((per, cells, features), BF16),
            pltpu.VMEM((per, cells, features), BF16),
            pltpu.VMEM((frames_local + 2 * DILATION_FIRST, cells_local, features), BF16),
            pltpu.VMEM(split, BF16),
            pltpu.VMEM((2,) + split, BF16),
            pltpu.VMEM(split, BF16),
            dma((6, n_sub - 1)), dma((6, n_sub - 1)), dma((6,)),
            dma((steps, n_cell - 1)), dma((steps, n_cell - 1)), dma((steps,)),
            dma((steps, n_cell - 1)), dma((steps, n_cell - 1)),
            dma((2, steps, n_cell)), dma((2, steps, n_cell)),
            dma((2, steps)), dma((2, steps)), dma((steps,)),
        ],
        compiler_params=pltpu.CompilerParams(
            collective_id=0, has_side_effects=True, vmem_limit_bytes=56 * 1024 * 1024
        ),
        name="video_block",
    )
    return call(frames, *halves).reshape(frames.shape)


def solution(mesh):
    sizes = (mesh.shape["tm"], mesh.shape["cell"], mesh.shape["sub"])
    placed = (P(("groups", "tm", "sub"), "cell", None),) + (P("sub", None),) * 6
    return jax.shard_map(
        functools.partial(local, sizes),
        mesh=mesh,
        in_specs=placed,
        out_specs=P(("groups", "tm", "sub"), "cell", None),
        check_vma=False,
    )
```

```python
import functools

import jax
import jax.numpy as jnp
from jax import lax
from jax.experimental import pallas as pl
from jax.experimental.pallas import tpu as pltpu
from jax.sharding import PartitionSpec as P

HEAD_DIM = 64
DILATION_FIRST = 16
DILATION_SECOND = 256
CHUNK = 2
AHEAD = 2
PAIR = 2 * HEAD_DIM
MESH = pl.DeviceIdType.MESH
F32 = jnp.float32
BF16 = jnp.bfloat16


def normalize(values):
    row_mean = jnp.mean(values, axis=-1, keepdims=True)
    centred = values - row_mean
    row_var = jnp.mean(centred * centred, axis=-1, keepdims=True)
    return centred * lax.rsqrt(row_var + 1e-05)


def dot(a, b):
    return jnp.dot(a, b, preferred_element_type=F32)


def attend(projected, frame_count, cells, features):
    lane = lax.broadcasted_iota(jnp.int32, (cells, PAIR), 1)
    scale = HEAD_DIM ** (-0.5)
    keep_a = jnp.where(lane < HEAD_DIM, scale, 0.0).astype(BF16)
    keep_b = jnp.where(lane < HEAD_DIM, 0.0, scale).astype(BF16)
    rows = []
    for f in range(frame_count):
        here = projected[f * cells : (f + 1) * cells]
        columns = []
        for p in range(features // PAIR):
            q = here[:, p * PAIR : (p + 1) * PAIR]
            k = here[:, features + p * PAIR : features + (p + 1) * PAIR]
            v = here[:, 2 * features + p * PAIR : 2 * features + (p + 1) * PAIR]
            stacked = jnp.concatenate([q * keep_a, q * keep_b], axis=0)
            scores = lax.dot_general(
                stacked, k, (((1,), (1,)), ((), ())), preferred_element_type=F32
            )
            exp_terms = jnp.exp(scores - jnp.max(scores, axis=-1, keepdims=True))
            probs = exp_terms * (1.0 / jnp.sum(exp_terms, axis=-1, keepdims=True))
            mixed = dot(probs.astype(BF16), v)
            columns.append(jnp.where(lane < HEAD_DIM, mixed[:cells], mixed[cells:]).astype(BF16))
        rows.append(jnp.concatenate(columns, axis=1))
    return jnp.concatenate(rows, axis=0)


def gated(center, earlier, later, weight_ref):
    features = center.shape[-1]
    preact = (
        dot(center, weight_ref[features : 2 * features])
        + dot(earlier, weight_ref[:features])
        + dot(later, weight_ref[2 * features :])
    )
    gate = 0.5 * jnp.tanh(0.5 * preact[:, features:]) + 0.5
    return (center.astype(F32) + jnp.tanh(preact[:, :features]) * gate).astype(BF16)


def gated_pair(center, other, weight_ref, earlier):
    features = center.shape[-1]
    other_rows = pl.ds(pl.multiple_of(jnp.where(earlier, 0, 2 * features), features), features)
    preact = dot(center, weight_ref[features : 2 * features]) + dot(other, weight_ref[other_rows])
    gate = 0.5 * jnp.tanh(0.5 * preact[:, features:]) + 0.5
    return (center.astype(F32) + jnp.tanh(preact[:, :features]) * gate).astype(BF16)


def kernel(
    sizes,
    frames, h_qkv, h_out, h_up, h_down, h_first, h_second,
    out,
    w_qkv, w_out, w_up, w_down, w_first, w_second,
    work, stage, pad, first, far, result,
    ws, wr, wl, in_s, in_r, in_l, own_s, own_r, halo_s, halo_r, far_s, far_r, out_s,
):
    n_tm, n_cell, n_sub = sizes
    n_blocks = n_tm * n_sub
    frames_local, cells_local, features = frames.shape
    per = frames_local // n_cell
    cells = n_cell * cells_local
    steps = per // CHUNK
    reach = DILATION_SECOND // frames_local
    width = DILATION_FIRST
    tm, x, sub = lax.axis_index("tm"), lax.axis_index("cell"), lax.axis_index("sub")
    block = tm * n_sub + sub

    def at(b, j):
        return {"tm": b // n_sub, "cell": j, "sub": lax.rem(b, n_sub)}

    def peer(d):
        return lax.rem(x + d, n_cell)

    def source(d):
        return lax.rem(x + n_cell - d, n_cell)

    def remote(src, dst, s, r, where):
        return pltpu.make_async_remote_copy(
            src_ref=src, dst_ref=dst, send_sem=s, recv_sem=r, device_id=where, device_id_type=MESH
        )

    has = {
        -1: block >= 1,
        1: block + 1 < n_blocks,
        -reach: block >= reach,
        reach: block + reach < n_blocks,
    }

    halves = (h_qkv, h_out, h_up, h_down, h_first, h_second)
    wholes = (w_qkv, w_out, w_up, w_down, w_first, w_second)

    def rows_of(half):
        size = half.shape[0]
        return pl.ds(pl.multiple_of(sub * size, 16), size)

    def local_weight(i):
        return pltpu.make_async_copy(halves[i], wholes[i].at[rows_of(halves[i])], wl.at[i])

    def remote_weight(i, d):
        return remote(
            halves[i], wholes[i].at[rows_of(halves[i])], ws.at[i, d - 1], wr.at[i, d - 1],
            {"sub": lax.rem(sub + d, n_sub)},
        )

    my_cells = pl.ds(pl.multiple_of(x * cells_local, 16), cells_local)

    def local_in(k):
        return pltpu.make_async_copy(
            frames.at[pl.ds(x * per + k * CHUNK, CHUNK)],
            work.at[pl.ds(k * CHUNK, CHUNK), my_cells],
            in_l.at[k],
        )

    def remote_in(k, d):
        return remote(
            frames.at[pl.ds(peer(d) * per + k * CHUNK, CHUNK)],
            work.at[pl.ds(k * CHUNK, CHUNK), my_cells],
            in_s.at[k, d - 1], in_r.at[k, d - 1], {"cell": peer(d)},
        )

    def staged(k, d):
        their_cells = pl.ds(pl.multiple_of(peer(d) * cells_local, 16), cells_local)
        return stage.at[pl.ds(k * CHUNK, CHUNK), their_cells]

    def own_copy(k, d):
        return remote(
            staged(k, d), pad.at[pl.ds(width + x * per + k * CHUNK, CHUNK)],
            own_s.at[k, d - 1], own_r.at[k, d - 1], {"cell": peer(d)},
        )

    def to_next(k, d):
        start = source(d) * per + k * CHUNK
        return remote(
            pad.at[pl.ds(width + start, CHUNK)],
            pad.at[pl.ds(start - (frames_local - width), CHUNK)],
            halo_s.at[0, k, d], halo_r.at[0, k, d], at(block + 1, x),
        )

    def to_last(k, d):
        start = width + source(d) * per + k * CHUNK
        return remote(
            pad.at[pl.ds(start, CHUNK)], pad.at[pl.ds(start + frames_local, CHUNK)],
            halo_s.at[1, k, d], halo_r.at[1, k, d], at(block - 1, x),
        )

    def from_halo(side, k, d):
        return remote(
            pad.at[pl.ds(width, CHUNK)], pad.at[pl.ds(0, CHUNK)],
            halo_s.at[side, k, d], halo_r.at[side, k, d], {"cell": x},
        )

    def late_half(j, k):
        return j * per + k * CHUNK >= frames_local - width

    def early_half(j, k):
        return j * per + k * CHUNK < width

    def far_copy(side, k):
        piece = pl.ds(k * CHUNK, CHUNK)
        by = reach if side == 0 else -reach
        return remote(
            first.at[:, piece], far.at[side, :, piece],
            far_s.at[side, k], far_r.at[side, k], at(block + by, x),
        )

    def out_copy(k):
        piece = pl.ds(k * CHUNK, CHUNK)
        return pltpu.make_async_copy(result.at[:, piece], out.at[:, piece], out_s.at[k])

    for i in range(6):
        local_weight(i).start()

    @pl.loop(0, steps)
    def _(k):
        local_in(k).start()

    barrier = pltpu.get_barrier_semaphore()
    for d in range(1, n_cell):
        pl.semaphore_signal(barrier, inc=1, device_id={"cell": peer(d)}, device_id_type=MESH)
    for by, cond in has.items():
        @pl.when(cond)
        def _():
            pl.semaphore_signal(
                barrier, inc=1, device_id=at(block + by, x), device_id_type=MESH
            )
    heard = n_cell - 1
    for cond in has.values():
        heard = heard + jnp.where(cond, 1, 0)
    pl.semaphore_wait(barrier, heard)

    for i in range(6):
        for d in range(1, n_sub):
            remote_weight(i, d).start()

    for k in range(min(AHEAD, steps)):
        for d in range(1, n_cell):
            remote_in(k, d).start()

    @pl.when(jnp.logical_not(has[-1]))
    def _():
        pad[:width] = jnp.zeros((width, cells_local, features), BF16)

    @pl.when(jnp.logical_not(has[1]))
    def _():
        pad[width + frames_local :] = jnp.zeros((width, cells_local, features), BF16)

    @pl.when(jnp.logical_not(has[-reach]))
    def _():
        far[0] = jnp.zeros(far.shape[1:], BF16)

    @pl.when(jnp.logical_not(has[reach]))
    def _():
        far[1] = jnp.zeros(far.shape[1:], BF16)

    def weight_ready(i):
        local_weight(i).wait()
        for d in range(1, n_sub):
            remote_weight(i, d).wait_recv()

    for i in range(4):
        weight_ready(i)

    def forward(k):
        for d in range(n_cell):
            if d:
                own_copy(k, d).wait_recv()

            @pl.when(jnp.logical_and(late_half(source(d), k), has[1]))
            def _():
                to_next(k, d).start()

            @pl.when(jnp.logical_and(early_half(source(d), k), has[-1]))
            def _():
                to_last(k, d).start()

    def block_step(k):
        @pl.when(k + AHEAD < steps)
        def _():
            for d in range(1, n_cell):
                remote_in(k + AHEAD, d).start()

        local_in(k).wait()
        for d in range(1, n_cell):
            remote_in(k, d).wait_recv()
        piece = pl.ds(k * CHUNK, CHUNK)
        residual = work[piece].reshape(CHUNK * cells, features).astype(F32)
        projected = dot(normalize(residual).astype(BF16), w_qkv[...]).astype(BF16)
        attended = attend(projected, CHUNK, cells, features)

        @pl.when(k >= 1)
        def _():
            forward(k - 1)

        mid = (residual + dot(attended, w_out[...])).astype(BF16).astype(F32)
        hidden = jax.nn.gelu(dot(normalize(mid).astype(BF16), w_up[...])).astype(BF16)
        done = (mid + dot(hidden, w_down[...])).astype(BF16)
        stage[piece] = done.reshape(CHUNK, cells, features)
        for d in range(1, n_cell):
            own_copy(k, d).start()
        pad[pl.ds(width + x * per + k * CHUNK, CHUNK)] = stage[piece, my_cells]

    def gather(ref, k, shift):
        parts = [
            ref[pl.ds(j * per + k * CHUNK + shift, CHUNK)].reshape(CHUNK * cells_local, features)
            for j in range(n_cell)
        ]
        return jnp.concatenate(parts, axis=0)

    def first_step(k):
        for d in range(n_cell):
            @pl.when(jnp.logical_and(late_half(source(d), k), has[-1]))
            def _():
                from_halo(0, k, d).wait_recv()

            @pl.when(jnp.logical_and(early_half(source(d), k), has[1]))
            def _():
                from_halo(1, k, d).wait_recv()
        value = gated(gather(pad, k, width), gather(pad, k, 0), gather(pad, k, 2 * width), w_first)
        first[:, pl.ds(k * CHUNK, CHUNK)] = value.reshape(n_cell, CHUNK, cells_local, features)

        @pl.when(has[reach])
        def _():
            far_copy(0, k).start()

        @pl.when(has[-reach])
        def _():
            far_copy(1, k).start()

    extra = 1 if steps >= 6 else 0
    late = steps - 2 * extra

    @pl.loop(0, steps)
    def _(k):
        block_step(k)

        @pl.when(k == min(1, steps - 1))
        def _():
            weight_ready(4)

        @pl.when(jnp.where(k < late, lax.rem(k, 2), 1) == 1)
        def _():
            first_step(jnp.where(k == steps - 1, (steps - 2) // 2 + extra, k // 2))

    forward(steps - 1)

    @pl.loop(steps // 2 + extra, steps)
    def _(k):
        first_step(k)

    weight_ready(5)

    @pl.loop(0, steps)
    def _(k):
        @pl.when(has[-reach])
        def _():
            far_copy(0, k).wait_recv()

        @pl.when(has[reach])
        def _():
            far_copy(1, k).wait_recv()

        piece = pl.ds(k * CHUNK, CHUNK)
        flat = (n_cell * CHUNK * cells_local, features)
        value = gated(
            first[:, piece].reshape(flat),
            far[0, :, piece].reshape(flat),
            far[1, :, piece].reshape(flat),
            w_second,
        )
        result[:, piece] = value.reshape(n_cell, CHUNK, cells_local, features)
        out_copy(k).start()

    for i in range(6):
        for d in range(1, n_sub):
            remote_weight(i, d).wait_send()

    @pl.loop(0, steps)
    def _(k):
        for d in range(n_cell):
            if d:
                remote_in(k, d).wait_send()
                own_copy(k, d).wait_send()

            @pl.when(jnp.logical_and(late_half(source(d), k), has[1]))
            def _():
                to_next(k, d).wait_send()

            @pl.when(jnp.logical_and(early_half(source(d), k), has[-1]))
            def _():
                to_last(k, d).wait_send()

        @pl.when(has[reach])
        def _():
            far_copy(0, k).wait_send()

        @pl.when(has[-reach])
        def _():
            far_copy(1, k).wait_send()

        out_copy(k).wait()


def regroup_kernel(
    sizes,
    frames, h_qkv, h_out, h_up, h_down, h_first, h_second,
    out,
    w_qkv, w_out, w_up, w_down, w_first, w_second,
    work, sect, first, result,
    ws, wr, in_s, in_r, halo_s, halo_r, out_s, out_r, met,
):
    n_tm, n_cell, n_sub = sizes
    n_blocks = n_tm * n_sub
    per, classes, cells_local, features = frames.shape
    segments, span, cells, _ = first.shape
    group = span // per
    reach = group * n_sub
    steps = segments * group
    tm, x, sub = lax.axis_index("tm"), lax.axis_index("cell"), lax.axis_index("sub")
    block = tm * n_sub + sub
    mine = tm * n_cell + x

    home, own = lax.div(lax.rem(block, reach), group), lax.div(block, reach)
    my_slot = own * group + lax.rem(block, group)
    my_cells = pl.ds(pl.multiple_of(x * cells_local, 16), cells_local)

    def remote(src, dst, s, r, where):
        return pltpu.make_async_remote_copy(
            src_ref=src, dst_ref=dst, send_sem=s, recv_sem=r, device_id=where, device_id_type=MESH
        )

    halves = (h_qkv, h_out, h_up, h_down, h_first, h_second)
    wholes = (w_qkv, w_out, w_up, w_down, w_first, w_second)

    def rows_of(half):
        size = half.shape[0]
        return pl.ds(pl.multiple_of(sub * size, 16), size)

    def local_weight(i):
        return pltpu.make_async_copy(halves[i], wholes[i].at[rows_of(halves[i])], wr.at[i])

    def remote_weight(i, d):
        return remote(
            halves[i], wholes[i].at[rows_of(halves[i])], ws.at[i], wr.at[i],
            {"sub": lax.rem(sub + d, n_sub)},
        )

    def weight_ready(i):
        pltpu.make_async_copy(wholes[i], wholes[i], wr.at[i]).wait()

    def cells_of(j):
        return pl.ds(pl.multiple_of(j * cells_local, 16), cells_local)

    near = classes // group // 2
    lanes = group // n_cell
    level, turn = lax.div(block, group), lax.rem(mine, group)

    def shift(a, k, sign):
        high = lax.rem(lax.div(a, n_cell) + lanes + sign * lax.div(k, n_cell), lanes)
        return high * n_cell + lax.rem(a + n_cell + sign * lax.rem(k, n_cell), n_cell)

    def in_copy(to):
        return remote(
            frames.at[:, to], work.at[my_slot, :, my_cells], in_s.at[0], in_r.at[my_slot],
            {"tm": lax.div(to, n_cell), "cell": lax.rem(to, n_cell), "sub": home},
        )

    def in_chip(across, d, k):
        base = lax.rem(lax.div(level, near) * near + near * across, 2 * near)
        to_turn = shift(shift(lax.rem(block, group), k, -1), home * n_cell, -1)
        return (base + lax.rem(level + d, near)) * group + to_turn

    first_turn = shift(shift(lax.rem(block, group), turn, -1), home * n_cell, -1)
    my_turn = shift(turn, sub * n_cell, 1)

    def in_local():
        return pltpu.make_async_copy(
            frames.at[:, mine], work.at[my_slot, :, my_cells], in_r.at[my_slot]
        )

    def in_ready(h, p):
        slot = h * group + p
        pltpu.make_async_copy(work.at[slot], work.at[slot], in_r.at[slot]).wait()

    def all_sent(sem):
        for away, part in ((False, frames.at[:, pl.ds(0, classes - 1)]), (True, frames)):
            @pl.when((home != sub) == away)
            def _():
                remote(part, part, sem, sem, {"cell": x}).wait_send()

    def halo_copy(side, h):
        at = h * n_sub + sub + (1 if side == 0 else -1)
        start, end = (span, 0) if side == 0 else (1, span + 1)
        to = lax.div(at, n_sub)
        return remote(
            sect.at[h, start], sect.at[to, end],
            halo_s.at[0], halo_r.at[side, to], {"sub": lax.rem(at, n_sub)},
        )

    def has_halo(side, h):
        at = h * n_sub + sub
        return at >= 1 if side == 0 else at + 1 < segments * n_sub

    def sends_halo(side, h):
        return has_halo(1 - side, h)

    def halo_ready(side, h):
        @pl.when(has_halo(side, h))
        def _():
            remote(
                sect.at[h, 1], sect.at[h, 0 if side == 0 else span + 1],
                halo_s.at[0], halo_r.at[side, h], {"cell": x},
            ).wait_recv()

    def out_target(h, f, j):
        to = h * reach + sub * group + lax.div(f, per)
        return to, jnp.logical_and(to == block, x == j)

    def out_copy(h, f, j):
        to, _ = out_target(h, f, j)
        return remote(
            result.at[h, f, cells_of(j)], out.at[lax.rem(f, per), mine], out_s.at[0], out_r.at[0],
            {"tm": lax.div(to, n_sub), "cell": j, "sub": lax.rem(to, n_sub)},
        )

    def out_local(h, f, j):
        return pltpu.make_async_copy(
            result.at[h, f, cells_of(j)], out.at[lax.rem(f, per), mine], out_r.at[0]
        )

    levels, lane = 2 * near, lax.rem(tm, lanes)
    over = [(step, level + step < levels if step > 0 else level + step >= 0) for step in (1, -1)]
    beside = [{"tm": tm, "cell": lax.rem(x + e, n_cell), "sub": sub} for e in range(1, n_cell)]
    below = [{"tm": tm - lane + lax.rem(lane + e, lanes), "cell": x, "sub": sub} for e in range(1, lanes)]
    inside = [{"tm": tm, "cell": x, "sub": lax.rem(sub + e, n_sub)} for e in range(1, n_sub)]
    barrier = pltpu.get_barrier_semaphore()
    neighbours = 0
    for step, there in over:
        neighbours = neighbours + jnp.where(there, 1, 0)

        @pl.when(there)
        def _():
            for core in range(n_sub):
                pl.semaphore_signal(
                    barrier, inc=1, device_id_type=MESH,
                    device_id={"tm": tm + step * lanes, "cell": x, "sub": core},
                )
    for where in beside + below + inside:
        pl.semaphore_signal(barrier, inc=1, device_id=where, device_id_type=MESH)

    for i in range(6):
        local_weight(i).start()

    @pl.when(home == sub)
    def _():
        in_local().start()

    for h in range(segments):
        for side in range(2):
            @pl.when(jnp.logical_not(has_halo(side, h)))
            def _():
                sect[h, 0 if side == 0 else span + 1] = jnp.zeros((cells, features), BF16)

    pl.semaphore_wait(barrier, n_sub * neighbours + len(beside + below + inside))

    def meet(i, around, count):
        for where, there in around:
            @pl.when(there)
            def _():
                pl.semaphore_signal(met.at[i], inc=1, device_id=where, device_id_type=MESH)
        return lambda: pl.semaphore_wait(met.at[i], count)

    def send_over(step):
        to = level + step
        inner = to < levels if step > 0 else to >= 0

        @pl.when(home != sub if step == 0 else inner)
        def _():
            in_copy(to * group + turn).start()

    column = [({"tm": tm + step * lanes, "cell": x, "sub": sub}, there) for step, there in over]
    for reached in range(1, levels):
        if reached < levels - 1:
            learned = meet(reached - 1, column, neighbours)
        else:
            learned = meet(reached - 1, [(where, True) for where in beside], len(beside))
        for step in (reached, -reached):
            send_over(step)
        if reached == 1:
            send_over(0)
            for d in range(1, n_sub):
                remote_weight(0, d).start()
        learned()
    meet(levels - 1, [(where, True) for where in below], len(below))()

    for across, d, k in [
        (1, d, k) for k in range(group) for d in range(near)
    ] + [(0, d, k) for d in range(near) for k in range(group)]:
        @pl.when(k != first_turn)
        def _():
            in_copy(in_chip(across, d, k)).start()
    for i in range(1, 6):
        for d in range(1, n_sub):
            remote_weight(i, d).start()

    for i in range(4):
        weight_ready(i)

    def block_step(h, p):
        in_ready(h, p)
        residual = work[h * group + p].reshape(per * cells, features).astype(F32)
        projected = dot(normalize(residual).astype(BF16), w_qkv[...]).astype(BF16)
        attended = attend(projected, per, cells, features)
        mid = (residual + dot(attended, w_out[...])).astype(BF16).astype(F32)
        hidden = jax.nn.gelu(dot(normalize(mid).astype(BF16), w_up[...])).astype(BF16)
        done = (mid + dot(hidden, w_down[...])).astype(BF16)
        sect[h, pl.ds(1 + p * per, per)] = done.reshape(per, cells, features)
        for side, edge in ((0, group - 1), (1, 0)):
            @pl.when(jnp.logical_and(p == edge, sends_halo(side, h)))
            def _():
                halo_copy(side, h).start()

    def flat(ref, h, picks):
        return jnp.concatenate([ref[h, f] for f in picks], axis=0)

    def temporal(p):
        picks = [lax.rem(p * per + 1 + q, span) for q in range(per)]

        @pl.loop(0, segments)
        def _(h):
            for side in range(2):
                @pl.when(p == group - 1)
                def _():
                    halo_ready(side, h)
            value = gated(
                flat(sect, h, [f + 1 for f in picks]),
                flat(sect, h, picks),
                flat(sect, h, [f + 2 for f in picks]),
                w_first,
            )
            for q, f in enumerate(picks):
                first[h, f] = value[q * cells : (q + 1) * cells]

        @pl.loop(0, segments)
        def _(k):
            h = lax.rem(own + 1 + k, segments)
            value = gated_pair(flat(first, h, picks), flat(first, 1 - h, picks), w_second, h == 1)
            for q, f in enumerate(picks):
                result[h, f] = value[q * cells : (q + 1) * cells]
            for f, e in [(f, e) for f in picks[::-1] for e in range(n_cell)]:
                j = lax.rem(x + 1 + e, n_cell)
                _, here = out_target(h, f, j)

                @pl.when(here)
                def _():
                    out_local(h, f, j).start()

                @pl.when(jnp.logical_not(here))
                def _():
                    out_copy(h, f, j).start()

    def position(p):
        return shift(lax.rem(p + group, group), my_turn, -1)

    @pl.loop(0, steps)
    def _(t):
        across = jnp.logical_or(t == group - 1, t > group)
        i = jnp.where(t < group - 1, t, jnp.where(t > group, t - group, jnp.where(across, 0, t - 1)))
        p = shift(my_turn, i, 1)
        block_step(jnp.where(across, 1 - own, own), p)

        @pl.when(t == 1)
        def _():
            weight_ready(4)
            weight_ready(5)

        @pl.when(t > group)
        def _():
            @pl.loop(0, 3)
            def _(m):
                q = jnp.where(m == 2, group - 1, p - 1 + m)
                both = jnp.logical_and(position(q) <= i, position(q + 1) <= i)
                inner = jnp.logical_and(q >= 0, q < group - 1)

                @pl.when(jnp.where(m == 2, i == group - 1, jnp.logical_and(both, inner)))
                def _():
                    temporal(q)

    for i in range(6):
        for d in range(1, n_sub):
            remote_weight(i, d).wait_send()
    edges = sect.at[0, pl.ds(0, 2 * segments - 1)]
    remote(edges, edges, halo_s.at[0], halo_s.at[0], {"cell": x}).wait_send()
    all_sent(in_s.at[0])
    all_sent(out_s.at[0])
    pltpu.make_async_copy(out, out, out_r.at[0]).wait()


def regroup(sizes, frames, *halves):
    n_tm, n_cell, n_sub = sizes
    frames_local, cells_local, features = frames.shape
    classes = DILATION_FIRST
    per = frames_local // classes
    cells = n_cell * cells_local
    reach = DILATION_SECOND // frames_local
    group = reach // n_sub
    segments = n_tm * n_sub // reach
    span = group * per
    split = (per, classes, cells_local, features)
    dma = pltpu.SemaphoreType.DMA
    anywhere = pl.BlockSpec(memory_space=pl.ANY)
    call = pl.pallas_call(
        functools.partial(regroup_kernel, sizes),
        out_shape=pltpu.VMEM(split, BF16),
        in_specs=[anywhere] * 7,
        out_specs=anywhere,
        scratch_shapes=[pltpu.VMEM((n_sub * w.shape[0], w.shape[1]), BF16) for w in halves]
        + [
            pltpu.VMEM((segments * group, per, cells, features), BF16),
            pltpu.VMEM((segments, span + 2, cells, features), BF16),
            pltpu.VMEM((segments, span, cells, features), BF16),
            pltpu.VMEM((segments, span, cells, features), BF16),
            dma((6,)), dma((6,)), dma((1,)), dma((segments * group,)),
            dma((1,)), dma((2, segments)), dma((1,)), dma((1,)),
            pltpu.SemaphoreType.REGULAR((n_tm * n_cell // group,)),
        ],
        compiler_params=pltpu.CompilerParams(
            collective_id=0, has_side_effects=True, vmem_limit_bytes=56 * 1024 * 1024
        ),
        name="video_regroup",
    )
    return call(frames.reshape(split), *halves).reshape(frames.shape)


def regroups(sizes, frames):
    n_tm, n_cell, n_sub = sizes
    frames_local = frames.shape[0]
    reach = DILATION_SECOND // frames_local
    return (
        n_tm * n_cell == DILATION_FIRST
        and n_sub == 2
        and frames_local % DILATION_FIRST == 0
        and DILATION_SECOND % frames_local == 0
        and reach % n_sub == 0
        and reach // n_sub >= 2
        and n_tm * n_sub == 2 * reach
        and DILATION_FIRST % (2 * (reach // n_sub)) == 0
        and reach // n_sub % n_cell == 0
    )


def local(sizes, frames, *halves):
    if regroups(sizes, frames):
        return regroup(sizes, frames, *halves)
    _, n_cell, n_sub = sizes
    frames_local, cells_local, features = frames.shape
    per = frames_local // n_cell
    cells = n_cell * cells_local
    steps = per // CHUNK
    split = (n_cell, per, cells_local, features)
    dma = pltpu.SemaphoreType.DMA
    anywhere = pl.BlockSpec(memory_space=pl.ANY)
    call = pl.pallas_call(
        functools.partial(kernel, sizes),
        out_shape=jax.ShapeDtypeStruct(split, BF16),
        in_specs=[anywhere] * 7,
        out_specs=anywhere,
        scratch_shapes=[pltpu.VMEM((n_sub * w.shape[0], w.shape[1]), BF16) for w in halves]
        + [
            pltpu.VMEM((per, cells, features), BF16),
            pltpu.VMEM((per, cells, features), BF16),
            pltpu.VMEM((frames_local + 2 * DILATION_FIRST, cells_local, features), BF16),
            pltpu.VMEM(split, BF16),
            pltpu.VMEM((2,) + split, BF16),
            pltpu.VMEM(split, BF16),
            dma((6, n_sub - 1)), dma((6, n_sub - 1)), dma((6,)),
            dma((steps, n_cell - 1)), dma((steps, n_cell - 1)), dma((steps,)),
            dma((steps, n_cell - 1)), dma((steps, n_cell - 1)),
            dma((2, steps, n_cell)), dma((2, steps, n_cell)),
            dma((2, steps)), dma((2, steps)), dma((steps,)),
        ],
        compiler_params=pltpu.CompilerParams(
            collective_id=0, has_side_effects=True, vmem_limit_bytes=56 * 1024 * 1024
        ),
        name="video_block",
    )
    return call(frames, *halves).reshape(frames.shape)


def solution(mesh):
    sizes = (mesh.shape["tm"], mesh.shape["cell"], mesh.shape["sub"])
    placed = (P(("groups", "tm", "sub"), "cell", None),) + (P("sub", None),) * 6
    return jax.shard_map(
        functools.partial(local, sizes),
        mesh=mesh,
        in_specs=placed,
        out_specs=P(("groups", "tm", "sub"), "cell", None),
        check_vma=False,
    )
```

```python
import functools

import jax
import jax.numpy as jnp
from jax import lax
from jax.experimental import pallas as pl
from jax.experimental.pallas import tpu as pltpu
from jax.sharding import PartitionSpec as P

HEAD_DIM = 64
DILATION_FIRST = 16
DILATION_SECOND = 256
CHUNK = 2
AHEAD = 2
PAIR = 2 * HEAD_DIM
MESH = pl.DeviceIdType.MESH
F32 = jnp.float32
BF16 = jnp.bfloat16


def normalize(values):
    row_mean = jnp.mean(values, axis=-1, keepdims=True)
    centred = values - row_mean
    row_var = jnp.mean(centred * centred, axis=-1, keepdims=True)
    return centred * lax.rsqrt(row_var + 1e-05)


def dot(a, b):
    return jnp.dot(a, b, preferred_element_type=F32)


def attend(projected, frame_count, cells, features):
    lane = lax.broadcasted_iota(jnp.int32, (cells, PAIR), 1)
    scale = HEAD_DIM ** (-0.5)
    keep_a = jnp.where(lane < HEAD_DIM, scale, 0.0).astype(BF16)
    keep_b = jnp.where(lane < HEAD_DIM, 0.0, scale).astype(BF16)
    rows = []
    for f in range(frame_count):
        here = projected[f * cells : (f + 1) * cells]
        columns = []
        for p in range(features // PAIR):
            q = here[:, p * PAIR : (p + 1) * PAIR]
            k = here[:, features + p * PAIR : features + (p + 1) * PAIR]
            v = here[:, 2 * features + p * PAIR : 2 * features + (p + 1) * PAIR]
            stacked = jnp.concatenate([q * keep_a, q * keep_b], axis=0)
            scores = lax.dot_general(
                stacked, k, (((1,), (1,)), ((), ())), preferred_element_type=F32
            )
            exp_terms = jnp.exp(scores - jnp.max(scores, axis=-1, keepdims=True))
            probs = exp_terms * (1.0 / jnp.sum(exp_terms, axis=-1, keepdims=True))
            mixed = dot(probs.astype(BF16), v)
            columns.append(jnp.where(lane < HEAD_DIM, mixed[:cells], mixed[cells:]).astype(BF16))
        rows.append(jnp.concatenate(columns, axis=1))
    return jnp.concatenate(rows, axis=0)


def gated(center, earlier, later, weight_ref):
    features = center.shape[-1]
    preact = (
        dot(center, weight_ref[features : 2 * features])
        + dot(earlier, weight_ref[:features])
        + dot(later, weight_ref[2 * features :])
    )
    gate = 0.5 * jnp.tanh(0.5 * preact[:, features:]) + 0.5
    return (center.astype(F32) + jnp.tanh(preact[:, :features]) * gate).astype(BF16)


def gated_pair(center, other, weight_ref, earlier):
    features = center.shape[-1]
    other_rows = pl.ds(pl.multiple_of(jnp.where(earlier, 0, 2 * features), features), features)
    preact = dot(center, weight_ref[features : 2 * features]) + dot(other, weight_ref[other_rows])
    gate = 0.5 * jnp.tanh(0.5 * preact[:, features:]) + 0.5
    return (center.astype(F32) + jnp.tanh(preact[:, :features]) * gate).astype(BF16)


def kernel(
    sizes,
    frames, h_qkv, h_out, h_up, h_down, h_first, h_second,
    out,
    w_qkv, w_out, w_up, w_down, w_first, w_second,
    work, stage, pad, first, far, result,
    ws, wr, wl, in_s, in_r, in_l, own_s, own_r, halo_s, halo_r, far_s, far_r, out_s,
):
    n_tm, n_cell, n_sub = sizes
    n_blocks = n_tm * n_sub
    frames_local, cells_local, features = frames.shape
    per = frames_local // n_cell
    cells = n_cell * cells_local
    steps = per // CHUNK
    reach = DILATION_SECOND // frames_local
    width = DILATION_FIRST
    tm, x, sub = lax.axis_index("tm"), lax.axis_index("cell"), lax.axis_index("sub")
    block = tm * n_sub + sub

    def at(b, j):
        return {"tm": b // n_sub, "cell": j, "sub": lax.rem(b, n_sub)}

    def peer(d):
        return lax.rem(x + d, n_cell)

    def source(d):
        return lax.rem(x + n_cell - d, n_cell)

    def remote(src, dst, s, r, where):
        return pltpu.make_async_remote_copy(
            src_ref=src, dst_ref=dst, send_sem=s, recv_sem=r, device_id=where, device_id_type=MESH
        )

    has = {
        -1: block >= 1,
        1: block + 1 < n_blocks,
        -reach: block >= reach,
        reach: block + reach < n_blocks,
    }

    halves = (h_qkv, h_out, h_up, h_down, h_first, h_second)
    wholes = (w_qkv, w_out, w_up, w_down, w_first, w_second)

    def rows_of(half):
        size = half.shape[0]
        return pl.ds(pl.multiple_of(sub * size, 16), size)

    def local_weight(i):
        return pltpu.make_async_copy(halves[i], wholes[i].at[rows_of(halves[i])], wl.at[i])

    def remote_weight(i, d):
        return remote(
            halves[i], wholes[i].at[rows_of(halves[i])], ws.at[i, d - 1], wr.at[i, d - 1],
            {"sub": lax.rem(sub + d, n_sub)},
        )

    my_cells = pl.ds(pl.multiple_of(x * cells_local, 16), cells_local)

    def local_in(k):
        return pltpu.make_async_copy(
            frames.at[pl.ds(x * per + k * CHUNK, CHUNK)],
            work.at[pl.ds(k * CHUNK, CHUNK), my_cells],
            in_l.at[k],
        )

    def remote_in(k, d):
        return remote(
            frames.at[pl.ds(peer(d) * per + k * CHUNK, CHUNK)],
            work.at[pl.ds(k * CHUNK, CHUNK), my_cells],
            in_s.at[k, d - 1], in_r.at[k, d - 1], {"cell": peer(d)},
        )

    def staged(k, d):
        their_cells = pl.ds(pl.multiple_of(peer(d) * cells_local, 16), cells_local)
        return stage.at[pl.ds(k * CHUNK, CHUNK), their_cells]

    def own_copy(k, d):
        return remote(
            staged(k, d), pad.at[pl.ds(width + x * per + k * CHUNK, CHUNK)],
            own_s.at[k, d - 1], own_r.at[k, d - 1], {"cell": peer(d)},
        )

    def to_next(k, d):
        start = source(d) * per + k * CHUNK
        return remote(
            pad.at[pl.ds(width + start, CHUNK)],
            pad.at[pl.ds(start - (frames_local - width), CHUNK)],
            halo_s.at[0, k, d], halo_r.at[0, k, d], at(block + 1, x),
        )

    def to_last(k, d):
        start = width + source(d) * per + k * CHUNK
        return remote(
            pad.at[pl.ds(start, CHUNK)], pad.at[pl.ds(start + frames_local, CHUNK)],
            halo_s.at[1, k, d], halo_r.at[1, k, d], at(block - 1, x),
        )

    def from_halo(side, k, d):
        return remote(
            pad.at[pl.ds(width, CHUNK)], pad.at[pl.ds(0, CHUNK)],
            halo_s.at[side, k, d], halo_r.at[side, k, d], {"cell": x},
        )

    def late_half(j, k):
        return j * per + k * CHUNK >= frames_local - width

    def early_half(j, k):
        return j * per + k * CHUNK < width

    def far_copy(side, k):
        piece = pl.ds(k * CHUNK, CHUNK)
        by = reach if side == 0 else -reach
        return remote(
            first.at[:, piece], far.at[side, :, piece],
            far_s.at[side, k], far_r.at[side, k], at(block + by, x),
        )

    def out_copy(k):
        piece = pl.ds(k * CHUNK, CHUNK)
        return pltpu.make_async_copy(result.at[:, piece], out.at[:, piece], out_s.at[k])

    for i in range(6):
        local_weight(i).start()

    @pl.loop(0, steps)
    def _(k):
        local_in(k).start()

    barrier = pltpu.get_barrier_semaphore()
    for d in range(1, n_cell):
        pl.semaphore_signal(barrier, inc=1, device_id={"cell": peer(d)}, device_id_type=MESH)
    for by, cond in has.items():
        @pl.when(cond)
        def _():
            pl.semaphore_signal(
                barrier, inc=1, device_id=at(block + by, x), device_id_type=MESH
            )
    heard = n_cell - 1
    for cond in has.values():
        heard = heard + jnp.where(cond, 1, 0)
    pl.semaphore_wait(barrier, heard)

    for i in range(6):
        for d in range(1, n_sub):
            remote_weight(i, d).start()

    for k in range(min(AHEAD, steps)):
        for d in range(1, n_cell):
            remote_in(k, d).start()

    @pl.when(jnp.logical_not(has[-1]))
    def _():
        pad[:width] = jnp.zeros((width, cells_local, features), BF16)

    @pl.when(jnp.logical_not(has[1]))
    def _():
        pad[width + frames_local :] = jnp.zeros((width, cells_local, features), BF16)

    @pl.when(jnp.logical_not(has[-reach]))
    def _():
        far[0] = jnp.zeros(far.shape[1:], BF16)

    @pl.when(jnp.logical_not(has[reach]))
    def _():
        far[1] = jnp.zeros(far.shape[1:], BF16)

    def weight_ready(i):
        local_weight(i).wait()
        for d in range(1, n_sub):
            remote_weight(i, d).wait_recv()

    for i in range(4):
        weight_ready(i)

    def forward(k):
        for d in range(n_cell):
            if d:
                own_copy(k, d).wait_recv()

            @pl.when(jnp.logical_and(late_half(source(d), k), has[1]))
            def _():
                to_next(k, d).start()

            @pl.when(jnp.logical_and(early_half(source(d), k), has[-1]))
            def _():
                to_last(k, d).start()

    def block_step(k):
        @pl.when(k + AHEAD < steps)
        def _():
            for d in range(1, n_cell):
                remote_in(k + AHEAD, d).start()

        local_in(k).wait()
        for d in range(1, n_cell):
            remote_in(k, d).wait_recv()
        piece = pl.ds(k * CHUNK, CHUNK)
        residual = work[piece].reshape(CHUNK * cells, features).astype(F32)
        projected = dot(normalize(residual).astype(BF16), w_qkv[...]).astype(BF16)
        attended = attend(projected, CHUNK, cells, features)

        @pl.when(k >= 1)
        def _():
            forward(k - 1)

        mid = (residual + dot(attended, w_out[...])).astype(BF16).astype(F32)
        hidden = jax.nn.gelu(dot(normalize(mid).astype(BF16), w_up[...])).astype(BF16)
        done = (mid + dot(hidden, w_down[...])).astype(BF16)
        stage[piece] = done.reshape(CHUNK, cells, features)
        for d in range(1, n_cell):
            own_copy(k, d).start()
        pad[pl.ds(width + x * per + k * CHUNK, CHUNK)] = stage[piece, my_cells]

    def gather(ref, k, shift):
        parts = [
            ref[pl.ds(j * per + k * CHUNK + shift, CHUNK)].reshape(CHUNK * cells_local, features)
            for j in range(n_cell)
        ]
        return jnp.concatenate(parts, axis=0)

    def first_step(k):
        for d in range(n_cell):
            @pl.when(jnp.logical_and(late_half(source(d), k), has[-1]))
            def _():
                from_halo(0, k, d).wait_recv()

            @pl.when(jnp.logical_and(early_half(source(d), k), has[1]))
            def _():
                from_halo(1, k, d).wait_recv()
        value = gated(gather(pad, k, width), gather(pad, k, 0), gather(pad, k, 2 * width), w_first)
        first[:, pl.ds(k * CHUNK, CHUNK)] = value.reshape(n_cell, CHUNK, cells_local, features)

        @pl.when(has[reach])
        def _():
            far_copy(0, k).start()

        @pl.when(has[-reach])
        def _():
            far_copy(1, k).start()

    extra = 1 if steps >= 6 else 0
    late = steps - 2 * extra

    @pl.loop(0, steps)
    def _(k):
        block_step(k)

        @pl.when(k == min(1, steps - 1))
        def _():
            weight_ready(4)

        @pl.when(jnp.where(k < late, lax.rem(k, 2), 1) == 1)
        def _():
            first_step(jnp.where(k == steps - 1, (steps - 2) // 2 + extra, k // 2))

    forward(steps - 1)

    @pl.loop(steps // 2 + extra, steps)
    def _(k):
        first_step(k)

    weight_ready(5)

    @pl.loop(0, steps)
    def _(k):
        @pl.when(has[-reach])
        def _():
            far_copy(0, k).wait_recv()

        @pl.when(has[reach])
        def _():
            far_copy(1, k).wait_recv()

        piece = pl.ds(k * CHUNK, CHUNK)
        flat = (n_cell * CHUNK * cells_local, features)
        value = gated(
            first[:, piece].reshape(flat),
            far[0, :, piece].reshape(flat),
            far[1, :, piece].reshape(flat),
            w_second,
        )
        result[:, piece] = value.reshape(n_cell, CHUNK, cells_local, features)
        out_copy(k).start()

    for i in range(6):
        for d in range(1, n_sub):
            remote_weight(i, d).wait_send()

    @pl.loop(0, steps)
    def _(k):
        for d in range(n_cell):
            if d:
                remote_in(k, d).wait_send()
                own_copy(k, d).wait_send()

            @pl.when(jnp.logical_and(late_half(source(d), k), has[1]))
            def _():
                to_next(k, d).wait_send()

            @pl.when(jnp.logical_and(early_half(source(d), k), has[-1]))
            def _():
                to_last(k, d).wait_send()

        @pl.when(has[reach])
        def _():
            far_copy(0, k).wait_send()

        @pl.when(has[-reach])
        def _():
            far_copy(1, k).wait_send()

        out_copy(k).wait()


def regroup_kernel(
    sizes,
    frames, h_qkv, h_out, h_up, h_down, h_first, h_second,
    out,
    w_qkv, w_out, w_up, w_down, w_first, w_second,
    work, sect, first, result,
    ws, wr, in_s, in_r, halo_s, halo_r, out_s, out_r, met,
):
    n_tm, n_cell, n_sub = sizes
    n_blocks = n_tm * n_sub
    per, classes, cells_local, features = frames.shape
    segments, span, cells, _ = first.shape
    group = span // per
    reach = group * n_sub
    steps = segments * group
    tm, x, sub = lax.axis_index("tm"), lax.axis_index("cell"), lax.axis_index("sub")
    block = tm * n_sub + sub
    mine = tm * n_cell + x

    home, own = lax.div(lax.rem(block, reach), group), lax.div(block, reach)
    my_slot = own * group + lax.rem(block, group)
    my_cells = pl.ds(pl.multiple_of(x * cells_local, 16), cells_local)

    def remote(src, dst, s, r, where):
        return pltpu.make_async_remote_copy(
            src_ref=src, dst_ref=dst, send_sem=s, recv_sem=r, device_id=where, device_id_type=MESH
        )

    halves = (h_qkv, h_out, h_up, h_down, h_first, h_second)
    wholes = (w_qkv, w_out, w_up, w_down, w_first, w_second)

    def rows_of(half):
        size = half.shape[0]
        return pl.ds(pl.multiple_of(sub * size, 16), size)

    def local_weight(i):
        return pltpu.make_async_copy(halves[i], wholes[i].at[rows_of(halves[i])], wr.at[i])

    def remote_weight(i, d):
        return remote(
            halves[i], wholes[i].at[rows_of(halves[i])], ws.at[i // 4], wr.at[i],
            {"sub": lax.rem(sub + d, n_sub)},
        )

    def weight_ready(i):
        pltpu.make_async_copy(wholes[i], wholes[i], wr.at[i]).wait()

    def cells_of(j):
        return pl.ds(pl.multiple_of(j * cells_local, 16), cells_local)

    near = classes // group // 2
    lanes = group // n_cell
    level, turn = lax.div(block, group), lax.rem(mine, group)

    def shift(a, k, sign):
        high = lax.rem(lax.div(a, n_cell) + lanes + sign * lax.div(k, n_cell), lanes)
        return high * n_cell + lax.rem(a + n_cell + sign * lax.rem(k, n_cell), n_cell)

    def in_chip(across, d, k):
        base = lax.rem(lax.div(level, near) * near + near * across, 2 * near)
        return (base + lax.rem(level + d, near)) * group + shift(shift(lax.rem(block, group), k, -1), home * n_cell, -1)

    def in_copy(across, d, k):
        to = in_chip(across, d, k)
        return remote(
            frames.at[:, to], work.at[my_slot, :, my_cells],
            in_s.at[0], in_r.at[my_slot],
            {"tm": lax.div(to, n_cell), "cell": lax.rem(to, n_cell), "sub": home},
        )

    def in_away(across, d, k):
        return jnp.logical_not(jnp.logical_and(in_chip(across, d, k) == mine, home == sub))

    first_turn = shift(shift(lax.rem(block, group), turn, -1), home * n_cell, -1)
    my_turn = shift(turn, sub * n_cell, 1)

    def in_local():
        return pltpu.make_async_copy(
            frames.at[:, mine], work.at[my_slot, :, my_cells], in_r.at[my_slot]
        )

    def in_ready(h, p):
        slot = h * group + p
        pltpu.make_async_copy(work.at[slot], work.at[slot], in_r.at[slot]).wait()

    def all_sent(sem):
        for away, part in ((False, frames.at[:, pl.ds(0, classes - 1)]), (True, frames)):
            @pl.when((home != sub) == away)
            def _():
                remote(part, part, sem, sem, {"cell": x}).wait_send()

    def halo_copy(side, h):
        at = h * n_sub + sub + (1 if side == 0 else -1)
        start, end = (span, 0) if side == 0 else (1, span + 1)
        to = lax.div(at, n_sub)
        return remote(
            sect.at[h, start], sect.at[to, end],
            halo_s.at[0], halo_r.at[side, to], {"sub": lax.rem(at, n_sub)},
        )

    def has_halo(side, h):
        at = h * n_sub + sub
        return at >= 1 if side == 0 else at + 1 < segments * n_sub

    def sends_halo(side, h):
        return has_halo(1 - side, h)

    def halo_ready(side, h):
        @pl.when(has_halo(side, h))
        def _():
            remote(
                sect.at[h, 1], sect.at[h, 0 if side == 0 else span + 1],
                halo_s.at[0], halo_r.at[side, h], {"cell": x},
            ).wait_recv()

    def out_target(h, f, j):
        to = h * reach + sub * group + lax.div(f, per)
        return to, jnp.logical_and(to == block, x == j)

    def out_copy(h, f, j):
        to, _ = out_target(h, f, j)
        return remote(
            result.at[h, f, cells_of(j)], out.at[lax.rem(f, per), mine], out_s.at[0], out_r.at[0],
            {"tm": lax.div(to, n_sub), "cell": j, "sub": lax.rem(to, n_sub)},
        )

    def out_local(h, f, j):
        return pltpu.make_async_copy(
            result.at[h, f, cells_of(j)], out.at[lax.rem(f, per), mine], out_r.at[0]
        )

    column = 2 * near * n_sub
    rank, lane = lax.div(tm, lanes) * n_sub + sub, lax.rem(tm, lanes)
    beside = [{"tm": tm, "cell": lax.rem(x + e, n_cell), "sub": sub} for e in range(1, n_cell)]
    below = [{"tm": tm - lane + lax.rem(lane + e, lanes), "cell": x, "sub": sub} for e in range(1, lanes)]
    barrier = pltpu.get_barrier_semaphore()
    for e in range(1, column):
        to = lax.rem(rank + e, column)
        pl.semaphore_signal(
            barrier, inc=1, device_id_type=MESH,
            device_id={"tm": lax.div(to, n_sub) * lanes + lane, "cell": x, "sub": lax.rem(to, n_sub)},
        )
    for where in beside + below:
        pl.semaphore_signal(barrier, inc=1, device_id=where, device_id_type=MESH)
    for i in range(6):
        local_weight(i).start()

    @pl.when(home == sub)
    def _():
        in_local().start()

    for h in range(segments):
        for side in range(2):
            @pl.when(jnp.logical_not(has_halo(side, h)))
            def _():
                sect[h, 0 if side == 0 else span + 1] = jnp.zeros((cells, features), BF16)

    pl.semaphore_wait(barrier, column - 1 + len(beside) + len(below))

    for across in (1, 0):
        for d in range(near):
            @pl.when(in_away(across, d, first_turn))
            def _():
                in_copy(across, d, first_turn).start()
    for d in range(1, n_sub):
        remote_weight(0, d).start()

    for i, (around, count) in enumerate(((beside, len(beside)), (below, len(below)))):
        for where in around:
            pl.semaphore_signal(met.at[i], inc=1, device_id=where, device_id_type=MESH)
        pl.semaphore_wait(met.at[i], count)

    for across, d, k in [(0, d, k) for d in range(near) for k in range(group)] + [
        (1, d, k) for k in range(group) for d in range(near)
    ]:
        @pl.when(k != first_turn)
        def _():
            in_copy(across, d, k).start()
    for i in range(1, 6):
        for d in range(1, n_sub):
            remote_weight(i, d).start()

    for i in range(4):
        weight_ready(i)

    def block_step(h, p):
        in_ready(h, p)
        residual = work[h * group + p].reshape(per * cells, features).astype(F32)
        projected = dot(normalize(residual).astype(BF16), w_qkv[...]).astype(BF16)
        attended = attend(projected, per, cells, features)
        mid = (residual + dot(attended, w_out[...])).astype(BF16).astype(F32)
        hidden = jax.nn.gelu(dot(normalize(mid).astype(BF16), w_up[...])).astype(BF16)
        done = (mid + dot(hidden, w_down[...])).astype(BF16)
        sect[h, pl.ds(1 + p * per, per)] = done.reshape(per, cells, features)
        for side, edge in ((0, group - 1), (1, 0)):
            @pl.when(jnp.logical_and(p == edge, sends_halo(side, h)))
            def _():
                halo_copy(side, h).start()

    def flat(ref, h, picks):
        return jnp.concatenate([ref[h, f] for f in picks], axis=0)

    def temporal(p):
        picks = [lax.rem(p * per + 1 + q, span) for q in range(per)]

        @pl.loop(0, segments)
        def _(h):
            for side in range(2):
                @pl.when(p == group - 1)
                def _():
                    halo_ready(side, h)
            value = gated(
                flat(sect, h, [f + 1 for f in picks]),
                flat(sect, h, picks),
                flat(sect, h, [f + 2 for f in picks]),
                w_first,
            )
            for q, f in enumerate(picks):
                first[h, f] = value[q * cells : (q + 1) * cells]

        @pl.loop(0, segments)
        def _(k):
            h = lax.rem(own + 1 + k, segments)
            value = gated_pair(flat(first, h, picks), flat(first, 1 - h, picks), w_second, h == 1)
            for q, f in enumerate(picks):
                result[h, f] = value[q * cells : (q + 1) * cells]
            for f, e in [(f, e) for f in picks[::-1] for e in range(n_cell)]:
                j = lax.rem(x + 1 + e, n_cell)
                _, here = out_target(h, f, j)

                @pl.when(here)
                def _():
                    out_local(h, f, j).start()

                @pl.when(jnp.logical_not(here))
                def _():
                    out_copy(h, f, j).start()

    def position(p):
        return shift(lax.rem(p + group, group), my_turn, -1)

    @pl.loop(0, steps)
    def _(t):
        across = jnp.logical_or(t == group - 1, t > group)
        i = jnp.where(t < group - 1, t, jnp.where(t > group, t - group, jnp.where(across, 0, t - 1)))
        p = shift(my_turn, i, 1)
        block_step(jnp.where(across, 1 - own, own), p)

        @pl.when(t == 1)
        def _():
            weight_ready(4)
            weight_ready(5)

        @pl.when(t > group)
        def _():
            @pl.loop(0, 3)
            def _(m):
                q = jnp.where(m == 2, group - 1, p - 1 + m)
                both = jnp.logical_and(position(q) <= i, position(q + 1) <= i)
                inner = jnp.logical_and(q >= 0, q < group - 1)

                @pl.when(jnp.where(m == 2, i == group - 1, jnp.logical_and(both, inner)))
                def _():
                    temporal(q)

    for i in range(2):
        remote(w_first, w_first, ws.at[i], ws.at[i], {"cell": x}).wait_send()
    edges = sect.at[0, pl.ds(0, 2 * segments - 1)]
    remote(edges, edges, halo_s.at[0], halo_s.at[0], {"cell": x}).wait_send()
    all_sent(in_s.at[0])
    all_sent(out_s.at[0])
    pltpu.make_async_copy(out, out, out_r.at[0]).wait()


def regroup(sizes, frames, *halves):
    n_tm, n_cell, n_sub = sizes
    frames_local, cells_local, features = frames.shape
    classes = DILATION_FIRST
    per = frames_local // classes
    cells = n_cell * cells_local
    reach = DILATION_SECOND // frames_local
    group = reach // n_sub
    segments = n_tm * n_sub // reach
    span = group * per
    split = (per, classes, cells_local, features)
    dma = pltpu.SemaphoreType.DMA
    anywhere = pl.BlockSpec(memory_space=pl.ANY)
    call = pl.pallas_call(
        functools.partial(regroup_kernel, sizes),
        out_shape=pltpu.VMEM(split, BF16),
        in_specs=[anywhere] * 7,
        out_specs=anywhere,
        scratch_shapes=[pltpu.VMEM((n_sub * w.shape[0], w.shape[1]), BF16) for w in halves]
        + [
            pltpu.VMEM((segments * group, per, cells, features), BF16),
            pltpu.VMEM((segments, span + 2, cells, features), BF16),
            pltpu.VMEM((segments, span, cells, features), BF16),
            pltpu.VMEM((segments, span, cells, features), BF16),
            dma((2,)), dma((6,)), dma((1,)), dma((segments * group,)),
            dma((1,)), dma((2, segments)), dma((1,)), dma((1,)),
            pltpu.SemaphoreType.REGULAR((2,)),
        ],
        compiler_params=pltpu.CompilerParams(
            collective_id=0, has_side_effects=True, vmem_limit_bytes=56 * 1024 * 1024
        ),
        name="video_regroup",
    )
    return call(frames.reshape(split), *halves).reshape(frames.shape)


def regroups(sizes, frames, halves):
    n_tm, n_cell, n_sub = sizes
    frames_local = frames.shape[0]
    reach = DILATION_SECOND // frames_local
    return (
        n_tm * n_cell == DILATION_FIRST
        and n_sub == 2
        and sum(w.size for w in halves[:4]) == sum(w.size for w in halves[4:]) == n_sub * halves[4].size
        and frames_local % DILATION_FIRST == 0
        and DILATION_SECOND % frames_local == 0
        and reach % n_sub == 0
        and reach // n_sub >= 2
        and n_tm * n_sub == 2 * reach
        and DILATION_FIRST % (2 * (reach // n_sub)) == 0
        and reach // n_sub % n_cell == 0
    )


def local(sizes, frames, *halves):
    if regroups(sizes, frames, halves):
        return regroup(sizes, frames, *halves)
    _, n_cell, n_sub = sizes
    frames_local, cells_local, features = frames.shape
    per = frames_local // n_cell
    cells = n_cell * cells_local
    steps = per // CHUNK
    split = (n_cell, per, cells_local, features)
    dma = pltpu.SemaphoreType.DMA
    anywhere = pl.BlockSpec(memory_space=pl.ANY)
    call = pl.pallas_call(
        functools.partial(kernel, sizes),
        out_shape=jax.ShapeDtypeStruct(split, BF16),
        in_specs=[anywhere] * 7,
        out_specs=anywhere,
        scratch_shapes=[pltpu.VMEM((n_sub * w.shape[0], w.shape[1]), BF16) for w in halves]
        + [
            pltpu.VMEM((per, cells, features), BF16),
            pltpu.VMEM((per, cells, features), BF16),
            pltpu.VMEM((frames_local + 2 * DILATION_FIRST, cells_local, features), BF16),
            pltpu.VMEM(split, BF16),
            pltpu.VMEM((2,) + split, BF16),
            pltpu.VMEM(split, BF16),
            dma((6, n_sub - 1)), dma((6, n_sub - 1)), dma((6,)),
            dma((steps, n_cell - 1)), dma((steps, n_cell - 1)), dma((steps,)),
            dma((steps, n_cell - 1)), dma((steps, n_cell - 1)),
            dma((2, steps, n_cell)), dma((2, steps, n_cell)),
            dma((2, steps)), dma((2, steps)), dma((steps,)),
        ],
        compiler_params=pltpu.CompilerParams(
            collective_id=0, has_side_effects=True, vmem_limit_bytes=56 * 1024 * 1024
        ),
        name="video_block",
    )
    return call(frames, *halves).reshape(frames.shape)


def solution(mesh):
    sizes = (mesh.shape["tm"], mesh.shape["cell"], mesh.shape["sub"])
    placed = (P(("groups", "tm", "sub"), "cell", None),) + (P("sub", None),) * 6
    return jax.shard_map(
        functools.partial(local, sizes),
        mesh=mesh,
        in_specs=placed,
        out_specs=P(("groups", "tm", "sub"), "cell", None),
        check_vma=False,
    )
```

```python
import functools

import jax
import jax.numpy as jnp
from jax import lax
from jax.experimental import pallas as pl
from jax.experimental.pallas import tpu as pltpu
from jax.sharding import PartitionSpec as P

HEAD_DIM = 64
DILATION_FIRST = 16
DILATION_SECOND = 256
CHUNK = 2
AHEAD = 2
PAIR = 2 * HEAD_DIM
MESH = pl.DeviceIdType.MESH
F32 = jnp.float32
BF16 = jnp.bfloat16


def normalize(values):
    row_mean = jnp.mean(values, axis=-1, keepdims=True)
    centred = values - row_mean
    row_var = jnp.mean(centred * centred, axis=-1, keepdims=True)
    return centred * lax.rsqrt(row_var + 1e-05)


def dot(a, b):
    return jnp.dot(a, b, preferred_element_type=F32)


def attend(projected, frame_count, cells, features):
    lane = lax.broadcasted_iota(jnp.int32, (cells, PAIR), 1)
    scale = HEAD_DIM ** (-0.5)
    keep_a = jnp.where(lane < HEAD_DIM, scale, 0.0).astype(BF16)
    keep_b = jnp.where(lane < HEAD_DIM, 0.0, scale).astype(BF16)
    rows = []
    for f in range(frame_count):
        here = projected[f * cells : (f + 1) * cells]
        columns = []
        for p in range(features // PAIR):
            q = here[:, p * PAIR : (p + 1) * PAIR]
            k = here[:, features + p * PAIR : features + (p + 1) * PAIR]
            v = here[:, 2 * features + p * PAIR : 2 * features + (p + 1) * PAIR]
            stacked = jnp.concatenate([q * keep_a, q * keep_b], axis=0)
            scores = lax.dot_general(
                stacked, k, (((1,), (1,)), ((), ())), preferred_element_type=F32
            )
            exp_terms = jnp.exp(scores - jnp.max(scores, axis=-1, keepdims=True))
            probs = exp_terms * (1.0 / jnp.sum(exp_terms, axis=-1, keepdims=True))
            mixed = dot(probs.astype(BF16), v)
            columns.append(jnp.where(lane < HEAD_DIM, mixed[:cells], mixed[cells:]).astype(BF16))
        rows.append(jnp.concatenate(columns, axis=1))
    return jnp.concatenate(rows, axis=0)


def gated(center, earlier, later, weight_ref):
    features = center.shape[-1]
    preact = (
        dot(center, weight_ref[features : 2 * features])
        + dot(earlier, weight_ref[:features])
        + dot(later, weight_ref[2 * features :])
    )
    gate = 0.5 * jnp.tanh(0.5 * preact[:, features:]) + 0.5
    return (center.astype(F32) + jnp.tanh(preact[:, :features]) * gate).astype(BF16)


def gated_pair(center, other, weight_ref, earlier):
    features = center.shape[-1]
    other_rows = pl.ds(pl.multiple_of(jnp.where(earlier, 0, 2 * features), features), features)
    preact = dot(center, weight_ref[features : 2 * features]) + dot(other, weight_ref[other_rows])
    gate = 0.5 * jnp.tanh(0.5 * preact[:, features:]) + 0.5
    return (center.astype(F32) + jnp.tanh(preact[:, :features]) * gate).astype(BF16)


def kernel(
    sizes,
    frames, h_qkv, h_out, h_up, h_down, h_first, h_second,
    out,
    w_qkv, w_out, w_up, w_down, w_first, w_second,
    work, stage, pad, first, far, result,
    ws, wr, wl, in_s, in_r, in_l, own_s, own_r, halo_s, halo_r, far_s, far_r, out_s,
):
    n_tm, n_cell, n_sub = sizes
    n_blocks = n_tm * n_sub
    frames_local, cells_local, features = frames.shape
    per = frames_local // n_cell
    cells = n_cell * cells_local
    steps = per // CHUNK
    reach = DILATION_SECOND // frames_local
    width = DILATION_FIRST
    tm, x, sub = lax.axis_index("tm"), lax.axis_index("cell"), lax.axis_index("sub")
    block = tm * n_sub + sub

    def at(b, j):
        return {"tm": b // n_sub, "cell": j, "sub": lax.rem(b, n_sub)}

    def peer(d):
        return lax.rem(x + d, n_cell)

    def source(d):
        return lax.rem(x + n_cell - d, n_cell)

    def remote(src, dst, s, r, where):
        return pltpu.make_async_remote_copy(
            src_ref=src, dst_ref=dst, send_sem=s, recv_sem=r, device_id=where, device_id_type=MESH
        )

    has = {
        -1: block >= 1,
        1: block + 1 < n_blocks,
        -reach: block >= reach,
        reach: block + reach < n_blocks,
    }

    halves = (h_qkv, h_out, h_up, h_down, h_first, h_second)
    wholes = (w_qkv, w_out, w_up, w_down, w_first, w_second)

    def rows_of(half):
        size = half.shape[0]
        return pl.ds(pl.multiple_of(sub * size, 16), size)

    def local_weight(i):
        return pltpu.make_async_copy(halves[i], wholes[i].at[rows_of(halves[i])], wl.at[i])

    def remote_weight(i, d):
        return remote(
            halves[i], wholes[i].at[rows_of(halves[i])], ws.at[i, d - 1], wr.at[i, d - 1],
            {"sub": lax.rem(sub + d, n_sub)},
        )

    my_cells = pl.ds(pl.multiple_of(x * cells_local, 16), cells_local)

    def local_in(k):
        return pltpu.make_async_copy(
            frames.at[pl.ds(x * per + k * CHUNK, CHUNK)],
            work.at[pl.ds(k * CHUNK, CHUNK), my_cells],
            in_l.at[k],
        )

    def remote_in(k, d):
        return remote(
            frames.at[pl.ds(peer(d) * per + k * CHUNK, CHUNK)],
            work.at[pl.ds(k * CHUNK, CHUNK), my_cells],
            in_s.at[k, d - 1], in_r.at[k, d - 1], {"cell": peer(d)},
        )

    def staged(k, d):
        their_cells = pl.ds(pl.multiple_of(peer(d) * cells_local, 16), cells_local)
        return stage.at[pl.ds(k * CHUNK, CHUNK), their_cells]

    def own_copy(k, d):
        return remote(
            staged(k, d), pad.at[pl.ds(width + x * per + k * CHUNK, CHUNK)],
            own_s.at[k, d - 1], own_r.at[k, d - 1], {"cell": peer(d)},
        )

    def to_next(k, d):
        start = source(d) * per + k * CHUNK
        return remote(
            pad.at[pl.ds(width + start, CHUNK)],
            pad.at[pl.ds(start - (frames_local - width), CHUNK)],
            halo_s.at[0, k, d], halo_r.at[0, k, d], at(block + 1, x),
        )

    def to_last(k, d):
        start = width + source(d) * per + k * CHUNK
        return remote(
            pad.at[pl.ds(start, CHUNK)], pad.at[pl.ds(start + frames_local, CHUNK)],
            halo_s.at[1, k, d], halo_r.at[1, k, d], at(block - 1, x),
        )

    def from_halo(side, k, d):
        return remote(
            pad.at[pl.ds(width, CHUNK)], pad.at[pl.ds(0, CHUNK)],
            halo_s.at[side, k, d], halo_r.at[side, k, d], {"cell": x},
        )

    def late_half(j, k):
        return j * per + k * CHUNK >= frames_local - width

    def early_half(j, k):
        return j * per + k * CHUNK < width

    def far_copy(side, k):
        piece = pl.ds(k * CHUNK, CHUNK)
        by = reach if side == 0 else -reach
        return remote(
            first.at[:, piece], far.at[side, :, piece],
            far_s.at[side, k], far_r.at[side, k], at(block + by, x),
        )

    def out_copy(k):
        piece = pl.ds(k * CHUNK, CHUNK)
        return pltpu.make_async_copy(result.at[:, piece], out.at[:, piece], out_s.at[k])

    for i in range(6):
        local_weight(i).start()

    @pl.loop(0, steps)
    def _(k):
        local_in(k).start()

    barrier = pltpu.get_barrier_semaphore()
    for d in range(1, n_cell):
        pl.semaphore_signal(barrier, inc=1, device_id={"cell": peer(d)}, device_id_type=MESH)
    for by, cond in has.items():
        @pl.when(cond)
        def _():
            pl.semaphore_signal(
                barrier, inc=1, device_id=at(block + by, x), device_id_type=MESH
            )
    heard = n_cell - 1
    for cond in has.values():
        heard = heard + jnp.where(cond, 1, 0)
    pl.semaphore_wait(barrier, heard)

    for i in range(6):
        for d in range(1, n_sub):
            remote_weight(i, d).start()

    for k in range(min(AHEAD, steps)):
        for d in range(1, n_cell):
            remote_in(k, d).start()

    @pl.when(jnp.logical_not(has[-1]))
    def _():
        pad[:width] = jnp.zeros((width, cells_local, features), BF16)

    @pl.when(jnp.logical_not(has[1]))
    def _():
        pad[width + frames_local :] = jnp.zeros((width, cells_local, features), BF16)

    @pl.when(jnp.logical_not(has[-reach]))
    def _():
        far[0] = jnp.zeros(far.shape[1:], BF16)

    @pl.when(jnp.logical_not(has[reach]))
    def _():
        far[1] = jnp.zeros(far.shape[1:], BF16)

    def weight_ready(i):
        local_weight(i).wait()
        for d in range(1, n_sub):
            remote_weight(i, d).wait_recv()

    for i in range(4):
        weight_ready(i)

    def forward(k):
        for d in range(n_cell):
            if d:
                own_copy(k, d).wait_recv()

            @pl.when(jnp.logical_and(late_half(source(d), k), has[1]))
            def _():
                to_next(k, d).start()

            @pl.when(jnp.logical_and(early_half(source(d), k), has[-1]))
            def _():
                to_last(k, d).start()

    def block_step(k):
        @pl.when(k + AHEAD < steps)
        def _():
            for d in range(1, n_cell):
                remote_in(k + AHEAD, d).start()

        local_in(k).wait()
        for d in range(1, n_cell):
            remote_in(k, d).wait_recv()
        piece = pl.ds(k * CHUNK, CHUNK)
        residual = work[piece].reshape(CHUNK * cells, features).astype(F32)
        projected = dot(normalize(residual).astype(BF16), w_qkv[...]).astype(BF16)
        attended = attend(projected, CHUNK, cells, features)

        @pl.when(k >= 1)
        def _():
            forward(k - 1)

        mid = (residual + dot(attended, w_out[...])).astype(BF16).astype(F32)
        hidden = jax.nn.gelu(dot(normalize(mid).astype(BF16), w_up[...])).astype(BF16)
        done = (mid + dot(hidden, w_down[...])).astype(BF16)
        stage[piece] = done.reshape(CHUNK, cells, features)
        for d in range(1, n_cell):
            own_copy(k, d).start()
        pad[pl.ds(width + x * per + k * CHUNK, CHUNK)] = stage[piece, my_cells]

    def gather(ref, k, shift):
        parts = [
            ref[pl.ds(j * per + k * CHUNK + shift, CHUNK)].reshape(CHUNK * cells_local, features)
            for j in range(n_cell)
        ]
        return jnp.concatenate(parts, axis=0)

    def first_step(k):
        for d in range(n_cell):
            @pl.when(jnp.logical_and(late_half(source(d), k), has[-1]))
            def _():
                from_halo(0, k, d).wait_recv()

            @pl.when(jnp.logical_and(early_half(source(d), k), has[1]))
            def _():
                from_halo(1, k, d).wait_recv()
        value = gated(gather(pad, k, width), gather(pad, k, 0), gather(pad, k, 2 * width), w_first)
        first[:, pl.ds(k * CHUNK, CHUNK)] = value.reshape(n_cell, CHUNK, cells_local, features)

        @pl.when(has[reach])
        def _():
            far_copy(0, k).start()

        @pl.when(has[-reach])
        def _():
            far_copy(1, k).start()

    extra = 1 if steps >= 6 else 0
    late = steps - 2 * extra

    @pl.loop(0, steps)
    def _(k):
        block_step(k)

        @pl.when(k == min(1, steps - 1))
        def _():
            weight_ready(4)

        @pl.when(jnp.where(k < late, lax.rem(k, 2), 1) == 1)
        def _():
            first_step(jnp.where(k == steps - 1, (steps - 2) // 2 + extra, k // 2))

    forward(steps - 1)

    @pl.loop(steps // 2 + extra, steps)
    def _(k):
        first_step(k)

    weight_ready(5)

    @pl.loop(0, steps)
    def _(k):
        @pl.when(has[-reach])
        def _():
            far_copy(0, k).wait_recv()

        @pl.when(has[reach])
        def _():
            far_copy(1, k).wait_recv()

        piece = pl.ds(k * CHUNK, CHUNK)
        flat = (n_cell * CHUNK * cells_local, features)
        value = gated(
            first[:, piece].reshape(flat),
            far[0, :, piece].reshape(flat),
            far[1, :, piece].reshape(flat),
            w_second,
        )
        result[:, piece] = value.reshape(n_cell, CHUNK, cells_local, features)
        out_copy(k).start()

    for i in range(6):
        for d in range(1, n_sub):
            remote_weight(i, d).wait_send()

    @pl.loop(0, steps)
    def _(k):
        for d in range(n_cell):
            if d:
                remote_in(k, d).wait_send()
                own_copy(k, d).wait_send()

            @pl.when(jnp.logical_and(late_half(source(d), k), has[1]))
            def _():
                to_next(k, d).wait_send()

            @pl.when(jnp.logical_and(early_half(source(d), k), has[-1]))
            def _():
                to_last(k, d).wait_send()

        @pl.when(has[reach])
        def _():
            far_copy(0, k).wait_send()

        @pl.when(has[-reach])
        def _():
            far_copy(1, k).wait_send()

        out_copy(k).wait()


def regroup_kernel(
    sizes,
    frames, h_qkv, h_out, h_up, h_down, h_first, h_second,
    out,
    w_qkv, w_out, w_up, w_down, w_first, w_second,
    work, sect, first, result,
    ws, wr, in_s, in_r, halo_s, halo_r, out_s, out_r, met,
):
    n_tm, n_cell, n_sub = sizes
    n_blocks = n_tm * n_sub
    per, classes, cells_local, features = frames.shape
    segments, span, cells, _ = first.shape
    group = span // per
    reach = group * n_sub
    steps = segments * group
    tm, x, sub = lax.axis_index("tm"), lax.axis_index("cell"), lax.axis_index("sub")
    block = tm * n_sub + sub
    mine = tm * n_cell + x

    home, own = lax.div(lax.rem(block, reach), group), lax.div(block, reach)
    my_slot = own * group + lax.rem(block, group)
    my_cells = pl.ds(pl.multiple_of(x * cells_local, 16), cells_local)

    def remote(src, dst, s, r, where):
        return pltpu.make_async_remote_copy(
            src_ref=src, dst_ref=dst, send_sem=s, recv_sem=r, device_id=where, device_id_type=MESH
        )

    halves = (h_qkv, h_out, h_up, h_down, h_first, h_second)
    wholes = (w_qkv, w_out, w_up, w_down, w_first, w_second)

    def rows_of(half):
        size = half.shape[0]
        return pl.ds(pl.multiple_of(sub * size, 16), size)

    def local_weight(i):
        return pltpu.make_async_copy(halves[i], wholes[i].at[rows_of(halves[i])], wr.at[i])

    def remote_weight(i, d):
        return remote(
            halves[i], wholes[i].at[rows_of(halves[i])], ws.at[i], wr.at[i],
            {"sub": lax.rem(sub + d, n_sub)},
        )

    def weight_ready(i):
        pltpu.make_async_copy(wholes[i], wholes[i], wr.at[i]).wait()

    def cells_of(j):
        return pl.ds(pl.multiple_of(j * cells_local, 16), cells_local)

    near = classes // group // 2
    lanes = group // n_cell
    level, turn = lax.div(block, group), lax.rem(mine, group)

    def shift(a, k, sign):
        high = lax.rem(lax.div(a, n_cell) + lanes + sign * lax.div(k, n_cell), lanes)
        return high * n_cell + lax.rem(a + n_cell + sign * lax.rem(k, n_cell), n_cell)

    def in_copy(to):
        return remote(
            frames.at[:, to], work.at[my_slot, :, my_cells], in_s.at[0], in_r.at[my_slot],
            {"tm": lax.div(to, n_cell), "cell": lax.rem(to, n_cell), "sub": home},
        )

    def in_chip(across, d, k):
        base = lax.rem(lax.div(level, near) * near + near * across, 2 * near)
        to_turn = shift(shift(lax.rem(block, group), k, -1), home * n_cell, -1)
        return (base + lax.rem(level + d, near)) * group + to_turn

    first_turn = shift(shift(lax.rem(block, group), turn, -1), home * n_cell, -1)
    my_turn = shift(turn, sub * n_cell, 1)

    def in_local():
        return pltpu.make_async_copy(
            frames.at[:, mine], work.at[my_slot, :, my_cells], in_r.at[my_slot]
        )

    def in_ready(h, p):
        slot = h * group + p
        pltpu.make_async_copy(work.at[slot], work.at[slot], in_r.at[slot]).wait()

    def all_sent(sem):
        for away, part in ((False, frames.at[:, pl.ds(0, classes - 1)]), (True, frames)):
            @pl.when((home != sub) == away)
            def _():
                remote(part, part, sem, sem, {"cell": x}).wait_send()

    def halo_copy(side, h):
        at = h * n_sub + sub + (1 if side == 0 else -1)
        start, end = (span, 0) if side == 0 else (1, span + 1)
        to = lax.div(at, n_sub)
        return remote(
            sect.at[h, start], sect.at[to, end],
            halo_s.at[0], halo_r.at[side, to], {"sub": lax.rem(at, n_sub)},
        )

    def has_halo(side, h):
        at = h * n_sub + sub
        return at >= 1 if side == 0 else at + 1 < segments * n_sub

    def sends_halo(side, h):
        return has_halo(1 - side, h)

    def halo_ready(side, h):
        @pl.when(has_halo(side, h))
        def _():
            remote(
                sect.at[h, 1], sect.at[h, 0 if side == 0 else span + 1],
                halo_s.at[0], halo_r.at[side, h], {"cell": x},
            ).wait_recv()

    def out_target(h, f, j):
        to = h * reach + sub * group + lax.div(f, per)
        return to, jnp.logical_and(to == block, x == j)

    def out_copy(h, f, j):
        to, _ = out_target(h, f, j)
        return remote(
            result.at[h, f, cells_of(j)], out.at[lax.rem(f, per), mine], out_s.at[0], out_r.at[0],
            {"tm": lax.div(to, n_sub), "cell": j, "sub": lax.rem(to, n_sub)},
        )

    def out_local(h, f, j):
        return pltpu.make_async_copy(
            result.at[h, f, cells_of(j)], out.at[lax.rem(f, per), mine], out_r.at[0]
        )

    levels, lane = 2 * near, lax.rem(tm, lanes)
    over = [(step, level + step < levels if step > 0 else level + step >= 0) for step in (1, -1)]
    beside = [{"tm": tm, "cell": lax.rem(x + e, n_cell), "sub": sub} for e in range(1, n_cell)]
    below = [{"tm": tm - lane + lax.rem(lane + e, lanes), "cell": x, "sub": sub} for e in range(1, lanes)]
    inside = [{"tm": tm, "cell": x, "sub": lax.rem(sub + e, n_sub)} for e in range(1, n_sub)]
    barrier = pltpu.get_barrier_semaphore()
    neighbours = 0
    for step, there in over:
        neighbours = neighbours + jnp.where(there, 1, 0)

        @pl.when(there)
        def _():
            for core in range(n_sub):
                pl.semaphore_signal(
                    barrier, inc=1, device_id_type=MESH,
                    device_id={"tm": tm + step * lanes, "cell": x, "sub": core},
                )
    for where in beside + below + inside:
        pl.semaphore_signal(barrier, inc=1, device_id=where, device_id_type=MESH)

    for i in range(6):
        local_weight(i).start()

    @pl.when(home == sub)
    def _():
        in_local().start()

    for h in range(segments):
        for side in range(2):
            @pl.when(jnp.logical_not(has_halo(side, h)))
            def _():
                sect[h, 0 if side == 0 else span + 1] = jnp.zeros((cells, features), BF16)

    pl.semaphore_wait(barrier, n_sub * neighbours + len(beside + below + inside))

    def meet(i, around, count):
        for where, there in around:
            @pl.when(there)
            def _():
                pl.semaphore_signal(met.at[i], inc=1, device_id=where, device_id_type=MESH)
        return lambda: pl.semaphore_wait(met.at[i], count)

    def send_over(step):
        to = level + step
        inner = to < levels if step > 0 else to >= 0

        @pl.when(home != sub if step == 0 else inner)
        def _():
            in_copy(to * group + turn).start()

    column = [({"tm": tm + step * lanes, "cell": x, "sub": sub}, there) for step, there in over]
    for reached in range(1, levels):
        if reached < levels - 1:
            learned = meet(reached - 1, column, neighbours)
        else:
            learned = meet(reached - 1, [(where, True) for where in beside], len(beside))
        for step in (reached, -reached):
            send_over(step)
        if reached == 1:
            send_over(0)
            for d in range(1, n_sub):
                remote_weight(0, d).start()
        learned()
    meet(levels - 1, [(where, True) for where in below], len(below))()

    for across, d, k in [
        (1, d, k) for k in range(group) for d in range(near)
    ] + [(0, d, k) for d in range(near) for k in range(group)]:
        @pl.when(k != first_turn)
        def _():
            in_copy(in_chip(across, d, k)).start()
    for i in range(1, 6):
        for d in range(1, n_sub):
            remote_weight(i, d).start()

    for i in range(4):
        weight_ready(i)

    def block_step(h, p):
        in_ready(h, p)
        residual = work[h * group + p].reshape(per * cells, features).astype(F32)
        projected = dot(normalize(residual).astype(BF16), w_qkv[...]).astype(BF16)
        attended = attend(projected, per, cells, features)
        mid = (residual + dot(attended, w_out[...])).astype(BF16).astype(F32)
        hidden = jax.nn.gelu(dot(normalize(mid).astype(BF16), w_up[...])).astype(BF16)
        done = (mid + dot(hidden, w_down[...])).astype(BF16)
        sect[h, pl.ds(1 + p * per, per)] = done.reshape(per, cells, features)
        for side, edge in ((0, group - 1), (1, 0)):
            @pl.when(jnp.logical_and(p == edge, sends_halo(side, h)))
            def _():
                halo_copy(side, h).start()

    def flat(ref, h, picks):
        return jnp.concatenate([ref[h, f] for f in picks], axis=0)

    def temporal(p):
        picks = [lax.rem(p * per + 1 + q, span) for q in range(per)]

        @pl.loop(0, segments)
        def _(h):
            for side in range(2):
                @pl.when(p == group - 1)
                def _():
                    halo_ready(side, h)
            value = gated(
                flat(sect, h, [f + 1 for f in picks]),
                flat(sect, h, picks),
                flat(sect, h, [f + 2 for f in picks]),
                w_first,
            )
            for q, f in enumerate(picks):
                first[h, f] = value[q * cells : (q + 1) * cells]

        @pl.loop(0, segments)
        def _(k):
            h = lax.rem(own + k, segments)
            value = gated_pair(flat(first, h, picks), flat(first, 1 - h, picks), w_second, h == 1)
            for q, f in enumerate(picks):
                result[h, f] = value[q * cells : (q + 1) * cells]
            for f, e in [(f, e) for f in picks[::-1] for e in range(n_cell)]:
                j = lax.rem(x + 1 + e, n_cell)
                _, here = out_target(h, f, j)

                @pl.when(here)
                def _():
                    out_local(h, f, j).start()

                @pl.when(jnp.logical_not(here))
                def _():
                    out_copy(h, f, j).start()

    def position(p):
        return shift(lax.rem(p + group, group), my_turn, -1)

    @pl.loop(0, steps)
    def _(t):
        across = jnp.logical_or(t == group - 1, t > group)
        i = jnp.where(t < group - 1, t, jnp.where(t > group, t - group, jnp.where(across, 0, t - 1)))
        p = shift(my_turn, i, 1)
        block_step(jnp.where(across, 1 - own, own), p)

        @pl.when(t == 1)
        def _():
            weight_ready(4)
            weight_ready(5)

        @pl.when(t > group)
        def _():
            @pl.loop(0, 3)
            def _(m):
                q = jnp.where(m == 2, group - 1, p - 1 + m)
                both = jnp.logical_and(position(q) <= i, position(q + 1) <= i)
                inner = jnp.logical_and(q >= 0, q < group - 1)

                @pl.when(jnp.where(m == 2, i == group - 1, jnp.logical_and(both, inner)))
                def _():
                    temporal(q)

    for i in range(6):
        for d in range(1, n_sub):
            remote_weight(i, d).wait_send()
    edges = sect.at[0, pl.ds(0, 2 * segments - 1)]
    remote(edges, edges, halo_s.at[0], halo_s.at[0], {"cell": x}).wait_send()
    all_sent(in_s.at[0])
    all_sent(out_s.at[0])
    pltpu.make_async_copy(out, out, out_r.at[0]).wait()


def regroup(sizes, frames, *halves):
    n_tm, n_cell, n_sub = sizes
    frames_local, cells_local, features = frames.shape
    classes = DILATION_FIRST
    per = frames_local // classes
    cells = n_cell * cells_local
    reach = DILATION_SECOND // frames_local
    group = reach // n_sub
    segments = n_tm * n_sub // reach
    span = group * per
    split = (per, classes, cells_local, features)
    dma = pltpu.SemaphoreType.DMA
    anywhere = pl.BlockSpec(memory_space=pl.ANY)
    call = pl.pallas_call(
        functools.partial(regroup_kernel, sizes),
        out_shape=pltpu.VMEM(split, BF16),
        in_specs=[anywhere] * 7,
        out_specs=anywhere,
        scratch_shapes=[pltpu.VMEM((n_sub * w.shape[0], w.shape[1]), BF16) for w in halves]
        + [
            pltpu.VMEM((segments * group, per, cells, features), BF16),
            pltpu.VMEM((segments, span + 2, cells, features), BF16),
            pltpu.VMEM((segments, span, cells, features), BF16),
            pltpu.VMEM((segments, span, cells, features), BF16),
            dma((6,)), dma((6,)), dma((1,)), dma((segments * group,)),
            dma((1,)), dma((2, segments)), dma((1,)), dma((1,)),
            pltpu.SemaphoreType.REGULAR((n_tm * n_cell // group,)),
        ],
        compiler_params=pltpu.CompilerParams(
            collective_id=0, has_side_effects=True, vmem_limit_bytes=56 * 1024 * 1024
        ),
        name="video_regroup",
    )
    return call(frames.reshape(split), *halves).reshape(frames.shape)


def regroups(sizes, frames):
    n_tm, n_cell, n_sub = sizes
    frames_local = frames.shape[0]
    reach = DILATION_SECOND // frames_local
    return (
        n_tm * n_cell == DILATION_FIRST
        and n_sub == 2
        and frames_local % DILATION_FIRST == 0
        and DILATION_SECOND % frames_local == 0
        and reach % n_sub == 0
        and reach // n_sub >= 2
        and n_tm * n_sub == 2 * reach
        and DILATION_FIRST % (2 * (reach // n_sub)) == 0
        and reach // n_sub % n_cell == 0
    )


def local(sizes, frames, *halves):
    if regroups(sizes, frames):
        return regroup(sizes, frames, *halves)
    _, n_cell, n_sub = sizes
    frames_local, cells_local, features = frames.shape
    per = frames_local // n_cell
    cells = n_cell * cells_local
    steps = per // CHUNK
    split = (n_cell, per, cells_local, features)
    dma = pltpu.SemaphoreType.DMA
    anywhere = pl.BlockSpec(memory_space=pl.ANY)
    call = pl.pallas_call(
        functools.partial(kernel, sizes),
        out_shape=jax.ShapeDtypeStruct(split, BF16),
        in_specs=[anywhere] * 7,
        out_specs=anywhere,
        scratch_shapes=[pltpu.VMEM((n_sub * w.shape[0], w.shape[1]), BF16) for w in halves]
        + [
            pltpu.VMEM((per, cells, features), BF16),
            pltpu.VMEM((per, cells, features), BF16),
            pltpu.VMEM((frames_local + 2 * DILATION_FIRST, cells_local, features), BF16),
            pltpu.VMEM(split, BF16),
            pltpu.VMEM((2,) + split, BF16),
            pltpu.VMEM(split, BF16),
            dma((6, n_sub - 1)), dma((6, n_sub - 1)), dma((6,)),
            dma((steps, n_cell - 1)), dma((steps, n_cell - 1)), dma((steps,)),
            dma((steps, n_cell - 1)), dma((steps, n_cell - 1)),
            dma((2, steps, n_cell)), dma((2, steps, n_cell)),
            dma((2, steps)), dma((2, steps)), dma((steps,)),
        ],
        compiler_params=pltpu.CompilerParams(
            collective_id=0, has_side_effects=True, vmem_limit_bytes=56 * 1024 * 1024
        ),
        name="video_block",
    )
    return call(frames, *halves).reshape(frames.shape)


def solution(mesh):
    sizes = (mesh.shape["tm"], mesh.shape["cell"], mesh.shape["sub"])
    placed = (P(("groups", "tm", "sub"), "cell", None),) + (P("sub", None),) * 6
    return jax.shard_map(
        functools.partial(local, sizes),
        mesh=mesh,
        in_specs=placed,
        out_specs=P(("groups", "tm", "sub"), "cell", None),
        check_vma=False,
    )
```
